128 devices in a mesh: tile: 64 (over x, z_hi, y, core), layer: 2 (over z_lo).
Axes of the slice: x: 4, y: 4, z: 4 (z_hi: 2, z_lo: 2; z = z_hi * 2 + z_lo), core: 2. Of those that a mesh axis runs over, the one named last changes fastest.
Arguments:
- viscosity: float32 [8, 4096, 1024], P('layer', 'tile'), may hold values from 0.02 to 0.16
- friction: float32 [4096, 1024], P('tile'), may hold values from 0.05 to 0.5
- base_vel: float32 [2, 4096, 1024], P(None, 'tile'), may hold values from -6 to 6
- surf_vel: float32 [2, 4096, 1024], P(None, 'tile'), may hold values from -6 to 6
- layer_thick: float32 [8], P('layer'), may hold values from 0.5 to 1.5
- ice_mask: int32 [4096, 1024], P('tile'), may hold values 0 or 1
- obs_slots: bfloat16 [4096, 64, 2, 128], P('tile'), may hold values from -6 to 6
- obs_target: int32 [4096, 64], P('tile'), may hold values from 0 to 1023
Outputs:
- adjoint: float32 [2, 8, 4096, 1024], P(None, 'layer', 'tile')
- gradient: float32 [4096, 1024], P('tile')
The draws below stay inside these ranges and needn't reach their ends.
Inputs may be any that keep to these rules, and one draw needn't show every extreme that they name: `obs_target`: values below 512 name a patch of the owner's strip; values 512 or more mark an empty slot. Several slots may name the same patch.
All inputs are finite; a program needn't handle non-finite values. No bound on the sum of `ice_mask` on one device may be relied on, other than what follows from the above.
Results may differ from the reference program's by a relative error of at most 0.0025.
Values may be sent and summed in bfloat16 or wider, within the bound.
No kernel may reach another device: no remote copies, remote signals or barrier semaphores. Data moves between devices by JAX's collectives and lax.ppermute only.
A program may use at most 64 MiB of HBM per device.

```python
import math
import jax
import jax.numpy as jnp
from jax import lax

RX = 64
NY = 1024
CAP = 64
PATCH = 128
SWEEPS = 3
OWNERS = 64
NX = 4096
LAYERS = 8
NPATCH = 512


def place_ends(entries, key, low, largest):
    longest = entries.shape.index(max(entries.shape))
    spots = []
    for shift in (0, 1):
        where = [jax.random.randint(jax.random.fold_in(key, axis), (), 0, length) for axis, length in enumerate(entries.shape)]
        where[longest] = (where[longest] + shift) % entries.shape[longest]
        spots.append(tuple(where))
    return entries.at[spots[0]].set(low).at[spots[1]].set(largest)


def shard_levels(key, shape, split, least, top_value):
    level, own = 1.0, jax.random.fold_in(key, 6)
    for position, blocks in split:
        heights = jnp.exp(jax.random.uniform(jax.random.fold_in(own, position), (blocks,), jnp.float32, least / len(split), top_value / len(split)))
        level = level * jnp.repeat(heights, shape[position] // blocks).reshape([-1 if axis == position else 1 for axis in range(len(shape))])
    return level


def centred(rng, dims, spread, bound, split=(), held_as=jnp.bfloat16):
    gain = shard_levels(rng, dims, split, -0.22, 0.18) if split else 1.0
    values = jax.random.normal(rng, dims, jnp.float32) * spread * gain
    return jnp.minimum(jnp.maximum(values, -bound), bound).astype(held_as)


def setup_inputs(seed: int = 0) -> dict:
    arg_keys = jax.random.split(jax.random.key(seed), 9)
    viscosity = jnp.clip(jnp.exp(math.log(0.16) - 2.0794415 * jax.random.uniform(arg_keys[0], (LAYERS, NX, NY), jnp.float32) ** shard_levels(arg_keys[0], (LAYERS, NX, NY), ((0, 2), (1, 64)), -0.2, 0.2)), 0.02, 0.16)
    friction = jnp.clip(jnp.exp(math.log(0.5) - 2.3025851 * jax.random.uniform(arg_keys[1], (NX, NY), jnp.float32) ** shard_levels(arg_keys[1], (NX, NY), ((0, 64),), -0.2, 0.2)), 0.05, 0.5)
    base_vel = centred(arg_keys[2], (2, NX, NY), 1.0, 6.0, ((1, 64),), jnp.float32)
    surf_vel = centred(arg_keys[3], (2, NX, NY), 1.0, 6.0, ((1, 64),), jnp.float32)
    layer_thick = jnp.clip(0.5 + 1.0 * jax.random.uniform(arg_keys[4], (LAYERS,), jnp.float32) ** shard_levels(arg_keys[4], (LAYERS,), ((0, 2),), -0.2, 0.2), 0.5, 1.5)
    ice_mask = place_ends((jax.random.randint(arg_keys[5], (NX, NY), 0, 5) < 4).astype(jnp.int32), jax.random.fold_in(arg_keys[5], 1), 0, 1)
    obs_slots = centred(arg_keys[6], (OWNERS * OWNERS, CAP, 2, PATCH), 1.0, 6.0, ((0, 64),))
    obs_target = place_ends(jax.random.randint(arg_keys[7], (OWNERS * OWNERS, CAP), 0, 2 * NPATCH), jax.random.fold_in(arg_keys[7], 1), 0, (2 * NPATCH) - 1).astype(jnp.int32)
    return dict(viscosity=viscosity, friction=friction, base_vel=base_vel, surf_vel=surf_vel, layer_thick=layer_thick, ice_mask=ice_mask, obs_slots=obs_slots, obs_target=obs_target)


vertical_weight = 8.0
along_weight = 4.0
cross_weight = 1.0
relax_factor = 0.7


def face_terms(visc_ext):
    centre = visc_ext[1:-1, 1:-1, 1:-1]
    below = 0.5 * (centre + visc_ext[:-2, 1:-1, 1:-1])
    above = 0.5 * (centre + visc_ext[2:, 1:-1, 1:-1])
    north = 0.5 * (centre + visc_ext[1:-1, :-2, 1:-1])
    south = 0.5 * (centre + visc_ext[1:-1, 2:, 1:-1])
    west = 0.5 * (centre + visc_ext[1:-1, 1:-1, :-2])
    east = 0.5 * (centre + visc_ext[1:-1, 1:-1, 2:])
    return (below, above, north, south, west, east)


def weights():
    row_weight = jnp.array([along_weight, cross_weight], jnp.float32).reshape(2, 1, 1, 1)
    col_weight = jnp.array([cross_weight, along_weight], jnp.float32).reshape(2, 1, 1, 1)
    return row_weight, col_weight


def diagonal(faces, bottom_drag):
    below, above, north, south, west, east = faces
    row_weight, col_weight = weights()
    return vertical_weight * (below + above) + row_weight * (north + south) + col_weight * (west + east) + bottom_drag


def neighbour_sum(extended, faces):
    below, above, north, south, west, east = faces
    row_weight, col_weight = weights()
    vertical = below * extended[:, :-2, 1:-1, 1:-1] + above * extended[:, 2:, 1:-1, 1:-1]
    rowwise = north * extended[:, 1:-1, :-2, 1:-1] + south * extended[:, 1:-1, 2:, 1:-1]
    colwise = west * extended[:, 1:-1, 1:-1, :-2] + east * extended[:, 1:-1, 1:-1, 2:]
    return vertical_weight * vertical + row_weight * rowwise + col_weight * colwise


def reference(viscosity, friction, base_vel, surf_vel, layer_thick, ice_mask, obs_slots, obs_target):
    by_owner = obs_slots.reshape(OWNERS, OWNERS, CAP, 2 * PATCH).transpose(1, 0, 2, 3)
    targets = obs_target.reshape(OWNERS, OWNERS, CAP).transpose(1, 0, 2)
    patch_ids = jnp.arange(NPATCH, dtype=jnp.int32)

    def owner_sums(pair):
        slots, marks = pair
        onehot = (marks.reshape(-1)[None, :] == patch_ids[:, None]).astype(jnp.bfloat16)
        summed = jnp.dot(onehot, slots.reshape(OWNERS * CAP, 2 * PATCH), preferred_element_type=jnp.float32)
        return summed, jnp.sum(onehot, axis=1, dtype=jnp.float32)

    summed, counts = lax.map(owner_sums, (by_owner, targets))
    obs_sum = summed.reshape(OWNERS, RX, NY // PATCH, 2, PATCH).transpose(3, 0, 1, 2, 4).reshape(2, NX, NY)
    count_map = jnp.repeat(counts.reshape(OWNERS, RX, NY // PATCH), PATCH, axis=2).reshape(NX, NY)
    maskf = ice_mask.astype(jnp.float32)
    misfit = maskf * (count_map * surf_vel - obs_sum)
    rhs = layer_thick[None, :, None, None] * misfit[:, None]
    faces = face_terms(jnp.pad(viscosity, 1))
    bottom_drag = jnp.where(jnp.arange(LAYERS, dtype=jnp.int32)[:, None, None] == 0, friction[None], jnp.float32(0.0))
    diag = diagonal(faces, bottom_drag)
    adjoint = maskf * (relax_factor * rhs / diag)
    for sweep_index in range(SWEEPS - 1):
        extended = jnp.pad(adjoint, ((0, 0), (1, 1), (1, 1), (1, 1)))
        adjoint = maskf * (adjoint + relax_factor * (rhs - diag * adjoint + neighbour_sum(extended, faces)) / diag)
    integral = jnp.sum(layer_thick[None, :, None, None] * adjoint, axis=1)
    gradient = -maskf * friction * (base_vel[0] * integral[0] + base_vel[1] * integral[1])
    return adjoint, gradient
```

```python
import jax
import jax.numpy as jnp
from jax import lax
from jax.experimental import pallas as pl
from jax.experimental.pallas import tpu as pltpu
from jax.sharding import PartitionSpec as P

F32 = jnp.float32
BF16 = jnp.bfloat16
ROWS = 64
EXT = 68
VROWS = 70
PAIR = ("tile", "layer")


def full(*shape):
    return pl.BlockSpec(memory_space=pltpu.VMEM)


def smem():
    return pl.BlockSpec(memory_space=pltpu.SMEM)


def out(shape, dtype=F32):
    return jax.ShapeDtypeStruct(shape, dtype)


def row(r):
    return pl.ds(pl.multiple_of(r * 8, 8), 8)


def east(x, last):
    r = pltpu.roll(x, 127, 1)
    return jnp.where(last, pltpu.roll(r, 7, 0), r)


def west(x, first):
    r = pltpu.roll(x, 1, 1)
    return jnp.where(first, pltpu.roll(r, 1, 0), r)


def lanes():
    lane = lax.broadcasted_iota(jnp.int32, (8, 128), 1)
    sub = lax.broadcasted_iota(jnp.int32, (8, 128), 0)
    return lane, sub


def code_of(t):
    return jnp.where(t < 512, (128 + (t & 127)) << (t >> 7), 0)


def pack_kernel(sc, slots, target, o, f, codes):
    own = sc[0]
    c = code_of(target[...]).astype(F32)
    codes[...] = jnp.concatenate([c, c], axis=1)
    for d in range(slots.shape[0]):
        f[d] = slots[d].astype(F32)
        o[d, pl.ds(0, 64), :] = f[d, pl.ds(own, 64, stride=2), :].astype(BF16)
        o[d, pl.ds(64, 8), :] = jnp.broadcast_to(codes[pl.ds(d, 1), :], (8, 128)).astype(BF16)


def pack(sc, slots, target):
    n = slots.shape[0]
    step = 16
    return pl.pallas_call(
        pack_kernel,
        grid=(n // step,),
        in_specs=[
            smem(),
            pl.BlockSpec((step, 128, 128), lambda i: (i, 0, 0)),
            pl.BlockSpec((step, 64), lambda i: (i, 0)),
        ],
        out_specs=pl.BlockSpec((step, 72, 128), lambda i: (i, 0, 0)),
        out_shape=out((n, 72, 128), BF16),
        scratch_shapes=[pltpu.VMEM((step, 128, 128), F32), pltpu.VMEM((step, 128), F32)],
    )(sc, slots, target)


def spread(dst, at, x):
    n = x.shape[0]
    for k in range(8):
        dst[pl.ds(at + k, n, stride=8), :] = x[:, k * 128 : (k + 1) * 128]


def coef_kernel(sc, visc, other, edges, fric, mask, bvel, svel, fz, fr, fc, inv, wgt, svm, msk, v, g, mk, fk, bv):
    own, odd = sc[0], sc[1]
    for i in range(4):
        for src, at in ((visc, own * 4 + i), (other, (1 - own) * 4 + i)):
            for h in range(0, ROWS, 16):
                spread(v.at[at], (3 + h) * 8, src[i, h : h + 16, :].astype(F32))
    for h in range(0, ROWS, 16):
        spread(mk, (2 + h) * 8, mask[h : h + 16, :].astype(F32))
        spread(fk, (2 + h) * 8, fric[h : h + 16, :])
        spread(svm, h * 8, svel[own, h : h + 16, :])
        for c in range(2):
            spread(bv.at[c], h * 8, bvel[c, h : h + 16, :])
    for kind in range(2):
        above = (odd + kind) % 2 == 1
        for who in range(2):
            spread(g.at[who], 0, edges[who, kind].astype(F32))
        vat = jnp.where(above, 0, 3 + ROWS)
        cat = jnp.where(above, 0, 2 + ROWS)
        for who in range(2):
            base = jnp.where(who == 0, own, 1 - own) * 4
            for i in range(4):
                for r in range(3):
                    v[base + i, row(vat + r), :] = g[who, pl.ds((i * 3 + r) * 8, 8), :]
        for r in range(2):
            mk[row(cat + r), :] = g[0, pl.ds((12 + r) * 8, 8), :]
            fk[row(cat + r), :] = g[0, pl.ds((14 + r) * 8, 8), :]
    lane, sub = lanes()
    last, first = lane == 127, lane == 0
    end = last & (sub == 7)
    start = first & (sub == 0)

    def step(r, carry):
        up, here, down = row(r), row(r + 1), row(r + 2)
        m = mk[here_of(r), :] > 0.5
        drag = fk[here_of(r), :]
        prev = None
        for l in range(8):
            c = v[l, here, :]
            fe = 0.5 * (c + jnp.where(end, 0.0, east(c, last)))
            fw = 0.5 * (c + jnp.where(start, 0.0, west(c, first)))
            south = 0.5 * (c + v[l, down, :])
            north = 0.5 * (c + v[l, up, :])
            below = 4.0 * c if l == 0 else prev
            above = 4.0 * (c + v[l + 1, here, :]) if l < 7 else 4.0 * c
            fz[l, here_of(r), :] = above
            fr[l, here_of(r), :] = south
            fc[l, here_of(r), :] = jnp.where(end, 0.0, fe)
            rows_, cols_, both = north + south, fe + fw, below + above
            if l == 0:
                both = both + drag
            for k, (rw, cw) in enumerate(((4.0, 1.0), (1.0, 4.0))):
                diag = both + rw * rows_ + cw * cols_
                inv[k, l, here_of(r), :] = jnp.where(m, 0.7 / diag, 0.0)
            prev = above
        return carry

    def here_of(r):
        return row(r)

    lax.fori_loop(0, EXT, step, 0)

    def weigh(r, carry):
        m = mk[row(r + 2), :]
        msk[row(r), :] = m
        svm[row(r), :] = svm[row(r), :] * m
        w = -m * fk[row(r + 2), :]
        for c in range(2):
            wgt[c, row(r), :] = w * bv[c, row(r), :]
        return carry

    lax.fori_loop(0, ROWS, weigh, 0)


def coefficients(sc, visc, other, edges, fric, mask, bvel, svel):
    field = (8, EXT * 8, 128)
    strip = (ROWS * 8, 128)
    return pl.pallas_call(
        coef_kernel,
        in_specs=[smem()] + [full()] * 7,
        out_specs=[full()] * 7,
        out_shape=[out(field), out(field), out(field), out((2, *field)), out((2, *strip)), out(strip), out(strip)],
        scratch_shapes=[
            pltpu.VMEM((8, VROWS * 8, 128), F32),
            pltpu.VMEM((2, 128, 128), F32),
            pltpu.VMEM((EXT * 8, 128), F32),
            pltpu.VMEM((EXT * 8, 128), F32),
            pltpu.VMEM((2, *strip), F32),
        ],
    )(sc, visc, other, edges, fric, mask, bvel, svel)


def misfit_kernel(sc, got, svm, msk, m_out, e_out, hot, rhs, pc):
    odd = sc[1]
    p = lax.broadcasted_iota(jnp.int32, (512, 128), 0)
    pc[...] = code_of(p).astype(F32)
    lane = lax.broadcasted_iota(jnp.int32, (8, 128), 1)
    for b in range(32):
        for h in range(2):
            rhs[pl.ds(b * 128 + h * 64, 64), pl.ds(0, 128)] = got[2 * b + h, pl.ds(0, 64), :]
        c = jnp.where(
            lane < 64, got[2 * b, pl.ds(64, 8), :].astype(F32), got[2 * b + 1, pl.ds(64, 8), :].astype(F32)
        )
        same = pc[...].reshape(64, 8, 128) == c[None]
        hot[:, pl.ds(b * 128, 128)] = jnp.where(same, 1.0, 0.0).reshape(512, 128).astype(BF16)
    rhs[:, pl.ds(128, 128)] = jnp.ones((4096, 128), BF16)
    sums = jnp.dot(hot[...], rhs[...], preferred_element_type=F32)
    m_out[...] = sums[:, 128:] * svm[...] - msk[...] * sums[:, :128]
    for kind in range(2):
        at = jnp.where((odd + kind) % 2 == 0, ROWS - 2, 0)
        for r in range(2):
            e_out[kind, pl.ds(r * 8, 8), :] = m_out[row(at + r), :]


def misfit(sc, got, svm, msk):
    return pl.pallas_call(
        misfit_kernel,
        in_specs=[smem()] + [full()] * 3,
        out_specs=[full()] * 2,
        out_shape=[out((ROWS * 8, 128)), out((2, 16, 128))],
        scratch_shapes=[
            pltpu.VMEM((512, 4096), BF16),
            pltpu.VMEM((4096, 256), BF16),
            pltpu.VMEM((512, 128), F32),
        ],
    )(sc, got, svm, msk)


def sweep_kernel(sc, thick, m_own, m_oth, e_own, e_oth, fz, fr, fc, inv, wgt, adj, grad, m, a1, a2, a3, acc):
    own, odd = sc[0], sc[1]
    lane, _ = lanes()
    last, first = lane == 127, lane == 0

    def relaxed(a, l, r, c, rw, cw):
        here = row(r)
        x = a[l, here, :]
        n = None
        if l < 7:
            n = fz[l, here, :] * a[l + 1, here, :]
        if l > 0:
            t = fz[l - 1, here, :] * a[l - 1, here, :]
            n = t if n is None else n + t
        rows_ = fr[l, here, :] * a[l, row(r + 1), :] + fr[l, row(r - 1), :] * a[l, row(r - 1), :]
        f = fc[l, here, :]
        cols_ = f * east(x, last) + west(f * x, first)
        n = n + rw * rows_ + cw * cols_
        return 0.3 * x + inv[c, l, here, :] * (thick[l] * m[here, :] + n)

    for q in range(2):
        c = own if q == 0 else 1 - own
        mine, edge = (m_own, e_own) if q == 0 else (m_oth, e_oth)
        m[pl.ds(16, ROWS * 8), :] = mine[...]
        for kind in range(2):
            above = (odd + kind) % 2 == 1
            at = jnp.where(above, 0, ROWS + 2)
            for r in range(2):
                m[row(at + r), :] = edge[kind, pl.ds(r * 8, 8), :]
        rw = jnp.where(c == 0, 4.0, 1.0)
        cw = jnp.where(c == 0, 1.0, 4.0)

        def first_sweep(r):
            for l in range(8):
                a1[l, row(r), :] = inv[c, l, row(r), :] * (thick[l] * m[row(r), :])

        def second_sweep(r):
            for l in range(8):
                a2[l, row(r), :] = relaxed(a1, l, r, c, rw, cw)

        def third_sweep(r):
            total = None
            for l in range(8):
                y = relaxed(a2, l, r, c, rw, cw)
                a3[l, row(r - 2), :] = y
                total = thick[l] * y if l == 0 else total + thick[l] * y
            w = wgt[c, row(r - 2), :] * total
            acc[row(r - 2), :] = w if q == 0 else acc[row(r - 2), :] + w

        for r in range(4):
            first_sweep(r)
        for r in range(1, 3):
            second_sweep(r)

        def step(r, carry):
            first_sweep(r)
            second_sweep(r - 1)
            third_sweep(r - 2)
            return carry

        lax.fori_loop(4, EXT, step, 0)
        for i in range(4):
            for h in range(0, ROWS, 8):
                for k in range(8):
                    adj[c, i, pl.ds(h, 8), pl.ds(k * 128, 128)] = a3[own * 4 + i, pl.ds(h * 8 + k, 8, stride=8), :]
    for h in range(0, ROWS, 8):
        for k in range(8):
            grad[pl.ds(h, 8), pl.ds(k * 128, 128)] = acc[pl.ds(h * 8 + k, 8, stride=8), :]


def sweeps(sc, thick, m_own, m_oth, e_own, e_oth, fz, fr, fc, inv, wgt):
    return pl.pallas_call(
        sweep_kernel,
        in_specs=[smem(), smem()] + [full()] * 9,
        out_specs=[full()] * 2,
        out_shape=[out((2, 4, ROWS, 1024)), out((ROWS, 1024))],
        scratch_shapes=[
            pltpu.VMEM((EXT * 8, 128), F32),
            pltpu.VMEM((8, EXT * 8, 128), F32),
            pltpu.VMEM((8, EXT * 8, 128), F32),
            pltpu.VMEM((8, ROWS * 8, 128), F32),
            pltpu.VMEM((ROWS * 8, 128), F32),
        ],
    )(sc, thick, m_own, m_oth, e_own, e_oth, fz, fr, fc, inv, wgt)


def swaps(tiles, offset, across):
    perm = []
    for t in range(offset, tiles - 1, 2):
        for layer in range(2):
            a, b = t * 2 + layer, (t + 1) * 2 + (1 - layer if across else layer)
            perm += [(a, b), (b, a)]
    return perm


def swap_layers(x):
    return lax.ppermute(x, "layer", [(0, 1), (1, 0)])


def body(viscosity, friction, base_vel, surf_vel, layer_thick, ice_mask, obs_slots, obs_target):
    tiles = lax.axis_size("tile")
    own = lax.axis_index("layer")
    odd = lax.axis_index("tile") % 2
    sc = jnp.stack([own, odd]).astype(jnp.int32)

    other = swap_layers(viscosity.astype(BF16))
    payload = pack(sc, obs_slots.reshape(tiles, 128, 128), obs_target)
    got = lax.all_to_all(payload, "tile", split_axis=0, concat_axis=0, tiled=True)

    def edge(at):
        return jnp.concatenate(
            [
                lax.slice_in_dim(viscosity, (ROWS - 3) if at else 0, ROWS if at else 3, axis=1).reshape(12, 1024),
                lax.slice_in_dim(ice_mask, (ROWS - 2) if at else 0, ROWS if at else 2, axis=0).astype(F32),
                lax.slice_in_dim(friction, (ROWS - 2) if at else 0, ROWS if at else 2, axis=0),
            ]
        ).astype(BF16)

    top, bottom = edge(0), edge(1)
    to_a = jnp.where(odd == 0, bottom, top)
    to_b = jnp.where(odd == 0, top, bottom)
    edges = jnp.stack(
        [
            jnp.stack([lax.ppermute(to_a, PAIR, swaps(tiles, 0, False)), lax.ppermute(to_b, PAIR, swaps(tiles, 1, False))]),
            jnp.stack([lax.ppermute(to_a, PAIR, swaps(tiles, 0, True)), lax.ppermute(to_b, PAIR, swaps(tiles, 1, True))]),
        ]
    )
    thick_other = swap_layers(layer_thick)
    thick = jnp.where(
        own == 0, jnp.concatenate([layer_thick, thick_other]), jnp.concatenate([thick_other, layer_thick])
    )
    fz, fr, fc, inv, wgt, svm, msk = coefficients(
        sc, viscosity, other, edges, friction, ice_mask, base_vel, surf_vel
    )
    m_own, e_send = misfit(sc, got, svm, msk)
    m_oth = swap_layers(m_own)
    e_own = jnp.stack(
        [
            lax.ppermute(e_send[0], PAIR, swaps(tiles, 0, False)),
            lax.ppermute(e_send[1], PAIR, swaps(tiles, 1, False)),
        ]
    )
    e_oth = swap_layers(e_own)
    adjoint, gradient = sweeps(sc, thick, m_own, m_oth, e_own, e_oth, fz, fr, fc, inv, wgt)
    return adjoint, gradient


def solution(mesh):
    in_specs = (
        P("layer", "tile", None),
        P("tile", None),
        P(None, "tile", None),
        P(None, "tile", None),
        P("layer"),
        P("tile", None),
        P("tile", None, None, None),
        P("tile", None),
    )
    out_specs = (P(None, "layer", "tile", None), P("tile", None))
    return jax.shard_map(body, mesh=mesh, in_specs=in_specs, out_specs=out_specs, check_vma=False)
```

```python
import jax
import jax.numpy as jnp
from jax import lax
from jax.experimental import pallas as pl
from jax.experimental.pallas import tpu as pltpu
from jax.sharding import PartitionSpec as P

F32 = jnp.float32
BF16 = jnp.bfloat16
ROWS = 64
EXT = 68
PAIR = ("tile", "layer")
FIELD = (8, EXT * 8, 128)
STRIP = (ROWS * 8, 128)
MIB = 1 << 20


def vm():
    return pl.BlockSpec(memory_space=pltpu.VMEM)


def sm():
    return pl.BlockSpec(memory_space=pltpu.SMEM)


def hbm():
    return pl.BlockSpec(memory_space=pl.ANY)


def kept(*shape, dtype=F32):
    return pltpu.VMEM(shape, dtype)


def near(x):
    return pltpu.with_memory_space_constraint(x, pltpu.VMEM)


def row(r):
    return pl.ds(pl.multiple_of(r * 8, 8), 8)


def place(sc):
    return sc[0] & 1, sc[0] >> 1


def lanes():
    lane = lax.broadcasted_iota(jnp.int32, (8, 128), 1)
    sub = lax.broadcasted_iota(jnp.int32, (8, 128), 0)
    return lane, sub


def east(x, last):
    r = pltpu.roll(x, 127, 1)
    return jnp.where(last, pltpu.roll(r, 7, 0), r)


def west(x, first):
    r = pltpu.roll(x, 1, 1)
    return jnp.where(first, pltpu.roll(r, 1, 0), r)


def code_of(t):
    return jnp.where(t < 512, (128 + (t & 127)) << (t >> 7), 0)


def pack_kernel(sc, slots, target, o, f, codes):
    own, _ = place(sc)
    c = code_of(target[...]).astype(F32)
    codes[...] = jnp.concatenate([c, c], axis=1)
    for d in range(slots.shape[0]):
        f[d] = slots[d].astype(F32)
        o[d, pl.ds(0, 64), :] = f[d, pl.ds(own, 64, stride=2), :].astype(BF16)
        o[d, pl.ds(64, 8), :] = jnp.broadcast_to(codes[pl.ds(d, 1), :], (8, 128)).astype(BF16)


def pack(sc, slots, target):
    n = slots.shape[0]
    step = 8
    return pl.pallas_call(
        pack_kernel,
        grid=(n // step,),
        in_specs=[
            sm(),
            pl.BlockSpec((step, 128, 128), lambda i: (i, 0, 0)),
            pl.BlockSpec((step, 64), lambda i: (i, 0)),
        ],
        out_specs=pl.BlockSpec((step, 72, 128), lambda i: (i, 0, 0)),
        out_shape=jax.ShapeDtypeStruct((n, 72, 128), BF16),
        scratch_shapes=[pltpu.VMEM((step, 128, 128), F32), pltpu.VMEM((step, 128), F32)],
        compiler_params=pltpu.CompilerParams(vmem_limit_bytes=8 * MIB),
    )(sc, slots, target)


def spread(dst, at, x):
    n = x.shape[0]
    for k in range(8):
        dst[pl.ds(at + k, n, stride=8), :] = x[:, k * 128 : (k + 1) * 128]


def coefficient_row(view, m, drag, r, fz, fr, fc, inv):
    lane, sub = lanes()
    last, first = lane == 127, lane == 0
    end = last & (sub == 7)
    start = first & (sub == 0)
    prev = None
    for l in range(8):
        c = view(l, 0)
        fe = 0.5 * (c + jnp.where(end, 0.0, east(c, last)))
        fw = 0.5 * (c + jnp.where(start, 0.0, west(c, first)))
        south = 0.5 * (c + view(l, 1))
        north = 0.5 * (c + view(l, -1))
        below = 4.0 * c if l == 0 else prev
        above = 4.0 * (c + view(l + 1, 0)) if l < 7 else 4.0 * c
        fz[l, row(r), :] = above
        fr[l, row(r), :] = south
        fc[l, row(r), :] = jnp.where(end, 0.0, fe)
        rows_, cols_, both = north + south, fe + fw, below + above
        if l == 0:
            both = both + drag
        for k, (rw, cw) in enumerate(((4.0, 1.0), (1.0, 4.0))):
            diag = both + rw * rows_ + cw * cols_
            inv[k, l, row(r), :] = jnp.where(m, 0.7 / diag, 0.0)
        prev = above


def coef_kernel(sc, t1, t2, visc, other, fric, mask, bvel, svel, fz, fr, fc, inv, wgt, svm, msk, drg, v, bv):
    own, _ = place(sc)
    for i in range(4):
        for src, at in ((visc, own * 4 + i), (other, (1 - own) * 4 + i)):
            for h in range(0, ROWS, 16):
                spread(v.at[at], h * 8, src[i, h : h + 16, :].astype(F32))
    for h in range(0, ROWS, 16):
        spread(msk, h * 8, mask[h : h + 16, :].astype(F32))
        spread(drg, h * 8, fric[h : h + 16, :])
        spread(svm, h * 8, svel[own, h : h + 16, :])
        for c in range(2):
            spread(bv.at[c], h * 8, bvel[c, h : h + 16, :])

    def step(r, carry):
        m, d = msk[row(r), :], drg[row(r), :]
        coefficient_row(lambda l, j: v[l, row(r + j), :], m > 0.5, d, r + 2, fz, fr, fc, inv)
        svm[row(r), :] = svm[row(r), :] * m
        for c in range(2):
            wgt[c, row(r), :] = (-m * d) * bv[c, row(r), :]
        return carry

    lax.fori_loop(1, ROWS - 1, step, 0)
    for r in (0, ROWS - 1):
        m, d = msk[row(r), :], drg[row(r), :]
        svm[row(r), :] = svm[row(r), :] * m
        for c in range(2):
            wgt[c, row(r), :] = (-m * d) * bv[c, row(r), :]


def coefficients(sc, t1, t2, visc, other, fric, mask, bvel, svel):
    return pl.pallas_call(
        coef_kernel,
        in_specs=[sm()] * 3 + [vm()] * 6,
        out_specs=[vm()] * 9,
        out_shape=[
            kept(*FIELD),
            kept(*FIELD),
            kept(*FIELD),
            kept(2, *FIELD),
            kept(2, *STRIP),
            kept(*STRIP),
            kept(*STRIP),
            kept(*STRIP),
            kept(8, *STRIP),
        ],
        scratch_shapes=[pltpu.VMEM((2, *STRIP), F32)],
        compiler_params=pltpu.CompilerParams(vmem_limit_bytes=24 * MIB),
    )(sc, t1, t2, visc, near(other), fric, mask, bvel, svel)


def ghost_kernel(sc, ea, eb, ea2, eb2, msk, drg, v, fz0, fr0, fc0, inv0, fz, fr, fc, inv, g, u):
    own, odd = place(sc)
    for kind, pair in enumerate(((ea, ea2), (eb, eb2))):
        side = jnp.where((odd + kind) % 2 == 1, 0, 1)
        for who, e in enumerate(pair):
            spread(g.at[side, who], 0, e[...].astype(F32))
    for side in range(2):
        at = 0 if side == 0 else 2
        for who in range(2):
            base = (own if who == 0 else 1 - own) * 4
            for i in range(4):
                for r in range(3):
                    u[side, base + i, row(at + r), :] = g[side, who, pl.ds((i * 3 + r) * 8, 8), :]
        for l in range(8):
            for r in range(2):
                strip_row = r if side == 0 else ROWS - 2 + r
                u[side, l, row(3 * (1 - side) + r), :] = v[l, row(strip_row), :]
        for j in range(3):
            if side == 0:
                r, ghost, inside = j, j, 0
            else:
                r, ghost, inside = ROWS + 1 + j, j - 1, ROWS - 1
            if (side == 0 and j == 2) or (side == 1 and j == 0):
                m, d = msk[row(inside), :], drg[row(inside), :]
            else:
                m, d = g[side, 0, pl.ds((12 + ghost) * 8, 8), :], g[side, 0, pl.ds((14 + ghost) * 8, 8), :]
            coefficient_row(lambda l, s: u[side, l, row(j + 1 + s), :], m > 0.5, d, r, fz, fr, fc, inv)


def ghosts(sc, ea, eb, ea2, eb2, msk, drg, v, fz, fr, fc, inv):
    return pl.pallas_call(
        ghost_kernel,
        in_specs=[sm()] + [vm()] * 11,
        out_specs=[vm()] * 4,
        out_shape=[kept(*FIELD), kept(*FIELD), kept(*FIELD), kept(2, *FIELD)],
        scratch_shapes=[pltpu.VMEM((2, 2, 128, 128), F32), pltpu.VMEM((2, 8, 40, 128), F32)],
        input_output_aliases={8: 0, 9: 1, 10: 2, 11: 3},
        compiler_params=pltpu.CompilerParams(vmem_limit_bytes=24 * MIB),
    )(sc, *(near(x) for x in (ea, eb, ea2, eb2, msk, drg, v, fz, fr, fc, inv)))


def misfit_kernel(sc, got, svm, msk, m_out, ea, eb, hot, rhs, pc):
    _, odd = place(sc)
    p = lax.broadcasted_iota(jnp.int32, (512, 128), 0)
    pc[...] = code_of(p).astype(F32)
    lane = lax.broadcasted_iota(jnp.int32, (8, 128), 1)
    for b in range(32):
        for h in range(2):
            rhs[pl.ds(b * 128 + h * 64, 64), pl.ds(0, 128)] = got[2 * b + h, pl.ds(0, 64), :]
        c = jnp.where(
            lane < 64, got[2 * b, pl.ds(64, 8), :].astype(F32), got[2 * b + 1, pl.ds(64, 8), :].astype(F32)
        )
        same = pc[...].reshape(64, 8, 128) == c[None]
        hot[:, pl.ds(b * 128, 128)] = jnp.where(same, 1.0, 0.0).reshape(512, 128).astype(BF16)
    rhs[:, pl.ds(128, 128)] = jnp.ones((4096, 128), BF16)
    sums = jnp.dot(hot[...], rhs[...], preferred_element_type=F32)
    m_out[...] = sums[:, 128:] * svm[...] - msk[...] * sums[:, :128]
    for kind, e in enumerate((ea, eb)):
        at = jnp.where((odd + kind) % 2 == 0, ROWS - 2, 0)
        for r in range(2):
            e[pl.ds(r * 8, 8), :] = m_out[row(at + r), :]


def misfit(sc, got, svm, msk):
    return pl.pallas_call(
        misfit_kernel,
        in_specs=[sm()] + [vm()] * 3,
        out_specs=[vm()] * 3,
        out_shape=[kept(*STRIP), kept(16, 128), kept(16, 128)],
        scratch_shapes=[
            pltpu.VMEM((512, 4096), BF16),
            pltpu.VMEM((4096, 256), BF16),
            pltpu.VMEM((512, 128), F32),
        ],
        compiler_params=pltpu.CompilerParams(vmem_limit_bytes=24 * MIB),
    )(sc, near(got), near(svm), near(msk))


class Sweeps:
    def __init__(self, sc, t1, t2, c, coefs, a1, a2, a3, acc):
        self.own, self.odd = place(sc)
        self.c = c
        self.fz, self.fr, self.fc, self.inv, self.wgt = coefs
        self.a1, self.a2, self.a3, self.acc = a1, a2, a3, acc
        mine = [jnp.where(self.own == l // 4, t1[l % 4], t2[l % 4]) for l in range(8)]
        self.thick = mine
        self.rw = jnp.where(c == 0, 4.0, 1.0)
        self.cw = jnp.where(c == 0, 1.0, 4.0)
        lane, _ = lanes()
        self.last, self.first_lane = lane == 127, lane == 0

    def neighbours(self, a, l, r, x):
        here = row(r)
        n = None
        if l < 7:
            n = self.fz[l, here, :] * a[l + 1, here, :]
        if l > 0:
            t = self.fz[l - 1, here, :] * a[l - 1, here, :]
            n = t if n is None else n + t
        rows_ = self.fr[l, here, :] * a[l, row(r + 1), :] + self.fr[l, row(r - 1), :] * a[l, row(r - 1), :]
        f = self.fc[l, here, :]
        cols_ = f * east(x, self.last) + west(f * x, self.first_lane)
        return self.inv[self.c, l, here, :] * (n + self.rw * rows_ + self.cw * cols_)

    def first(self, r, m):
        for l in range(8):
            self.a1[l, row(r), :] = self.inv[self.c, l, row(r), :] * (self.thick[l] * m)

    def second(self, r):
        for l in range(8):
            x = self.a1[l, row(r), :]
            self.a2[l, row(r), :] = 1.3 * x + self.neighbours(self.a1, l, r, x)

    def third(self, r):
        total = None
        for l in range(8):
            x = self.a2[l, row(r), :]
            y = 0.3 * x + (self.a1[l, row(r), :] + self.neighbours(self.a2, l, r, x))
            self.a3[l, row(r - 2), :] = y
            total = self.thick[l] * y if l == 0 else total + self.thick[l] * y
        self.acc[row(r - 2), :] = self.wgt[self.c, row(r - 2), :] * total

    def interior(self, m):
        def load(r):
            return m[row(r - 2), :]

        for r in (2, 3, 4):
            self.first(r, load(r))
        for r in (3, 4, 5):
            self.second(r)
            self.first(r + 2, load(r + 2))

        def step(r, carry):
            self.third(r - 2)
            self.second(r)
            self.first(r + 2, load(r + 2))
            return carry

        lax.fori_loop(6, 64, step, 0)
        self.third(62)
        self.second(64)
        self.third(63)

    def edges(self, ga, gb):
        up = jnp.where(self.odd == 1, ga[...], gb[...])
        down = jnp.where(self.odd == 1, gb[...], ga[...])
        for ghost, firsts, seconds, thirds in (
            (up, (0, 1), (1, 2), (2, 3)),
            (down, (66, 67), (65, 66), (64, 65)),
        ):
            for i, r in enumerate(firsts):
                self.first(r, ghost[i * 8 : i * 8 + 8, :])
            for r in seconds:
                self.second(r)
            for r in thirds:
                self.third(r)


def gather_rows(dst, src):
    for h in range(0, ROWS, 8):
        for k in range(8):
            dst[pl.ds(h, 8), pl.ds(k * 128, 128)] = src[pl.ds(h * 8 + k, 8, stride=8), :]


def own_kernel(sc, t1, t2, m, fz, fr, fc, inv, wgt, a1, a2, a3, acc):
    own, _ = place(sc)
    Sweeps(sc, t1, t2, own, (fz, fr, fc, inv, wgt), a1, a2, a3, acc).interior(m)


STATE = (FIELD, FIELD, (8, *STRIP), STRIP)


def own_sweeps(sc, t1, t2, m, coefs):
    return pl.pallas_call(
        own_kernel,
        in_specs=[sm()] * 3 + [vm()] * 6,
        out_specs=[vm()] * 4,
        out_shape=[kept(*s) for s in STATE],
        compiler_params=pltpu.CompilerParams(vmem_limit_bytes=24 * MIB),
    )(sc, t1, t2, near(m), *(near(x) for x in coefs))


def both_kernel(sc, t1, t2, ga, gb, m, fz, fr, fc, inv, wgt, *refs):
    (_, _, _, _), (b1, b2, b3, bacc, a1, a2, a3, acc, adj), (stage, sem) = refs[:4], refs[4:13], refs[13:]
    own, _ = place(sc)
    coefs = (fz, fr, fc, inv, wgt)
    Sweeps(sc, t1, t2, own, coefs, b1, b2, b3, bacc).edges(ga, gb)
    for i in range(4):
        gather_rows(stage.at[i], b3.at[own * 4 + i])
    copy = pltpu.make_async_copy(stage, adj.at[own], sem)
    copy.start()
    Sweeps(sc, t1, t2, 1 - own, coefs, a1, a2, a3, acc).interior(m)
    copy.wait()


def both_sweeps(sc, t1, t2, ga, gb, m, coefs, state):
    return pl.pallas_call(
        both_kernel,
        in_specs=[sm()] * 3 + [vm()] * 12,
        out_specs=[vm()] * 8 + [hbm()],
        out_shape=[kept(*s) for s in STATE] * 2 + [jax.ShapeDtypeStruct((2, 4, ROWS, 1024), F32)],
        scratch_shapes=[pltpu.VMEM((4, ROWS, 1024), F32), pltpu.SemaphoreType.DMA],
        input_output_aliases={11: 0, 12: 1, 13: 2, 14: 3},
        compiler_params=pltpu.CompilerParams(vmem_limit_bytes=24 * MIB),
    )(sc, t1, t2, near(ga), near(gb), near(m), *(near(x) for x in coefs), *(near(x) for x in state))


def last_kernel(sc, t1, t2, g, racc, fz, fr, fc, inv, wgt, *refs):
    (_, _, _, _, _), (a1, a2, a3, acc, adj, grad), (stage, sem) = refs[:5], refs[5:11], refs[11:]
    own, _ = place(sc)
    Sweeps(sc, t1, t2, 1 - own, (fz, fr, fc, inv, wgt), a1, a2, a3, acc).edges(
        g.at[pl.ds(0, 16), :], g.at[pl.ds(16, 16), :]
    )
    for i in range(4):
        gather_rows(stage.at[i], a3.at[own * 4 + i])
    copy = pltpu.make_async_copy(stage, adj.at[1 - own], sem)
    copy.start()
    acc[...] = acc[...] + racc[...]
    gather_rows(grad, acc)
    copy.wait()


def last_sweeps(sc, t1, t2, g, racc, coefs, state, adj):
    return pl.pallas_call(
        last_kernel,
        in_specs=[sm()] * 3 + [vm()] * 11 + [hbm()],
        out_specs=[vm()] * 4 + [hbm(), vm()],
        out_shape=[kept(*s) for s in STATE]
        + [jax.ShapeDtypeStruct((2, 4, ROWS, 1024), F32), jax.ShapeDtypeStruct((ROWS, 1024), F32)],
        scratch_shapes=[pltpu.VMEM((4, ROWS, 1024), F32), pltpu.SemaphoreType.DMA],
        input_output_aliases={10: 0, 11: 1, 12: 2, 13: 3, 14: 4},
        compiler_params=pltpu.CompilerParams(vmem_limit_bytes=24 * MIB),
    )(sc, t1, t2, near(g), near(racc), *(near(x) for x in coefs), *(near(x) for x in state), adj)[4:]


def swaps(tiles, offset, across):
    perm = []
    for t in range(offset, tiles - 1, 2):
        for layer in range(2):
            a, b = t * 2 + layer, (t + 1) * 2 + (1 - layer if across else layer)
            perm += [(a, b), (b, a)]
    return perm


def swap_layers(x):
    return lax.ppermute(x, "layer", [(0, 1), (1, 0)])


def body(viscosity, friction, base_vel, surf_vel, layer_thick, ice_mask, obs_slots, obs_target):
    tiles = lax.axis_size("tile")
    own = lax.axis_index("layer")
    odd = lax.axis_index("tile") % 2
    sc = (own + 2 * odd).astype(jnp.int32).reshape(1)

    def swap(x, kind, across=False):
        return lax.ppermute(x, PAIR, swaps(tiles, kind, across))

    other = swap_layers(viscosity.astype(BF16))
    payload = pack(sc, obs_slots.reshape(tiles, 128, 128), obs_target)
    got = lax.all_to_all(payload, "tile", split_axis=0, concat_axis=0, tiled=True)
    thick_other = swap_layers(layer_thick)

    def edge(at):
        return jnp.concatenate(
            [
                lax.slice_in_dim(viscosity, (ROWS - 3) if at else 0, ROWS if at else 3, axis=1).reshape(12, 1024),
                lax.slice_in_dim(ice_mask, (ROWS - 2) if at else 0, ROWS if at else 2, axis=0).astype(F32),
                lax.slice_in_dim(friction, (ROWS - 2) if at else 0, ROWS if at else 2, axis=0),
            ]
        ).astype(BF16)

    top, bottom = edge(0), edge(1)
    to_a = jnp.where(odd == 0, bottom, top)
    to_b = jnp.where(odd == 0, top, bottom)
    near_rows = (swap(to_a, 0), swap(to_b, 1), swap(to_a, 0, True), swap(to_b, 1, True))
    fz, fr, fc, inv, wgt, svm, msk, drg, v = coefficients(
        sc, layer_thick, thick_other, viscosity, other, friction, ice_mask, base_vel, surf_vel
    )
    fz, fr, fc, inv = ghosts(sc, *near_rows, msk, drg, v, fz, fr, fc, inv)
    coefs = (fz, fr, fc, inv, wgt)

    m_own, ea, eb = misfit(sc, got, svm, msk)
    ga, gb = swap(ea, 0), swap(eb, 1)
    m_oth = swap_layers(m_own)
    state = own_sweeps(sc, layer_thick, thick_other, m_own, coefs)
    g_oth = swap_layers(jnp.concatenate([ga, gb]))
    *both, adj = both_sweeps(sc, layer_thick, thick_other, ga, gb, m_oth, coefs, state)
    adjoint, gradient = last_sweeps(sc, layer_thick, thick_other, g_oth, both[3], coefs, both[4:], adj)
    return adjoint, gradient


def solution(mesh):
    in_specs = (
        P("layer", "tile", None),
        P("tile", None),
        P(None, "tile", None),
        P(None, "tile", None),
        P("layer"),
        P("tile", None),
        P("tile", None, None, None),
        P("tile", None),
    )
    out_specs = (P(None, "layer", "tile", None), P("tile", None))
    return jax.shard_map(body, mesh=mesh, in_specs=in_specs, out_specs=out_specs, check_vma=False)
```

```python
import jax
import jax.numpy as jnp
from jax import lax
from jax.experimental import pallas as pl
from jax.experimental.pallas import tpu as pltpu
from jax.sharding import PartitionSpec as P


F32 = jnp.float32
BF16 = jnp.bfloat16
ROWS = 64
EXT = 68
PAIR = ("tile", "layer")
FIELD = (8, EXT * 8, 128)
STRIP = (ROWS * 8, 128)
MIB = 1 << 20


def vm():
    return pl.BlockSpec(memory_space=pltpu.VMEM)


def sm():
    return pl.BlockSpec(memory_space=pltpu.SMEM)


def hbm():
    return pl.BlockSpec(memory_space=pltpu.HBM)


def far(x):
    return pltpu.with_memory_space_constraint(x, pltpu.HBM)


def kept(*shape, dtype=F32):
    return pltpu.VMEM(shape, dtype)


def near(x):
    return pltpu.with_memory_space_constraint(x, pltpu.VMEM)


def row(r):
    return pl.ds(pl.multiple_of(r * 8, 8), 8)


def place(sc):
    return sc[0] & 1, sc[0] >> 1


def lanes():
    lane = lax.broadcasted_iota(jnp.int32, (8, 128), 1)
    sub = lax.broadcasted_iota(jnp.int32, (8, 128), 0)
    return lane, sub


def east(x, last):
    r = pltpu.roll(x, 127, 1)
    return jnp.where(last, pltpu.roll(r, 7, 0), r)


def west(x, first):
    r = pltpu.roll(x, 1, 1)
    return jnp.where(first, pltpu.roll(r, 1, 0), r)


def code_of(t):
    return jnp.where(t < 512, (128 + (t & 127)) << (t >> 7), 0)


def pack_kernel(sc, slots, target, o, x, y, t, f, codes, sin, sout, st):
    own, _ = place(sc)
    n = slots.shape[0]
    step = n // CHUNKS
    tin = pltpu.make_async_copy(target, t, st)
    tin.start()
    ins = [
        pltpu.make_async_copy(slots.at[pl.ds(i * step, step)], x.at[pl.ds(i * step, step)], sin.at[i])
        for i in range(CHUNKS)
    ]
    outs = [
        pltpu.make_async_copy(y.at[pl.ds(i * step, step)], o.at[pl.ds(i * step, step)], sout.at[i])
        for i in range(CHUNKS)
    ]
    for i in ins:
        i.start()
    tin.wait()
    c = code_of(t[...]).astype(F32)
    codes[...] = jnp.concatenate([c, c], axis=1)
    for i in range(CHUNKS):
        ins[i].wait()

        def one(d, carry):
            f[d] = x[d].astype(F32)
            y[d, pl.ds(0, 64), :] = f[d, pl.ds(own, 64, stride=2), :].astype(BF16)
            y[d, pl.ds(64, 8), :] = jnp.broadcast_to(codes[pl.ds(d, 1), :], (8, 128)).astype(BF16)
            return carry

        lax.fori_loop(i * step, (i + 1) * step, one, 0, unroll=8)
        outs[i].start()
    for i in outs:
        i.wait()


CHUNKS = 4


def pack(sc, slots, target):
    n = slots.shape[0]
    return pl.pallas_call(
        pack_kernel,
        in_specs=[sm(), hbm(), hbm()],
        out_specs=hbm(),
        out_shape=pltpu.HBM((n, 72, 128), BF16),
        scratch_shapes=[
            pltpu.VMEM((n, 128, 128), BF16),
            pltpu.VMEM((n, 72, 128), BF16),
            pltpu.VMEM((n, 64), jnp.int32),
            pltpu.VMEM((n, 128, 128), F32),
            pltpu.VMEM((n, 128), F32),
            pltpu.SemaphoreType.DMA((CHUNKS,)),
            pltpu.SemaphoreType.DMA((CHUNKS,)),
            pltpu.SemaphoreType.DMA,
        ],
        compiler_params=pltpu.CompilerParams(vmem_limit_bytes=16 * MIB),
    )(sc, far(slots), far(target))


def edge_kernel(sc, visc, mask, fric, to_a, to_b, v, m, d, s, sem):
    _, odd = place(sc)
    copies = []
    for side in range(2):
        at = pl.ds(side * (ROWS - 8), 8)
        copies.append(pltpu.make_async_copy(visc.at[:, at, :], v.at[side], sem.at[side * 3]))
        copies.append(pltpu.make_async_copy(mask.at[at, :], m.at[side], sem.at[side * 3 + 1]))
        copies.append(pltpu.make_async_copy(fric.at[at, :], d.at[side], sem.at[side * 3 + 2]))
    for c in copies:
        c.start()
    for c in copies:
        c.wait()
    for side in range(2):
        for i in range(4):
            s[side, pl.ds(3 * i, 3), :] = v[side, i, pl.ds(5 * side, 3), :]
        s[side, pl.ds(12, 2), :] = m[side, pl.ds(6 * side, 2), :].astype(F32)
        s[side, pl.ds(14, 2), :] = d[side, pl.ds(6 * side, 2), :]
    to_a[...] = s[1 - odd].astype(BF16)
    to_b[...] = s[odd].astype(BF16)


def edge_rows(sc, visc, mask, fric):
    return pl.pallas_call(
        edge_kernel,
        in_specs=[sm(), hbm(), hbm(), hbm()],
        out_specs=[vm()] * 2,
        out_shape=[kept(16, 1024, dtype=BF16)] * 2,
        scratch_shapes=[
            pltpu.VMEM((2, 4, 8, 1024), F32),
            pltpu.VMEM((2, 8, 1024), jnp.int32),
            pltpu.VMEM((2, 8, 1024), F32),
            pltpu.VMEM((2, 16, 1024), F32),
            pltpu.SemaphoreType.DMA((6,)),
        ],
        compiler_params=pltpu.CompilerParams(vmem_limit_bytes=8 * MIB),
    )(sc, far(visc), far(mask), far(fric))


def spread(dst, at, x):
    n = x.shape[0]
    for k in range(8):
        dst[pl.ds(at + k, n, stride=8), :] = x[:, k * 128 : (k + 1) * 128]


def coefficient_row(view, m, drag, r, fz, fr, fc, inv):
    lane, sub = lanes()
    last, first = lane == 127, lane == 0
    end = last & (sub == 7)
    start = first & (sub == 0)
    prev = None
    for l in range(8):
        c = view(l, 0)
        fe = 0.5 * (c + jnp.where(end, 0.0, east(c, last)))
        fw = 0.5 * (c + jnp.where(start, 0.0, west(c, first)))
        south = 0.5 * (c + view(l, 1))
        north = 0.5 * (c + view(l, -1))
        below = 4.0 * c if l == 0 else prev
        above = 4.0 * (c + view(l + 1, 0)) if l < 7 else 4.0 * c
        fz[l, row(r), :] = above
        fr[l, row(r), :] = south
        fc[l, row(r), :] = jnp.where(end, 0.0, fe)
        rows_, cols_, both = north + south, fe + fw, below + above
        if l == 0:
            both = both + drag
        for k, (rw, cw) in enumerate(((4.0, 1.0), (1.0, 4.0))):
            diag = both + rw * rows_ + cw * cols_
            inv[k, l, row(r), :] = jnp.where(m, 0.7 / diag, 0.0)
        prev = above


GROUPS = ((2, 16), (16, 32), (32, 48), (48, 66))


def coef_kernel(sc, visc, other, fric, mask, bvel, svel, *refs):
    outs, (fz, fr, fc, inv, wgt, svm, msk, drg, v, bv, sem, sem2) = refs[:9], refs[9:]
    own, _ = place(sc)
    for i in range(4):
        for src, at in ((visc, own * 4 + i), (other, (1 - own) * 4 + i)):
            for h in range(0, ROWS, 16):
                spread(v.at[at], h * 8, src[i, h : h + 16, :].astype(F32))
    for h in range(0, ROWS, 16):
        spread(msk, h * 8, mask[h : h + 16, :].astype(F32))
        spread(drg, h * 8, fric[h : h + 16, :])
        spread(svm, h * 8, svel[own, h : h + 16, :])
        for c in range(2):
            spread(bv.at[c], h * 8, bvel[c, h : h + 16, :])

    def strips(r):
        m, d = msk[row(r), :], drg[row(r), :]
        svm[row(r), :] = svm[row(r), :] * m
        for c in range(2):
            wgt[c, row(r), :] = (-m * d) * bv[c, row(r), :]
        return m, d

    def step(r, carry):
        m, d = strips(r)
        coefficient_row(lambda l, j: v[l, row(r + j), :], m > 0.5, d, r + 2, fz, fr, fc, inv)
        return carry

    strips(0)
    strips(ROWS - 1)
    copies = []
    for i, (src, dst) in enumerate(zip((msk, drg, v), (outs[6], outs[7], outs[8]))):
        copies.append(pltpu.make_async_copy(src, dst, sem2.at[i]))
    for c in copies:
        c.start()
    for k, (a, b) in enumerate(GROUPS):
        lax.fori_loop(max(a - 2, 1), min(b - 2, ROWS - 1), step, 0)
        part = pl.ds(a * 8, (b - a) * 8)
        for i, src in enumerate((fz, fr, fc)):
            copies.append(pltpu.make_async_copy(src.at[:, part, :], outs[i].at[:, part, :], sem.at[k, i]))
            copies[-1].start()
        copies.append(pltpu.make_async_copy(inv.at[:, :, part, :], outs[3].at[:, :, part, :], sem.at[k, 3]))
        copies[-1].start()
    for i, (src, dst) in enumerate(zip((wgt, svm), (outs[4], outs[5]))):
        copies.append(pltpu.make_async_copy(src, dst, sem2.at[3 + i]))
        copies[-1].start()
    for c in copies:
        c.wait()


def coefficients(sc, visc, other, fric, mask, bvel, svel):
    shapes = (FIELD, FIELD, FIELD, (2, *FIELD), (2, *STRIP), STRIP, STRIP, STRIP, (8, *STRIP))
    return pl.pallas_call(
        coef_kernel,
        in_specs=[sm()] + [vm()] * 6,
        out_specs=[hbm()] * 9,
        out_shape=[pltpu.HBM(x, F32) for x in shapes],
        scratch_shapes=[pltpu.VMEM(x, F32) for x in shapes]
        + [
            pltpu.VMEM((2, *STRIP), F32),
            pltpu.SemaphoreType.DMA((len(GROUPS), 4)),
            pltpu.SemaphoreType.DMA((5,)),
        ],
        compiler_params=pltpu.CompilerParams(vmem_limit_bytes=32 * MIB),
    )(sc, visc, other, fric, mask, bvel, svel)


def ghost_kernel(sc, ea, eb, ea2, eb2, msk, drg, v, fz0, fr0, fc0, inv0, fz, fr, fc, inv, g, u):
    own, odd = place(sc)
    for kind, pair in enumerate(((ea, ea2), (eb, eb2))):
        side = jnp.where((odd + kind) % 2 == 1, 0, 1)
        for who, e in enumerate(pair):
            spread(g.at[side, who], 0, e[...].astype(F32))
    for side in range(2):
        at = 0 if side == 0 else 2
        for who in range(2):
            base = (own if who == 0 else 1 - own) * 4
            for i in range(4):
                for r in range(3):
                    u[side, base + i, row(at + r), :] = g[side, who, pl.ds((i * 3 + r) * 8, 8), :]
        for l in range(8):
            for r in range(2):
                strip_row = r if side == 0 else ROWS - 2 + r
                u[side, l, row(3 * (1 - side) + r), :] = v[l, row(strip_row), :]
        for j in range(3):
            if side == 0:
                r, ghost, inside = j, j, 0
            else:
                r, ghost, inside = ROWS + 1 + j, j - 1, ROWS - 1
            if (side == 0 and j == 2) or (side == 1 and j == 0):
                m, d = msk[row(inside), :], drg[row(inside), :]
            else:
                m, d = g[side, 0, pl.ds((12 + ghost) * 8, 8), :], g[side, 0, pl.ds((14 + ghost) * 8, 8), :]
            coefficient_row(lambda l, s: u[side, l, row(j + 1 + s), :], m > 0.5, d, r, fz, fr, fc, inv)


def ghosts(sc, ea, eb, ea2, eb2, msk, drg, v, fz, fr, fc, inv):
    return pl.pallas_call(
        ghost_kernel,
        in_specs=[sm()] + [vm()] * 11,
        out_specs=[vm()] * 4,
        out_shape=[kept(*FIELD), kept(*FIELD), kept(*FIELD), kept(2, *FIELD)],
        scratch_shapes=[pltpu.VMEM((2, 2, 128, 128), F32), pltpu.VMEM((2, 8, 40, 128), F32)],
        input_output_aliases={8: 0, 9: 1, 10: 2, 11: 3},
        compiler_params=pltpu.CompilerParams(vmem_limit_bytes=24 * MIB),
    )(sc, *(near(x) for x in (ea, eb, ea2, eb2, msk, drg, v, fz, fr, fc, inv)))


PARTS = 4


def misfit_kernel(sc, got_h, svm_h, *refs):
    here, m_out, ea, eb = refs[:8], *refs[8:11]
    kept_, (got, svm, hot, rhs, pc, sem, sem2) = refs[11:19], refs[19:]
    _, odd = place(sc)
    n = got.shape[0] // PARTS
    parts = [
        pltpu.make_async_copy(got_h.at[pl.ds(i * n, n)], got.at[pl.ds(i * n, n)], sem.at[i]) for i in range(PARTS)
    ]
    strips = pltpu.make_async_copy(svm_h, svm, sem.at[PARTS])
    rest = [pltpu.make_async_copy(x, y, sem2.at[i]) for i, (x, y) in enumerate(zip(here, kept_))]
    for c in (*parts, strips, *rest):
        c.start()
    msk = kept_[0]
    p = lax.broadcasted_iota(jnp.int32, (512, 128), 0)
    pc[...] = code_of(p).astype(F32)
    rhs[:, pl.ds(128, 128)] = jnp.ones((4096, 128), BF16)
    lane = lax.broadcasted_iota(jnp.int32, (8, 128), 1)
    for b in range(32):
        if b % (32 // PARTS) == 0:
            parts[b // (32 // PARTS)].wait()
        for h in range(2):
            rhs[pl.ds(b * 128 + h * 64, 64), pl.ds(0, 128)] = got[2 * b + h, pl.ds(0, 64), :]
        c = jnp.where(
            lane < 64, got[2 * b, pl.ds(64, 8), :].astype(F32), got[2 * b + 1, pl.ds(64, 8), :].astype(F32)
        )
        same = pc[...].reshape(64, 8, 128) == c[None]
        hot[:, pl.ds(b * 128, 128)] = jnp.where(same, 1.0, 0.0).reshape(512, 128).astype(BF16)
    sums = jnp.dot(hot[...], rhs[...], preferred_element_type=F32)
    strips.wait()
    rest[0].wait()
    m_out[...] = sums[:, 128:] * svm[...] - msk[...] * sums[:, :128]
    for kind, e in enumerate((ea, eb)):
        at = jnp.where((odd + kind) % 2 == 0, ROWS - 2, 0)
        for r in range(2):
            e[pl.ds(r * 8, 8), :] = m_out[row(at + r), :]
    for c in rest[1:]:
        c.wait()


def misfit(sc, got, svm, *rest):
    return pl.pallas_call(
        misfit_kernel,
        in_specs=[sm()] + [hbm()] * 10,
        out_specs=[vm()] * 11,
        out_shape=[kept(*STRIP), kept(16, 128), kept(16, 128)] + [kept(*x.shape) for x in rest],
        scratch_shapes=[
            pltpu.VMEM(got.shape, BF16),
            pltpu.VMEM(STRIP, F32),
            pltpu.VMEM((512, 4096), BF16),
            pltpu.VMEM((4096, 256), BF16),
            pltpu.VMEM((512, 128), F32),
            pltpu.SemaphoreType.DMA((PARTS + 1,)),
            pltpu.SemaphoreType.DMA((8,)),
        ],
        compiler_params=pltpu.CompilerParams(vmem_limit_bytes=24 * MIB),
    )(sc, *(far(x) for x in (got, svm, *rest)))


class Sweeps:
    def __init__(self, sc, t1, t2, c, coefs, a1, a2, a3, acc):
        self.own, self.odd = place(sc)
        self.c = c
        self.fz, self.fr, self.fc, self.inv, self.wgt = coefs
        self.a1, self.a2, self.a3, self.acc = a1, a2, a3, acc
        mine = [jnp.where(self.own == l // 4, t1[l % 4], t2[l % 4]) for l in range(8)]
        self.thick = mine
        self.rw = jnp.where(c == 0, 4.0, 1.0)
        self.cw = jnp.where(c == 0, 1.0, 4.0)
        lane, _ = lanes()
        self.last, self.first_lane = lane == 127, lane == 0

    def neighbours(self, a, l, r, x):
        here = row(r)
        n = None
        if l < 7:
            n = self.fz[l, here, :] * a[l + 1, here, :]
        if l > 0:
            t = self.fz[l - 1, here, :] * a[l - 1, here, :]
            n = t if n is None else n + t
        rows_ = self.fr[l, here, :] * a[l, row(r + 1), :] + self.fr[l, row(r - 1), :] * a[l, row(r - 1), :]
        f = self.fc[l, here, :]
        cols_ = f * east(x, self.last) + west(f * x, self.first_lane)
        return self.inv[self.c, l, here, :] * (n + self.rw * rows_ + self.cw * cols_)

    def first(self, r, m):
        for l in range(8):
            self.a1[l, row(r), :] = self.inv[self.c, l, row(r), :] * (self.thick[l] * m)

    def second(self, r):
        for l in range(8):
            x = self.a1[l, row(r), :]
            self.a2[l, row(r), :] = 1.3 * x + self.neighbours(self.a1, l, r, x)

    def third(self, r):
        total = None
        for l in range(8):
            x = self.a2[l, row(r), :]
            y = 0.3 * x + (self.a1[l, row(r), :] + self.neighbours(self.a2, l, r, x))
            self.a3[l, row(r - 2), :] = y
            total = self.thick[l] * y if l == 0 else total + self.thick[l] * y
        self.acc[row(r - 2), :] = self.wgt[self.c, row(r - 2), :] * total

    def interior(self, m):
        def load(r):
            return m[row(r - 2), :]

        for r in (2, 3, 4):
            self.first(r, load(r))
        for r in (3, 4, 5):
            self.second(r)
            self.first(r + 2, load(r + 2))

        def step(r, carry):
            self.third(r - 2)
            self.second(r)
            self.first(r + 2, load(r + 2))
            return carry

        lax.fori_loop(6, 64, step, 0)
        self.third(62)
        self.second(64)
        self.third(63)

    def edges(self, ga, gb):
        up = jnp.where(self.odd == 1, ga[...], gb[...])
        down = jnp.where(self.odd == 1, gb[...], ga[...])
        for ghost, firsts, seconds, thirds in (
            (up, (0, 1), (1, 2), (2, 3)),
            (down, (66, 67), (65, 66), (64, 65)),
        ):
            for i, r in enumerate(firsts):
                self.first(r, ghost[i * 8 : i * 8 + 8, :])
            for r in seconds:
                self.second(r)
            for r in thirds:
                self.third(r)


def gather_rows(dst, src):
    for h in range(0, ROWS, 8):
        for k in range(8):
            dst[pl.ds(h, 8), pl.ds(k * 128, 128)] = src[pl.ds(h * 8 + k, 8, stride=8), :]


def own_kernel(sc, t1, t2, m, fz, fr, fc, inv, wgt, a1, a2, a3, acc):
    own, _ = place(sc)
    Sweeps(sc, t1, t2, own, (fz, fr, fc, inv, wgt), a1, a2, a3, acc).interior(m)


STATE = (FIELD, FIELD, (8, *STRIP), STRIP)


def own_sweeps(sc, t1, t2, m, coefs):
    return pl.pallas_call(
        own_kernel,
        in_specs=[sm()] * 3 + [vm()] * 6,
        out_specs=[vm()] * 4,
        out_shape=[kept(*s) for s in STATE],
        compiler_params=pltpu.CompilerParams(vmem_limit_bytes=24 * MIB),
    )(sc, t1, t2, near(m), *(near(x) for x in coefs))


def both_kernel(sc, t1, t2, ga, gb, m, fz, fr, fc, inv, wgt, *refs):
    (_, _, _, _), (b1, b2, b3, bacc, a1, a2, a3, acc, adj), (stage, sem) = refs[:4], refs[4:13], refs[13:]
    own, _ = place(sc)
    coefs = (fz, fr, fc, inv, wgt)
    Sweeps(sc, t1, t2, own, coefs, b1, b2, b3, bacc).edges(ga, gb)
    for i in range(4):
        gather_rows(stage.at[i], b3.at[own * 4 + i])
    copy = pltpu.make_async_copy(stage, adj.at[own], sem)
    copy.start()
    Sweeps(sc, t1, t2, 1 - own, coefs, a1, a2, a3, acc).interior(m)
    copy.wait()


def both_sweeps(sc, t1, t2, ga, gb, m, coefs, state):
    return pl.pallas_call(
        both_kernel,
        in_specs=[sm()] * 3 + [vm()] * 12,
        out_specs=[vm()] * 8 + [hbm()],
        out_shape=[kept(*s) for s in STATE] * 2 + [pltpu.HBM((2, 4, ROWS, 1024), F32)],
        scratch_shapes=[pltpu.VMEM((4, ROWS, 1024), F32), pltpu.SemaphoreType.DMA],
        input_output_aliases={11: 0, 12: 1, 13: 2, 14: 3},
        compiler_params=pltpu.CompilerParams(vmem_limit_bytes=24 * MIB),
    )(sc, t1, t2, near(ga), near(gb), near(m), *(near(x) for x in coefs), *(near(x) for x in state))


def last_kernel(sc, t1, t2, g, racc, fz, fr, fc, inv, wgt, *refs):
    (_, _, _, _, _), (a1, a2, a3, acc, adj, grad), (stage, sem) = refs[:5], refs[5:11], refs[11:]
    own, _ = place(sc)
    Sweeps(sc, t1, t2, 1 - own, (fz, fr, fc, inv, wgt), a1, a2, a3, acc).edges(
        g.at[pl.ds(0, 16), :], g.at[pl.ds(16, 16), :]
    )
    for i in range(4):
        gather_rows(stage.at[i], a3.at[own * 4 + i])
    copy = pltpu.make_async_copy(stage, adj.at[1 - own], sem)
    copy.start()
    acc[...] = acc[...] + racc[...]
    gather_rows(grad, acc)
    copy.wait()


def last_sweeps(sc, t1, t2, g, racc, coefs, state, adj):
    return pl.pallas_call(
        last_kernel,
        in_specs=[sm()] * 3 + [vm()] * 11 + [hbm()],
        out_specs=[vm()] * 4 + [hbm(), vm()],
        out_shape=[kept(*s) for s in STATE]
        + [pltpu.HBM((2, 4, ROWS, 1024), F32), jax.ShapeDtypeStruct((ROWS, 1024), F32)],
        scratch_shapes=[pltpu.VMEM((4, ROWS, 1024), F32), pltpu.SemaphoreType.DMA],
        input_output_aliases={10: 0, 11: 1, 12: 2, 13: 3, 14: 4},
        compiler_params=pltpu.CompilerParams(vmem_limit_bytes=24 * MIB),
    )(sc, t1, t2, near(g), near(racc), *(near(x) for x in coefs), *(near(x) for x in state), far(adj))[4:]


def swaps(tiles, offset, across):
    perm = []
    for t in range(offset, tiles - 1, 2):
        for layer in range(2):
            a, b = t * 2 + layer, (t + 1) * 2 + (1 - layer if across else layer)
            perm += [(a, b), (b, a)]
    return perm


def swap_layers(x):
    return lax.ppermute(x, "layer", [(0, 1), (1, 0)])


def body(viscosity, friction, base_vel, surf_vel, layer_thick, ice_mask, obs_slots, obs_target):
    tiles = lax.axis_size("tile")
    own = lax.axis_index("layer")
    odd = lax.axis_index("tile") % 2
    sc = (own + 2 * odd).astype(jnp.int32).reshape(1)

    def swap(x, kind, across=False):
        return lax.ppermute(x, PAIR, swaps(tiles, kind, across))

    other = swap_layers(viscosity.astype(BF16))
    payload = pack(sc, obs_slots.reshape(tiles, 128, 128), obs_target)
    got = lax.all_to_all(payload, "tile", split_axis=0, concat_axis=0, tiled=True)
    thick_other = swap_layers(layer_thick)

    to_a, to_b = edge_rows(sc, viscosity, ice_mask, friction)
    near_rows = (swap(to_a, 0), swap(to_b, 1), swap(to_a, 0, True), swap(to_b, 1, True))
    fz, fr, fc, inv, wgt, svm, msk, drg, v = coefficients(sc, viscosity, other, friction, ice_mask, base_vel, surf_vel)
    got, near_rows, thick_other = lax.optimization_barrier((got, near_rows, thick_other))
    m_own, ea, eb, msk, drg, v, fz, fr, fc, inv, wgt = misfit(
        sc, got, svm, msk, drg, v, fz, fr, fc, inv, wgt
    )
    fz, fr, fc, inv = ghosts(sc, *near_rows, msk, drg, v, fz, fr, fc, inv)
    coefs = (fz, fr, fc, inv, wgt)

    ga, gb = swap(ea, 0), swap(eb, 1)
    m_oth = swap_layers(m_own)
    state = own_sweeps(sc, layer_thick, thick_other, m_own, coefs)
    g_oth = swap_layers(jnp.concatenate([ga, gb]))
    *both, adj = both_sweeps(sc, layer_thick, thick_other, ga, gb, m_oth, coefs, state)
    adjoint, gradient = last_sweeps(sc, layer_thick, thick_other, g_oth, both[3], coefs, both[4:], adj)
    return adjoint, gradient


def solution(mesh):
    in_specs = (
        P("layer", "tile", None),
        P("tile", None),
        P(None, "tile", None),
        P(None, "tile", None),
        P("layer"),
        P("tile", None),
        P("tile", None, None, None),
        P("tile", None),
    )
    out_specs = (P(None, "layer", "tile", None), P("tile", None))

    return jax.shard_map(body, mesh=mesh, in_specs=in_specs, out_specs=out_specs, check_vma=False)
```

```python
import jax
import jax.numpy as jnp
from jax import lax
from jax.experimental import pallas as pl
from jax.experimental.pallas import tpu as pltpu
from jax.sharding import PartitionSpec as P


F32 = jnp.float32
BF16 = jnp.bfloat16
ROWS = 64
EXT = 68
PAIR = ("tile", "layer")
FIELD = (EXT, 64, 128)
STRIP = (ROWS * 8, 128)
MIB = 1 << 20


def vm():
    return pl.BlockSpec(memory_space=pltpu.VMEM)


def sm():
    return pl.BlockSpec(memory_space=pltpu.SMEM)


def hbm():
    return pl.BlockSpec(memory_space=pltpu.HBM)


def far(x):
    return pltpu.with_memory_space_constraint(x, pltpu.HBM)


def kept(*shape, dtype=F32):
    return pltpu.VMEM(shape, dtype)


def near(x):
    return pltpu.with_memory_space_constraint(x, pltpu.VMEM)


def row(r):
    return pl.ds(pl.multiple_of(r * 8, 8), 8)


def at(l):
    return pl.ds(l * 8, 8)


def place(sc):
    return sc[0] & 1, sc[0] >> 1


def lanes():
    lane = lax.broadcasted_iota(jnp.int32, (8, 128), 1)
    sub = lax.broadcasted_iota(jnp.int32, (8, 128), 0)
    return lane, sub


def east(x, last):
    r = pltpu.roll(x, 127, 1)
    return jnp.where(last, pltpu.roll(r, 7, 0), r)


def west(x, first):
    r = pltpu.roll(x, 1, 1)
    return jnp.where(first, pltpu.roll(r, 1, 0), r)


def code_of(t):
    return jnp.where(t < 512, (128 + (t & 127)) << (t >> 7), 0)


def pack_kernel(sc, slots, target, o, x, y, t, f, codes, sin, sout, st):
    own, _ = place(sc)
    n = slots.shape[0]
    step = n // CHUNKS
    tin = pltpu.make_async_copy(target, t, st)
    tin.start()
    ins = [
        pltpu.make_async_copy(slots.at[pl.ds(i * step, step)], x.at[pl.ds(i * step, step)], sin.at[i])
        for i in range(CHUNKS)
    ]
    outs = [
        pltpu.make_async_copy(y.at[pl.ds(i * step, step)], o.at[pl.ds(i * step, step)], sout.at[i])
        for i in range(CHUNKS)
    ]
    for i in ins:
        i.start()
    tin.wait()
    c = code_of(t[...]).astype(F32)
    codes[...] = jnp.concatenate([c, c], axis=1)
    for i in range(CHUNKS):
        ins[i].wait()

        def one(d, carry):
            f[d] = x[d].astype(F32)
            y[d, pl.ds(0, 64), :] = f[d, pl.ds(own, 64, stride=2), :].astype(BF16)
            y[d, pl.ds(64, 8), :] = jnp.broadcast_to(codes[pl.ds(d, 1), :], (8, 128)).astype(BF16)
            return carry

        lax.fori_loop(i * step, (i + 1) * step, one, 0, unroll=8)
        outs[i].start()
    for i in outs:
        i.wait()


CHUNKS = 4


def pack(sc, slots, target):
    n = slots.shape[0]
    return pl.pallas_call(
        pack_kernel,
        in_specs=[sm(), hbm(), hbm()],
        out_specs=hbm(),
        out_shape=pltpu.HBM((n, 72, 128), BF16),
        scratch_shapes=[
            pltpu.VMEM((n, 128, 128), BF16),
            pltpu.VMEM((n, 72, 128), BF16),
            pltpu.VMEM((n, 64), jnp.int32),
            pltpu.VMEM((n, 128, 128), F32),
            pltpu.VMEM((n, 128), F32),
            pltpu.SemaphoreType.DMA((CHUNKS,)),
            pltpu.SemaphoreType.DMA((CHUNKS,)),
            pltpu.SemaphoreType.DMA,
        ],
        compiler_params=pltpu.CompilerParams(vmem_limit_bytes=16 * MIB),
    )(sc, far(slots), far(target))


def edge_kernel(sc, visc, mask, fric, to_a, to_b, v, m, d, s, sem):
    _, odd = place(sc)
    copies = []
    for side in range(2):
        at = pl.ds(side * (ROWS - 8), 8)
        copies.append(pltpu.make_async_copy(visc.at[:, at, :], v.at[side], sem.at[side * 3]))
        copies.append(pltpu.make_async_copy(mask.at[at, :], m.at[side], sem.at[side * 3 + 1]))
        copies.append(pltpu.make_async_copy(fric.at[at, :], d.at[side], sem.at[side * 3 + 2]))
    for c in copies:
        c.start()
    for c in copies:
        c.wait()
    for side in range(2):
        for i in range(4):
            s[side, pl.ds(3 * i, 3), :] = v[side, i, pl.ds(5 * side, 3), :]
        s[side, pl.ds(12, 2), :] = m[side, pl.ds(6 * side, 2), :].astype(F32)
        s[side, pl.ds(14, 2), :] = d[side, pl.ds(6 * side, 2), :]
    to_a[...] = s[1 - odd].astype(BF16)
    to_b[...] = s[odd].astype(BF16)


def edge_rows(sc, visc, mask, fric):
    return pl.pallas_call(
        edge_kernel,
        in_specs=[sm(), hbm(), hbm(), hbm()],
        out_specs=[vm()] * 2,
        out_shape=[kept(16, 1024, dtype=BF16)] * 2,
        scratch_shapes=[
            pltpu.VMEM((2, 4, 8, 1024), F32),
            pltpu.VMEM((2, 8, 1024), jnp.int32),
            pltpu.VMEM((2, 8, 1024), F32),
            pltpu.VMEM((2, 16, 1024), F32),
            pltpu.SemaphoreType.DMA((6,)),
        ],
        compiler_params=pltpu.CompilerParams(vmem_limit_bytes=8 * MIB),
    )(sc, far(visc), far(mask), far(fric))


def spread(dst, at, x):
    n = x.shape[0]
    for k in range(8):
        dst[pl.ds(at + k, n, stride=8), :] = x[:, k * 128 : (k + 1) * 128]


def weights(c):
    return jnp.where(c == 0, 4.0, 1.0), jnp.where(c == 0, 1.0, 4.0)


def coefficient_row(view, m, drag, r, pairs, fz, fr, fc, invs):
    lane, sub = lanes()
    last, first = lane == 127, lane == 0
    end = last & (sub == 7)
    start = first & (sub == 0)
    prev = None
    for l in range(8):
        c = view(l, 0)
        fe = 0.5 * (c + jnp.where(end, 0.0, east(c, last)))
        fw = 0.5 * (c + jnp.where(start, 0.0, west(c, first)))
        south = 0.5 * (c + view(l, 1))
        north = 0.5 * (c + view(l, -1))
        below = 4.0 * c if l == 0 else prev
        above = 4.0 * (c + view(l + 1, 0)) if l < 7 else 4.0 * c
        fz[r, at(l), :] = above
        fr[r, at(l), :] = south
        fc[r, at(l), :] = jnp.where(end, 0.0, fe)
        rows_, cols_, both = north + south, fe + fw, below + above
        if l == 0:
            both = both + drag
        for (rw, cw), inv, shift in zip(pairs, *invs):
            diag = both + rw * rows_ + cw * cols_
            inv[r + shift, at(l), :] = jnp.where(m, 0.7 / diag, 0.0)
        prev = above


GROUPS = ((3, 16), (16, 32), (32, 48), (48, 65))
INSIDE = pl.ds(3, 62)
RIM = (8, 32, 128)
N_FIELDS = 5


def coef_kernel(sc, visc, other, fric, mask, bvel, svel, *refs):
    outs, rest = refs[:11], refs[11:]
    fields, (wo, wx, svm, msk, rim, rimd, drg, v, bv, sem, sem2) = rest[:N_FIELDS], rest[N_FIELDS:]
    fz, fr, fc, inv_own, inv_oth = fields
    own, _ = place(sc)
    for i in range(4):
        for src, to in ((visc, own * 4 + i), (other, (1 - own) * 4 + i)):
            for h in range(0, ROWS, 16):
                spread(v.at[to], h * 8, src[i, h : h + 16, :].astype(F32))
    for h in range(0, ROWS, 16):
        spread(msk, h * 8, mask[h : h + 16, :].astype(F32))
        spread(drg, h * 8, fric[h : h + 16, :])
        spread(svm, h * 8, svel[own, h : h + 16, :])
        spread(bv.at[0], h * 8, bvel[own, h : h + 16, :])
        spread(bv.at[1], h * 8, bvel[1 - own, h : h + 16, :])
    for l in range(8):
        rim[l, pl.ds(0, 16), :] = v[l, pl.ds(0, 16), :]
        rim[l, pl.ds(16, 16), :] = v[l, pl.ds((ROWS - 2) * 8, 16), :]
    rimd[pl.ds(0, 8), :] = drg[row(0), :]
    rimd[pl.ds(8, 8), :] = drg[row(ROWS - 1), :]
    pairs = (weights(own), weights(1 - own))

    def strips(r):
        m, d = msk[row(r), :], drg[row(r), :]
        svm[row(r), :] = svm[row(r), :] * m
        for c, w in enumerate((wo, wx)):
            w[row(r), :] = (-m * d) * bv[c, row(r), :]
        return m, d

    def step(r, carry):
        m, d = strips(r)
        invs = ((inv_own, inv_oth), (0, 0))
        coefficient_row(lambda l, j: v[l, row(r + j), :], m > 0.5, d, r + 2, pairs, fz, fr, fc, invs)
        return carry

    strips(0)
    strips(ROWS - 1)
    copies = []
    for i, (src, dst) in enumerate(zip((msk, rim, rimd), outs[8:])):
        copies.append(pltpu.make_async_copy(src, dst, sem2.at[i]))
    for c in copies:
        c.start()
    for k, (a, b) in enumerate(GROUPS):
        lax.fori_loop(a - 2, b - 2, step, 0)
        part = pl.ds(a, b - a)
        for i, src in enumerate(fields):
            copies.append(pltpu.make_async_copy(src.at[part], outs[i].at[part], sem.at[k, i]))
            copies[-1].start()
    for i, (src, dst) in enumerate(zip((wo, wx, svm), outs[5:])):
        copies.append(pltpu.make_async_copy(src, dst, sem2.at[3 + i]))
        copies[-1].start()
    for c in copies:
        c.wait()


def coefficients(sc, visc, other, fric, mask, bvel, svel):
    shapes = (FIELD,) * N_FIELDS + (STRIP,) * 4 + (RIM, (16, 128))
    return pl.pallas_call(
        coef_kernel,
        in_specs=[sm()] + [vm()] * 6,
        out_specs=[hbm()] * 11,
        out_shape=[pltpu.HBM(x, F32) for x in shapes],
        scratch_shapes=[pltpu.VMEM(x, F32) for x in shapes]
        + [
            pltpu.VMEM(STRIP, F32),
            pltpu.VMEM((8, (ROWS + 1) * 8, 128), F32),
            pltpu.VMEM((2, *STRIP), F32),
            pltpu.SemaphoreType.DMA((len(GROUPS), N_FIELDS)),
            pltpu.SemaphoreType.DMA((6,)),
        ],
        compiler_params=pltpu.CompilerParams(vmem_limit_bytes=32 * MIB),
    )(sc, visc, other, fric, mask, bvel, svel)


def ghost_kernel(sc, ea, eb, ea2, eb2, msk, rim, rimd, fz0, fr0, fc0, inv0, fz, fr, fc, inv, gx, g, u):
    own, odd = place(sc)
    pairs = (weights(own), weights(1 - own))
    for kind, pair in enumerate(((ea, ea2), (eb, eb2))):
        side = jnp.where((odd + kind) % 2 == 1, 0, 1)
        for who, e in enumerate(pair):
            spread(g.at[side, who], 0, e[...].astype(F32))
    for side in range(2):
        to = 0 if side == 0 else 2
        for who in range(2):
            base = (own if who == 0 else 1 - own) * 4
            for i in range(4):
                u[side, base + i, pl.ds(to * 8, 24), :] = g[side, who, pl.ds(i * 24, 24), :]
        for l in range(8):
            u[side, l, pl.ds(24 * (1 - side), 16), :] = rim[l, pl.ds(16 * side, 16), :]
        for j in range(3):
            if side == 0:
                r, ghost, inside = j, j, 0
            else:
                r, ghost, inside = ROWS + 1 + j, j - 1, ROWS - 1
            if (side == 0 and j == 2) or (side == 1 and j == 0):
                m, d = msk[row(inside), :], rimd[pl.ds(8 * side, 8), :]
            else:
                m, d = g[side, 0, pl.ds((12 + ghost) * 8, 8), :], g[side, 0, pl.ds((14 + ghost) * 8, 8), :]
            invs = ((inv, gx), (0, 0 if side == 0 else 3 - (ROWS + 1)))
            coefficient_row(lambda l, s: u[side, l, row(j + 1 + s), :], m > 0.5, d, r, pairs, fz, fr, fc, invs)


def ghosts(sc, ea, eb, ea2, eb2, msk, rim, rimd, fz, fr, fc, inv):
    return pl.pallas_call(
        ghost_kernel,
        in_specs=[sm()] + [vm()] * 11,
        out_specs=[vm()] * 5,
        out_shape=[kept(*FIELD)] * 4 + [kept(6, 64, 128)],
        scratch_shapes=[pltpu.VMEM((2, 2, 128, 128), F32), pltpu.VMEM((2, 8, 40, 128), F32)],
        input_output_aliases={8: 0, 9: 1, 10: 2, 11: 3},
        compiler_params=pltpu.CompilerParams(vmem_limit_bytes=24 * MIB),
    )(sc, *(near(x) for x in (ea, eb, ea2, eb2, msk, rim, rimd, fz, fr, fc, inv)))


PARTS = 4


def misfit_kernel(sc, got_h, svm_h, *refs):
    n_kept = len(KEPT)
    here, (m_out, ea, eb), refs = refs[:n_kept], refs[n_kept : n_kept + 3], refs[n_kept + 3 :]
    kept_, (got, svm, hot, rhs, pc, acc, sem, sem2) = refs[:n_kept], refs[n_kept:]
    _, odd = place(sc)
    n = got.shape[0] // PARTS
    parts = [
        pltpu.make_async_copy(got_h.at[pl.ds(i * n, n)], got.at[pl.ds(i * n, n)], sem.at[i]) for i in range(PARTS)
    ]
    strips = pltpu.make_async_copy(svm_h, svm, sem.at[PARTS])
    rest = []
    for i, (x, y) in enumerate(zip(here, kept_)):
        if KEPT[i] == FIELD:
            x, y = x.at[INSIDE], y.at[INSIDE]
        rest.append(pltpu.make_async_copy(x, y, sem2.at[i]))
    for c in (*parts, strips, *rest):
        c.start()
    msk = kept_[0]
    p = lax.broadcasted_iota(jnp.int32, (512, 128), 0)
    pc[...] = code_of(p).astype(F32)
    rhs[:, pl.ds(128, 128)] = jnp.ones((rhs.shape[0], 128), BF16)
    lane = lax.broadcasted_iota(jnp.int32, (8, 128), 1)
    for part in range(PARTS):
        parts[part].wait()
        for b in range(n // 2):
            s = part * n + 2 * b
            for h in range(2):
                rhs[pl.ds((2 * b + h) * 64, 64), pl.ds(0, 128)] = got[s + h, pl.ds(0, 64), :]
            c = jnp.where(lane < 64, got[s, pl.ds(64, 8), :].astype(F32), got[s + 1, pl.ds(64, 8), :].astype(F32))
            same = pc[...].reshape(64, 8, 128) == c[None]
            hot[:, pl.ds(b * 128, 128)] = jnp.where(same, 1.0, 0.0).reshape(512, 128).astype(BF16)
        sums = jnp.dot(hot[...], rhs[...], preferred_element_type=F32)
        acc[...] = sums if part == 0 else acc[...] + sums
    strips.wait()
    rest[0].wait()
    m_out[...] = acc[:, 128:] * svm[...] - msk[...] * acc[:, :128]
    for kind, e in enumerate((ea, eb)):
        start = jnp.where((odd + kind) % 2 == 0, ROWS - 2, 0)
        for r in range(2):
            e[pl.ds(r * 8, 8), :] = m_out[row(start + r), :]
    for c in rest[1:]:
        c.wait()


KEPT = (STRIP, RIM, (16, 128), STRIP) + (FIELD,) * 4


def misfit(sc, got, svm, *rest):
    k = got.shape[0] // PARTS * 64
    return pl.pallas_call(
        misfit_kernel,
        in_specs=[sm()] + [hbm()] * (2 + len(KEPT)),
        out_specs=[vm()] * (3 + len(KEPT)),
        out_shape=[kept(*STRIP), kept(16, 128), kept(16, 128)] + [kept(*x) for x in KEPT],
        scratch_shapes=[
            pltpu.VMEM(got.shape, BF16),
            pltpu.VMEM(STRIP, F32),
            pltpu.VMEM((512, k), BF16),
            pltpu.VMEM((k, 256), BF16),
            pltpu.VMEM((512, 128), F32),
            pltpu.VMEM((512, 256), F32),
            pltpu.SemaphoreType.DMA((PARTS + 1,)),
            pltpu.SemaphoreType.DMA((len(KEPT),)),
        ],
        compiler_params=pltpu.CompilerParams(vmem_limit_bytes=24 * MIB),
    )(sc, *(far(x) for x in (got, svm, *rest)))


class Sweeps:
    def __init__(self, sc, t1, t2, c, coefs, state, turned):
        self.own, self.odd = place(sc)
        self.fz, self.fr, self.fc, self.inv, self.wgt = coefs
        self.a1, self.a2, self.a3, self.acc = state
        self.turned = turned
        self.thick = [jnp.where(self.own == l // 4, t1[l % 4], t2[l % 4]) for l in range(8)]
        self.rw, self.cw = weights(c)
        lane, _ = lanes()
        self.last, self.first_lane = lane == 127, lane == 0

    def turn(self, k, r, slot=0):
        a = (self.a1, self.a2)[k]
        for l in range(8):
            x, f = a[r, at(l), :], self.fc[r, at(l), :]
            self.turned[k, slot, l] = self.cw * (f * east(x, self.last) + west(f * x, self.first_lane))

    def neighbours(self, k, l, r, slot):
        a = (self.a1, self.a2)[k]
        n = None
        if l < 7:
            n = self.fz[r, at(l), :] * a[r, at(l + 1), :]
        if l > 0:
            t = self.fz[r, at(l - 1), :] * a[r, at(l - 1), :]
            n = t if n is None else n + t
        rows_ = self.fr[r, at(l), :] * a[r + 1, at(l), :] + self.fr[r - 1, at(l), :] * a[r - 1, at(l), :]
        return self.inv[r, at(l), :] * (n + self.rw * rows_ + self.turned[k, slot, l])

    def first(self, r, m):
        for l in range(8):
            self.a1[r, at(l), :] = self.inv[r, at(l), :] * (self.thick[l] * m)

    def second(self, r, slot=0):
        for l in range(8):
            self.a2[r, at(l), :] = 1.3 * self.a1[r, at(l), :] + self.neighbours(0, l, r, slot)

    def third(self, r, slot=0):
        total = None
        for l in range(8):
            y = 0.3 * self.a2[r, at(l), :] + (self.a1[r, at(l), :] + self.neighbours(1, l, r, slot))
            self.a3[pl.ds(pl.multiple_of((r - 2) * 64 + l * 8, 8), 8), :] = y
            total = self.thick[l] * y if l == 0 else total + self.thick[l] * y
        self.acc[row(r - 2), :] = self.wgt[row(r - 2), :] * total

    def interior(self, m):
        for r in (1, EXT - 2):
            self.a1[r] = jnp.zeros((64, 128), F32)

        def stage(p, static):
            for k, back in ((1, 4), (1, 3), (0, 2), (0, 1), (None, 0)):
                q = p - back
                if static and not (2 if k == 1 else 1) <= q <= (31 if k == 1 else 32):
                    continue
                for j in range(2):
                    r = 2 * q + j
                    if back == 4:
                        self.third(r, j)
                    elif back == 2:
                        self.second(r, j)
                    elif back:
                        self.turn(k, r, j)
                    else:
                        self.first(r, m[row(r - 2), :])

        def step(p, carry):
            stage(p, False)
            return carry

        for p in range(1, 6):
            stage(p, True)
        lax.fori_loop(6, 33, step, 0)
        for p in range(33, 36):
            stage(p, True)

    def edges(self, ga, gb):
        up = jnp.where(self.odd == 1, ga[...], gb[...])
        down = jnp.where(self.odd == 1, gb[...], ga[...])
        for ghost, firsts, seconds, thirds in (
            (up, (0, 1), (1, 2), (2, 3)),
            (down, (66, 67), (65, 66), (64, 65)),
        ):
            for i, r in enumerate(firsts):
                self.first(r, ghost[i * 8 : i * 8 + 8, :])
            for r in seconds:
                self.turn(0, r)
                self.second(r)
            for r in thirds:
                self.turn(1, r)
                self.third(r)


def gather_rows(dst, src, first, stride):
    for h in range(0, ROWS, 8):
        for k in range(8):
            dst[pl.ds(h, 8), pl.ds(k * 128, 128)] = src[pl.ds(h * stride + first + k, 8, stride=stride), :]


TURNED = (2, 2, 8, 8, 128)
STATE = (FIELD, FIELD, (ROWS * 64, 128), STRIP)
N_STATE = len(STATE)
STAGE = (4, ROWS, 1024)


def own_kernel(sc, t1, t2, invx_h, wgtx_h, gx, m, *refs):
    coefs, state, (invx, wgtx, turned, sem) = refs[:5], refs[5:9], refs[9:]
    own, _ = place(sc)
    copies = (
        pltpu.make_async_copy(invx_h.at[INSIDE], invx.at[INSIDE], sem.at[0]),
        pltpu.make_async_copy(wgtx_h, wgtx, sem.at[1]),
    )
    for c in copies:
        c.start()
    Sweeps(sc, t1, t2, own, coefs, state, turned).interior(m)
    for c in copies:
        c.wait()
    invx[pl.ds(0, 3)] = gx[pl.ds(0, 3)]
    invx[pl.ds(ROWS + 1, 3)] = gx[pl.ds(3, 3)]


def own_sweeps(sc, t1, t2, invx, wgtx, gx, m, coefs):
    return pl.pallas_call(
        own_kernel,
        in_specs=[sm()] * 3 + [hbm()] * 2 + [vm()] * 7,
        out_specs=[vm()] * 6,
        out_shape=[kept(*s) for s in (*STATE, FIELD, STRIP)],
        scratch_shapes=[pltpu.VMEM(TURNED, F32), pltpu.SemaphoreType.DMA((2,))],
        compiler_params=pltpu.CompilerParams(vmem_limit_bytes=24 * MIB),
    )(sc, t1, t2, far(invx), far(wgtx), *(near(x) for x in (gx, m, *coefs)))


def both_kernel(sc, t1, t2, ga, gb, m, *refs):
    (fz, fr, fc, inv, wgt, invx, wgtx), refs = refs[:7], refs[7 + N_STATE :]
    done, todo, adj, (stage, turned, sem) = refs[:4], refs[4:8], refs[8], refs[9:]
    own, _ = place(sc)
    Sweeps(sc, t1, t2, own, (fz, fr, fc, inv, wgt), done, turned).edges(ga, gb)
    for i in range(4):
        gather_rows(stage.at[i], done[2], (own * 4 + i) * 8, 64)
    copy = pltpu.make_async_copy(stage, adj.at[own], sem)
    copy.start()
    Sweeps(sc, t1, t2, 1 - own, (fz, fr, fc, invx, wgtx), todo, turned).interior(m)
    copy.wait()


def both_sweeps(sc, t1, t2, ga, gb, m, coefs, others, state):
    return pl.pallas_call(
        both_kernel,
        in_specs=[sm()] * 3 + [vm()] * (3 + 7 + N_STATE),
        out_specs=[vm()] * (2 * N_STATE) + [hbm()],
        out_shape=[kept(*s) for s in STATE] * 2 + [pltpu.HBM((2, *STAGE), F32)],
        scratch_shapes=[pltpu.VMEM(STAGE, F32), pltpu.VMEM(TURNED, F32), pltpu.SemaphoreType.DMA],
        input_output_aliases={13 + i: i for i in range(N_STATE)},
        compiler_params=pltpu.CompilerParams(vmem_limit_bytes=24 * MIB),
    )(sc, t1, t2, *(near(x) for x in (ga, gb, m, *coefs, *others, *state)))


def last_kernel(sc, t1, t2, g, racc, fz, fr, fc, inv, wgt, *refs):
    state, (adj, grad), (stage, turned, sem) = refs[5:9], refs[9:11], refs[11:]
    _, _, a3, acc = state
    own, _ = place(sc)
    Sweeps(sc, t1, t2, 1 - own, (fz, fr, fc, inv, wgt), state, turned).edges(
        g.at[pl.ds(0, 16), :], g.at[pl.ds(16, 16), :]
    )
    for i in range(4):
        gather_rows(stage.at[i], a3, (own * 4 + i) * 8, 64)
    copy = pltpu.make_async_copy(stage, adj.at[1 - own], sem)
    copy.start()
    acc[...] = acc[...] + racc[...]
    gather_rows(grad, acc, 0, 8)
    copy.wait()


def last_sweeps(sc, t1, t2, g, racc, coefs, state, adj):
    return pl.pallas_call(
        last_kernel,
        in_specs=[sm()] * 3 + [vm()] * 11 + [hbm()],
        out_specs=[vm()] * 4 + [hbm(), vm()],
        out_shape=[kept(*s) for s in STATE]
        + [pltpu.HBM((2, *STAGE), F32), jax.ShapeDtypeStruct((ROWS, 1024), F32)],
        scratch_shapes=[pltpu.VMEM(STAGE, F32), pltpu.VMEM(TURNED, F32), pltpu.SemaphoreType.DMA],
        input_output_aliases={10: 0, 11: 1, 12: 2, 13: 3, 14: 4},
        compiler_params=pltpu.CompilerParams(vmem_limit_bytes=24 * MIB),
    )(sc, t1, t2, *(near(x) for x in (g, racc, *coefs, *state)), far(adj))[4:]


def swaps(tiles, offset, across):
    perm = []
    for t in range(offset, tiles - 1, 2):
        for layer in range(2):
            a, b = t * 2 + layer, (t + 1) * 2 + (1 - layer if across else layer)
            perm += [(a, b), (b, a)]
    return perm


def swap_layers(x):
    return lax.ppermute(x, "layer", [(0, 1), (1, 0)])


def body(viscosity, friction, base_vel, surf_vel, layer_thick, ice_mask, obs_slots, obs_target):
    tiles = lax.axis_size("tile")
    own = lax.axis_index("layer")
    odd = lax.axis_index("tile") % 2
    sc = (own + 2 * odd).astype(jnp.int32).reshape(1)

    def swap(x, kind, across=False):
        return lax.ppermute(x, PAIR, swaps(tiles, kind, across))

    other = swap_layers(viscosity.astype(BF16))
    payload = pack(sc, obs_slots.reshape(tiles, 128, 128), obs_target)
    got = lax.all_to_all(payload, "tile", split_axis=0, concat_axis=0, tiled=True)
    thick_other = swap_layers(layer_thick)

    to_a, to_b = edge_rows(sc, viscosity, ice_mask, friction)
    near_rows = (swap(to_a, 0), swap(to_b, 1), swap(to_a, 0, True), swap(to_b, 1, True))
    fz, fr, fc, inv, invx, wgt, wgtx, svm, msk, rim, rimd = coefficients(
        sc, viscosity, other, friction, ice_mask, base_vel, surf_vel
    )
    got, near_rows, thick_other = lax.optimization_barrier((got, near_rows, thick_other))
    m_own, ea, eb, msk, rim, rimd, wgt, fz, fr, fc, inv = misfit(
        sc, got, svm, msk, rim, rimd, wgt, fz, fr, fc, inv
    )
    fz, fr, fc, inv, gx = ghosts(sc, *near_rows, msk, rim, rimd, fz, fr, fc, inv)
    th = (sc, layer_thick, thick_other)

    ga, gb = swap(ea, 0), swap(eb, 1)
    m_oth = swap_layers(m_own)
    *state, invx, wgtx = own_sweeps(*th, invx, wgtx, gx, m_own, (fz, fr, fc, inv, wgt))
    g_oth = swap_layers(jnp.concatenate([ga, gb]))
    *both, adj = both_sweeps(*th, ga, gb, m_oth, (fz, fr, fc, inv, wgt), (invx, wgtx), state)
    adjoint, gradient = last_sweeps(*th, g_oth, both[3], (fz, fr, fc, invx, wgtx), both[4:], adj)
    return adjoint, gradient


def solution(mesh):
    in_specs = (
        P("layer", "tile", None),
        P("tile", None),
        P(None, "tile", None),
        P(None, "tile", None),
        P("layer"),
        P("tile", None),
        P("tile", None, None, None),
        P("tile", None),
    )
    out_specs = (P(None, "layer", "tile", None), P("tile", None))

    return jax.shard_map(body, mesh=mesh, in_specs=in_specs, out_specs=out_specs, check_vma=False)
```

```python
import jax
import jax.numpy as jnp
from jax import lax
from jax.experimental import pallas as pl
from jax.experimental.pallas import tpu as pltpu
from jax.sharding import PartitionSpec as P


F32 = jnp.float32
BF16 = jnp.bfloat16
ROWS = 64
EXT = 68
FIELD = (EXT, 64, 128)
STRIP = (ROWS * 8, 128)
MIB = 1 << 20


def vm():
    return pl.BlockSpec(memory_space=pltpu.VMEM)


def sm():
    return pl.BlockSpec(memory_space=pltpu.SMEM)


def hbm():
    return pl.BlockSpec(memory_space=pltpu.HBM)


def far(x):
    return pltpu.with_memory_space_constraint(x, pltpu.HBM)


def kept(*shape, dtype=F32):
    return pltpu.VMEM(shape, dtype)


def near(x):
    return pltpu.with_memory_space_constraint(x, pltpu.VMEM)


def row(r):
    return pl.ds(pl.multiple_of(r * 8, 8), 8)


def at(l):
    return pl.ds(l * 8, 8)


def place(sc):
    return sc[0] & 1, sc[0] >> 1


def lanes():
    lane = lax.broadcasted_iota(jnp.int32, (8, 128), 1)
    sub = lax.broadcasted_iota(jnp.int32, (8, 128), 0)
    return lane, sub


def east(x, last):
    r = pltpu.roll(x, 127, 1)
    return jnp.where(last, pltpu.roll(r, 7, 0), r)


def west(x, first):
    r = pltpu.roll(x, 1, 1)
    return jnp.where(first, pltpu.roll(r, 1, 0), r)


def code_of(t):
    return jnp.where(t < 512, (128 + (t & 127)) << (t >> 7), 0)


def pack_kernel(sc, slots, target, visc, o, narrow, x, y, t, f, codes, vx, vy, sin, sout, st, vin, vout):
    own, _ = place(sc)
    layers = visc.shape[0]
    takes = [pltpu.make_async_copy(visc.at[i], vx.at[i], vin.at[i]) for i in range(layers)]
    gives = [pltpu.make_async_copy(vy.at[i], narrow.at[i], vout.at[i]) for i in range(layers)]
    n = slots.shape[0]
    step = n // CHUNKS
    tin = pltpu.make_async_copy(target, t, st)
    tin.start()
    ins = [
        pltpu.make_async_copy(slots.at[pl.ds(i * step, step)], x.at[pl.ds(i * step, step)], sin.at[i])
        for i in range(CHUNKS)
    ]
    outs = [
        pltpu.make_async_copy(y.at[pl.ds(i * step, step)], o.at[pl.ds(i * step, step)], sout.at[i])
        for i in range(CHUNKS)
    ]
    for i in (*takes, *ins):
        i.start()
    for i in range(layers):
        takes[i].wait()
        vy[i] = vx[i].astype(BF16)
        gives[i].start()
    tin.wait()
    c = code_of(t[...]).astype(F32)
    codes[...] = jnp.concatenate([c, c], axis=1)
    for i in range(CHUNKS):
        ins[i].wait()

        def one(d, carry):
            f[d] = x[d].astype(F32)
            y[d, pl.ds(0, 64), :] = f[d, pl.ds(own, 64, stride=2), :].astype(BF16)
            y[d, pl.ds(64, 8), :] = jnp.broadcast_to(codes[pl.ds(d, 1), :], (8, 128)).astype(BF16)
            return carry

        lax.fori_loop(i * step, (i + 1) * step, one, 0, unroll=8)
        outs[i].start()
    for i in (*gives, *outs):
        i.wait()


CHUNKS = 8


def pack(sc, slots, target, visc):
    n = slots.shape[0]
    return pl.pallas_call(
        pack_kernel,
        in_specs=[sm(), hbm(), hbm(), hbm()],
        out_specs=[hbm(), hbm()],
        out_shape=[pltpu.HBM((n, 72, 128), BF16), pltpu.HBM(visc.shape, BF16)],
        scratch_shapes=[
            pltpu.VMEM((n, 128, 128), BF16),
            pltpu.VMEM((n, 72, 128), BF16),
            pltpu.VMEM((n, 64), jnp.int32),
            pltpu.VMEM((n, 128, 128), F32),
            pltpu.VMEM((n, 128), F32),
            pltpu.VMEM(visc.shape, F32),
            pltpu.VMEM(visc.shape, BF16),
            pltpu.SemaphoreType.DMA((CHUNKS,)),
            pltpu.SemaphoreType.DMA((CHUNKS,)),
            pltpu.SemaphoreType.DMA,
            pltpu.SemaphoreType.DMA((visc.shape[0],)),
            pltpu.SemaphoreType.DMA((visc.shape[0],)),
        ],
        compiler_params=pltpu.CompilerParams(vmem_limit_bytes=16 * MIB),
    )(sc, far(slots), far(target), far(visc))


def edge_kernel(sc, visc, mask, fric, to_a, to_b, v, m, d, s, sem):
    _, odd = place(sc)
    copies = []
    for side in range(2):
        at = pl.ds(side * (ROWS - 8), 8)
        copies.append(pltpu.make_async_copy(visc.at[:, at, :], v.at[side], sem.at[side * 3]))
        copies.append(pltpu.make_async_copy(mask.at[at, :], m.at[side], sem.at[side * 3 + 1]))
        copies.append(pltpu.make_async_copy(fric.at[at, :], d.at[side], sem.at[side * 3 + 2]))
    for c in copies:
        c.start()
    for c in copies:
        c.wait()
    for side in range(2):
        for i in range(4):
            s[side, pl.ds(3 * i, 3), :] = v[side, i, pl.ds(5 * side, 3), :]
        s[side, pl.ds(12, 2), :] = m[side, pl.ds(6 * side, 2), :].astype(F32)
        s[side, pl.ds(14, 2), :] = d[side, pl.ds(6 * side, 2), :]
    to_a[...] = s[1 - odd].astype(BF16)
    to_b[...] = s[odd].astype(BF16)


def edge_rows(sc, visc, mask, fric):
    return pl.pallas_call(
        edge_kernel,
        in_specs=[sm(), hbm(), hbm(), hbm()],
        out_specs=[vm()] * 2,
        out_shape=[kept(16, 1024, dtype=BF16)] * 2,
        scratch_shapes=[
            pltpu.VMEM((2, 4, 8, 1024), F32),
            pltpu.VMEM((2, 8, 1024), jnp.int32),
            pltpu.VMEM((2, 8, 1024), F32),
            pltpu.VMEM((2, 16, 1024), F32),
            pltpu.SemaphoreType.DMA((6,)),
        ],
        compiler_params=pltpu.CompilerParams(vmem_limit_bytes=8 * MIB),
    )(sc, far(visc), far(mask), far(fric))


def spread(dst, at, x):
    n = x.shape[0]
    for k in range(8):
        dst[pl.ds(at + k, n, stride=8), :] = x[:, k * 128 : (k + 1) * 128]


def weights(c):
    return jnp.where(c == 0, 4.0, 1.0), jnp.where(c == 0, 1.0, 4.0)


def coefficient_row(view, m, drag, r, pairs, fz, fr, fc, invs):
    lane, sub = lanes()
    last, first = lane == 127, lane == 0
    end = last & (sub == 7)
    start = first & (sub == 0)
    prev = None
    for l in range(8):
        c = view(l, 0)
        fe = 0.5 * (c + jnp.where(end, 0.0, east(c, last)))
        fw = 0.5 * (c + jnp.where(start, 0.0, west(c, first)))
        south = 0.5 * (c + view(l, 1))
        north = 0.5 * (c + view(l, -1))
        below = 4.0 * c if l == 0 else prev
        above = 4.0 * (c + view(l + 1, 0)) if l < 7 else 4.0 * c
        fz[r, at(l), :] = above
        fr[r, at(l), :] = south
        fc[r, at(l), :] = jnp.where(end, 0.0, fe)
        rows_, cols_, both = north + south, fe + fw, below + above
        if l == 0:
            both = both + drag
        for (rw, cw), inv, shift in zip(pairs, *invs):
            diag = both + rw * rows_ + cw * cols_
            inv[r + shift, at(l), :] = jnp.where(m, 0.7 / diag, 0.0)
        prev = above


GROUPS = ((3, 16), (16, 32), (32, 48), (48, 60), (60, 65))
INSIDE = pl.ds(3, 62)
RIM = (8, 32, 128)
N_FIELDS = 5


def coef_kernel(sc, visc, other, fric, mask, bvel, svel, *refs):
    outs, rest = refs[:11], refs[11:]
    fields, (wo, wx, svm, msk, rim, rimd, drg, v, bv, sem, sem2) = rest[:N_FIELDS], rest[N_FIELDS:]
    fz, fr, fc, inv_own, inv_oth = fields
    own, _ = place(sc)
    for i in range(4):
        for src, to in ((visc, own * 4 + i), (other, (1 - own) * 4 + i)):
            for h in range(0, ROWS, 16):
                spread(v.at[to], h * 8, src[i, h : h + 16, :].astype(F32))
    for h in range(0, ROWS, 16):
        spread(msk, h * 8, mask[h : h + 16, :].astype(F32))
        spread(drg, h * 8, fric[h : h + 16, :])
        spread(svm, h * 8, svel[own, h : h + 16, :])
        spread(bv.at[0], h * 8, bvel[own, h : h + 16, :])
        spread(bv.at[1], h * 8, bvel[1 - own, h : h + 16, :])
    for l in range(8):
        rim[l, pl.ds(0, 16), :] = v[l, pl.ds(0, 16), :]
        rim[l, pl.ds(16, 16), :] = v[l, pl.ds((ROWS - 2) * 8, 16), :]
    rimd[pl.ds(0, 8), :] = drg[row(0), :]
    rimd[pl.ds(8, 8), :] = drg[row(ROWS - 1), :]
    pairs = (weights(own), weights(1 - own))

    def strips(r):
        m, d = msk[row(r), :], drg[row(r), :]
        svm[row(r), :] = svm[row(r), :] * m
        for c, w in enumerate((wo, wx)):
            w[row(r), :] = (-m * d) * bv[c, row(r), :]
        return m, d

    def step(r, carry):
        m, d = strips(r)
        invs = ((inv_own, inv_oth), (0, 0))
        coefficient_row(lambda l, j: v[l, row(r + j), :], m > 0.5, d, r + 2, pairs, fz, fr, fc, invs)
        return carry

    strips(0)
    strips(ROWS - 1)
    copies = []
    for i, (src, dst) in enumerate(zip((msk, rim, rimd), outs[8:])):
        copies.append(pltpu.make_async_copy(src, dst, sem2.at[i]))
    for c in copies:
        c.start()
    for k, (a, b) in enumerate(GROUPS):
        lax.fori_loop(a - 2, b - 2, step, 0)
        part = pl.ds(a, b - a)
        for i, src in enumerate(fields):
            copies.append(pltpu.make_async_copy(src.at[part], outs[i].at[part], sem.at[k, i]))
            copies[-1].start()
    for i, (src, dst) in enumerate(zip((wo, wx, svm), outs[5:])):
        copies.append(pltpu.make_async_copy(src, dst, sem2.at[3 + i]))
        copies[-1].start()
    for c in copies:
        c.wait()


def coefficients(sc, visc, other, fric, mask, bvel, svel):
    shapes = (FIELD,) * N_FIELDS + (STRIP,) * 4 + (RIM, (16, 128))
    return pl.pallas_call(
        coef_kernel,
        in_specs=[sm()] + [vm()] * 6,
        out_specs=[hbm()] * 11,
        out_shape=[pltpu.HBM(x, F32) for x in shapes],
        scratch_shapes=[pltpu.VMEM(x, F32) for x in shapes]
        + [
            pltpu.VMEM(STRIP, F32),
            pltpu.VMEM((8, (ROWS + 1) * 8, 128), F32),
            pltpu.VMEM((2, *STRIP), F32),
            pltpu.SemaphoreType.DMA((len(GROUPS), N_FIELDS)),
            pltpu.SemaphoreType.DMA((6,)),
        ],
        compiler_params=pltpu.CompilerParams(vmem_limit_bytes=32 * MIB),
    )(sc, visc, other, fric, mask, bvel, svel)


def ghost_kernel(sc, ea, eb, relayed, msk, rim, rimd, fz0, fr0, fc0, inv0, fz, fr, fc, inv, gx, g, u):
    own, odd = place(sc)
    pairs = (weights(own), weights(1 - own))
    for kind, pair in enumerate(((ea, relayed.at[pl.ds(0, 16)]), (eb, relayed.at[pl.ds(16, 16)]))):
        side = jnp.where((odd + kind) % 2 == 1, 0, 1)
        for who, e in enumerate(pair):
            spread(g.at[side, who], 0, e[...].astype(F32))
    for side in range(2):
        to = 0 if side == 0 else 2
        for who in range(2):
            base = (own if who == 0 else 1 - own) * 4
            for i in range(4):
                u[side, base + i, pl.ds(to * 8, 24), :] = g[side, who, pl.ds(i * 24, 24), :]
        for l in range(8):
            u[side, l, pl.ds(24 * (1 - side), 16), :] = rim[l, pl.ds(16 * side, 16), :]
        for j in range(3):
            if side == 0:
                r, ghost, inside = j, j, 0
            else:
                r, ghost, inside = ROWS + 1 + j, j - 1, ROWS - 1
            if (side == 0 and j == 2) or (side == 1 and j == 0):
                m, d = msk[row(inside), :], rimd[pl.ds(8 * side, 8), :]
            else:
                m, d = g[side, 0, pl.ds((12 + ghost) * 8, 8), :], g[side, 0, pl.ds((14 + ghost) * 8, 8), :]
            invs = ((inv, gx), (0, 0 if side == 0 else 3 - (ROWS + 1)))
            coefficient_row(lambda l, s: u[side, l, row(j + 1 + s), :], m > 0.5, d, r, pairs, fz, fr, fc, invs)


def ghosts(sc, ea, eb, relayed, msk, rim, rimd, fz, fr, fc, inv):
    return pl.pallas_call(
        ghost_kernel,
        in_specs=[sm()] + [vm()] * 10,
        out_specs=[vm()] * 5,
        out_shape=[kept(*FIELD)] * 4 + [kept(6, 64, 128)],
        scratch_shapes=[pltpu.VMEM((2, 2, 128, 128), F32), pltpu.VMEM((2, 8, 40, 128), F32)],
        input_output_aliases={7: 0, 8: 1, 9: 2, 10: 3},
        compiler_params=pltpu.CompilerParams(vmem_limit_bytes=24 * MIB),
    )(sc, *(near(x) for x in (ea, eb, relayed, msk, rim, rimd, fz, fr, fc, inv)))


PARTS = 4


def misfit_kernel(sc, got_h, svm_h, *refs):
    n_kept = len(KEPT)
    here, (m_out, ea, eb), refs = refs[:n_kept], refs[n_kept : n_kept + 3], refs[n_kept + 3 :]
    kept_, (got, svm, hot, rhs, pc, sem, sem2) = refs[:n_kept], refs[n_kept:]
    _, odd = place(sc)
    n = got.shape[0] // PARTS
    parts = [
        pltpu.make_async_copy(got_h.at[pl.ds(i * n, n)], got.at[pl.ds(i * n, n)], sem.at[i]) for i in range(PARTS)
    ]
    strips = pltpu.make_async_copy(svm_h, svm, sem.at[PARTS])
    rest = []
    for i, (x, y) in enumerate(zip(here, kept_)):
        if KEPT[i] == FIELD:
            x, y = x.at[INSIDE], y.at[INSIDE]
        rest.append(pltpu.make_async_copy(x, y, sem2.at[i]))
    for c in (*parts, strips, *rest):
        c.start()
    msk = kept_[0]
    p = lax.broadcasted_iota(jnp.int32, (512, 128), 0)
    pc[...] = code_of(p).astype(F32)
    rhs[:, pl.ds(128, 128)] = jnp.ones((rhs.shape[0], 128), BF16)
    lane = lax.broadcasted_iota(jnp.int32, (8, 128), 1)
    for part in parts:
        part.wait()
    for part in range(PARTS):
        for b in range(n // 2):
            s = part * n + 2 * b
            for h in range(2):
                rhs[pl.ds((s + h) * 64, 64), pl.ds(0, 128)] = got[s + h, pl.ds(0, 64), :]
            c = jnp.where(lane < 64, got[s, pl.ds(64, 8), :].astype(F32), got[s + 1, pl.ds(64, 8), :].astype(F32))
            same = pc[...].reshape(64, 8, 128) == c[None]
            hot[:, pl.ds(s * 64, 128)] = jnp.where(same, 1.0, 0.0).reshape(512, 128).astype(BF16)
    sums = jnp.dot(hot[...], rhs[...], preferred_element_type=F32)
    strips.wait()
    rest[0].wait()
    m_out[...] = sums[:, 128:] * svm[...] - msk[...] * sums[:, :128]
    for kind, e in enumerate((ea, eb)):
        start = jnp.where((odd + kind) % 2 == 0, ROWS - 2, 0)
        for r in range(2):
            e[pl.ds(r * 8, 8), :] = m_out[row(start + r), :]
    for c in rest[1:]:
        c.wait()


KEPT = (STRIP, RIM, (16, 128), STRIP) + (FIELD,) * 4


def misfit(sc, got, svm, *rest):
    k = got.shape[0] * 64
    return pl.pallas_call(
        misfit_kernel,
        in_specs=[sm()] + [hbm()] * (2 + len(KEPT)),
        out_specs=[vm()] * (3 + len(KEPT)),
        out_shape=[kept(*STRIP), kept(16, 128), kept(16, 128)] + [kept(*x) for x in KEPT],
        scratch_shapes=[
            pltpu.VMEM(got.shape, BF16),
            pltpu.VMEM(STRIP, F32),
            pltpu.VMEM((512, k), BF16),
            pltpu.VMEM((k, 256), BF16),
            pltpu.VMEM((512, 128), F32),
            pltpu.SemaphoreType.DMA((PARTS + 1,)),
            pltpu.SemaphoreType.DMA((len(KEPT),)),
        ],
        compiler_params=pltpu.CompilerParams(vmem_limit_bytes=24 * MIB),
    )(sc, *(far(x) for x in (got, svm, *rest)))


class Sweeps:
    def __init__(self, sc, t1, t2, c, coefs, state, turned):
        self.own, self.odd = place(sc)
        self.fz, self.fr, self.fc, self.inv, self.wgt = coefs
        self.a1, self.a2, self.a3, self.acc = state
        self.turned = turned
        self.thick = [jnp.where(self.own == l // 4, t1[l % 4], t2[l % 4]) for l in range(8)]
        self.rw, self.cw = weights(c)
        lane, _ = lanes()
        self.last, self.first_lane = lane == 127, lane == 0

    def turn(self, k, r, slot=0):
        a = (self.a1, self.a2)[k]
        for l in range(8):
            x, f = a[r, at(l), :], self.fc[r, at(l), :]
            self.turned[k, slot, l] = self.cw * (f * east(x, self.last) + west(f * x, self.first_lane))

    def neighbours(self, k, l, r, slot):
        a = (self.a1, self.a2)[k]
        n = None
        if l < 7:
            n = self.fz[r, at(l), :] * a[r, at(l + 1), :]
        if l > 0:
            t = self.fz[r, at(l - 1), :] * a[r, at(l - 1), :]
            n = t if n is None else n + t
        rows_ = self.fr[r, at(l), :] * a[r + 1, at(l), :] + self.fr[r - 1, at(l), :] * a[r - 1, at(l), :]
        return self.inv[r, at(l), :] * (n + self.rw * rows_ + self.turned[k, slot, l])

    def first(self, r, m):
        for l in range(8):
            self.a1[r, at(l), :] = self.inv[r, at(l), :] * (self.thick[l] * m)

    def second(self, r, slot=0):
        for l in range(8):
            self.a2[r, at(l), :] = 1.3 * self.a1[r, at(l), :] + self.neighbours(0, l, r, slot)

    def third(self, r, slot=0):
        total = None
        for l in range(8):
            y = 0.3 * self.a2[r, at(l), :] + (self.a1[r, at(l), :] + self.neighbours(1, l, r, slot))
            self.a3[l, row(r - 2), :] = y
            total = self.thick[l] * y if l == 0 else total + self.thick[l] * y
        self.acc[row(r - 2), :] = self.wgt[row(r - 2), :] * total

    def interior(self, m):
        for r in (1, EXT - 2):
            self.a1[r] = jnp.zeros((64, 128), F32)

        def stage(p, static):
            for k, back in ((1, 4), (1, 3), (0, 2), (0, 1), (None, 0)):
                q = p - back
                if static and not (2 if k == 1 else 1) <= q <= (31 if k == 1 else 32):
                    continue
                for j in range(2):
                    r = 2 * q + j
                    if back == 4:
                        self.third(r, j)
                    elif back == 2:
                        self.second(r, j)
                    elif back:
                        self.turn(k, r, j)
                    else:
                        self.first(r, m[row(r - 2), :])

        def step(p, carry):
            stage(p, False)
            return carry

        for p in range(1, 6):
            stage(p, True)
        lax.fori_loop(6, 33, step, 0)
        for p in range(33, 36):
            stage(p, True)

    def edges(self, ga, gb):
        up = jnp.where(self.odd == 1, ga[...], gb[...])
        down = jnp.where(self.odd == 1, gb[...], ga[...])
        for ghost, firsts, seconds, thirds in (
            (up, (0, 1), (1, 2), (2, 3)),
            (down, (66, 67), (65, 66), (64, 65)),
        ):
            for i, r in enumerate(firsts):
                self.first(r, ghost[i * 8 : i * 8 + 8, :])
            for r in seconds:
                self.turn(0, r)
                self.second(r)
            for r in thirds:
                self.turn(1, r)
                self.third(r)


INNER, OUTER = range(8, ROWS - 8, 8), (0, ROWS - 8)


def gather_rows(dst, src, rows=range(0, ROWS, 8)):
    for h in rows:
        for k in range(8):
            dst[pl.ds(h, 8), pl.ds(k * 128, 128)] = src[pl.ds(h * 8 + k, 8, stride=8), :]


TURNED = (2, 2, 8, 8, 128)
STATE = (FIELD, FIELD, (8, (ROWS + 1) * 8, 128), STRIP)
N_STATE = len(STATE)
STAGE = (4, ROWS, 1024)


def own_kernel(sc, t1, t2, invx_h, wgtx_h, gx, m, *refs):
    coefs, state, (invx, wgtx, turned, sem) = refs[:5], refs[5:9], refs[9:]
    own, _ = place(sc)
    copies = (
        pltpu.make_async_copy(invx_h.at[INSIDE], invx.at[INSIDE], sem.at[0]),
        pltpu.make_async_copy(wgtx_h, wgtx, sem.at[1]),
    )
    for c in copies:
        c.start()
    Sweeps(sc, t1, t2, own, coefs, state, turned).interior(m)
    for c in copies:
        c.wait()
    invx[pl.ds(0, 3)] = gx[pl.ds(0, 3)]
    invx[pl.ds(ROWS + 1, 3)] = gx[pl.ds(3, 3)]


def own_sweeps(sc, t1, t2, invx, wgtx, gx, m, coefs):
    return pl.pallas_call(
        own_kernel,
        in_specs=[sm()] * 3 + [hbm()] * 2 + [vm()] * 7,
        out_specs=[vm()] * 6,
        out_shape=[kept(*s) for s in (*STATE, FIELD, STRIP)],
        scratch_shapes=[pltpu.VMEM(TURNED, F32), pltpu.SemaphoreType.DMA((2,))],
        compiler_params=pltpu.CompilerParams(vmem_limit_bytes=24 * MIB),
    )(sc, t1, t2, far(invx), far(wgtx), *(near(x) for x in (gx, m, *coefs)))


def both_kernel(sc, t1, t2, ga, gb, m, *refs):
    (fz, fr, fc, inv, wgt, invx, wgtx), refs = refs[:7], refs[7 + N_STATE :]
    done, todo, adj, (stage, turned, sem) = refs[:4], refs[4:8], refs[8], refs[9:]
    own, _ = place(sc)
    Sweeps(sc, t1, t2, own, (fz, fr, fc, inv, wgt), done, turned).edges(ga, gb)
    for i in range(4):
        gather_rows(stage.at[i], done[2].at[own * 4 + i])
    copy = pltpu.make_async_copy(stage, adj.at[own], sem)
    copy.start()
    Sweeps(sc, t1, t2, 1 - own, (fz, fr, fc, invx, wgtx), todo, turned).interior(m)
    copy.wait()


def both_sweeps(sc, t1, t2, ga, gb, m, coefs, others, state):
    return pl.pallas_call(
        both_kernel,
        in_specs=[sm()] * 3 + [vm()] * (3 + 7 + N_STATE),
        out_specs=[vm()] * (2 * N_STATE) + [hbm()],
        out_shape=[kept(*s) for s in STATE] * 2 + [pltpu.HBM((2, *STAGE), F32)],
        scratch_shapes=[pltpu.VMEM(STAGE, F32), pltpu.VMEM(TURNED, F32), pltpu.SemaphoreType.DMA],
        input_output_aliases={13 + i: i for i in range(N_STATE)},
        compiler_params=pltpu.CompilerParams(vmem_limit_bytes=24 * MIB),
    )(sc, t1, t2, *(near(x) for x in (ga, gb, m, *coefs, *others, *state)))


def last_kernel(sc, t1, t2, g, racc, fz, fr, fc, inv, wgt, *refs):
    state, (adj, grad), (stage, sum_, turned, sem) = refs[5:9], refs[9:11], refs[11:]
    _, _, a3, acc = state
    own, _ = place(sc)
    to = adj.at[1 - own]
    spans = (pl.ds(8, ROWS - 16), pl.ds(0, 8), pl.ds(ROWS - 8, 8))
    copies = [pltpu.make_async_copy(stage.at[:, x, :], to.at[:, x, :], sem.at[i]) for i, x in enumerate(spans)]
    copies += [pltpu.make_async_copy(sum_.at[x, :], grad.at[x, :], sem.at[3 + i]) for i, x in enumerate(spans)]
    for i in range(4):
        gather_rows(stage.at[i], a3.at[own * 4 + i], INNER)
    copies[0].start()
    for r in INNER:
        acc[pl.ds(r * 8, 64), :] = acc[pl.ds(r * 8, 64), :] + racc[pl.ds(r * 8, 64), :]
    gather_rows(sum_, acc, INNER)
    copies[3].start()
    Sweeps(sc, t1, t2, 1 - own, (fz, fr, fc, inv, wgt), state, turned).edges(
        g.at[pl.ds(0, 16), :], g.at[pl.ds(16, 16), :]
    )
    for i in range(4):
        gather_rows(stage.at[i], a3.at[own * 4 + i], OUTER)
    copies[1].start()
    copies[2].start()
    for r in OUTER:
        acc[pl.ds(r * 8, 64), :] = acc[pl.ds(r * 8, 64), :] + racc[pl.ds(r * 8, 64), :]
    gather_rows(sum_, acc, OUTER)
    copies[4].start()
    copies[5].start()
    for c in copies:
        c.wait()


def last_sweeps(sc, t1, t2, g, racc, coefs, state, adj):
    return pl.pallas_call(
        last_kernel,
        in_specs=[sm()] * 3 + [vm()] * 11 + [hbm()],
        out_specs=[vm()] * 4 + [hbm(), hbm()],
        out_shape=[kept(*s) for s in STATE]
        + [pltpu.HBM((2, *STAGE), F32), pltpu.HBM((ROWS, 1024), F32)],
        scratch_shapes=[
            pltpu.VMEM(STAGE, F32),
            pltpu.VMEM((ROWS, 1024), F32),
            pltpu.VMEM(TURNED, F32),
            pltpu.SemaphoreType.DMA((6,)),
        ],
        input_output_aliases={10: 0, 11: 1, 12: 2, 13: 3, 14: 4},
        compiler_params=pltpu.CompilerParams(vmem_limit_bytes=24 * MIB),
    )(sc, t1, t2, *(near(x) for x in (g, racc, *coefs, *state)), far(adj))[4:]


def swaps(tiles, offset):
    perm = []
    for t in range(offset, tiles - 1, 2):
        perm += [(t, t + 1), (t + 1, t)]
    return perm


def swap_layers(x):
    return lax.ppermute(x, "layer", [(0, 1), (1, 0)])


def body(viscosity, friction, base_vel, surf_vel, layer_thick, ice_mask, obs_slots, obs_target):
    tiles = lax.axis_size("tile")
    own = lax.axis_index("layer")
    odd = lax.axis_index("tile") % 2
    sc = (own + 2 * odd).astype(jnp.int32).reshape(1)

    def swap(x, kind):
        return lax.ppermute(x, "tile", swaps(tiles, kind))

    payload, narrow = pack(sc, obs_slots.reshape(tiles, 128, 128), obs_target, viscosity)
    other = swap_layers(narrow)
    got = lax.all_to_all(payload, "tile", split_axis=0, concat_axis=0, tiled=True)
    thick_other = swap_layers(layer_thick)

    to_a, to_b = edge_rows(sc, viscosity, ice_mask, friction)
    near_rows = (swap(to_a, 0), swap(to_b, 1))
    relayed = swap_layers(jnp.concatenate(near_rows))
    fz, fr, fc, inv, invx, wgt, wgtx, svm, msk, rim, rimd = coefficients(
        sc, viscosity, other, friction, ice_mask, base_vel, surf_vel
    )
    got, near_rows, thick_other = lax.optimization_barrier((got, near_rows, thick_other))
    m_own, ea, eb, msk, rim, rimd, wgt, fz, fr, fc, inv = misfit(
        sc, got, svm, msk, rim, rimd, wgt, fz, fr, fc, inv
    )
    fz, fr, fc, inv, gx = ghosts(sc, *near_rows, relayed, msk, rim, rimd, fz, fr, fc, inv)
    th = (sc, layer_thick, thick_other)

    ga, gb = swap(ea, 0), swap(eb, 1)
    m_oth = swap_layers(m_own)
    *state, invx, wgtx = own_sweeps(*th, invx, wgtx, gx, m_own, (fz, fr, fc, inv, wgt))
    g_oth = swap_layers(jnp.concatenate([ga, gb]))
    *both, adj = both_sweeps(*th, ga, gb, m_oth, (fz, fr, fc, inv, wgt), (invx, wgtx), state)
    adjoint, gradient = last_sweeps(*th, g_oth, both[3], (fz, fr, fc, invx, wgtx), both[4:], adj)
    return adjoint, gradient


def solution(mesh):
    in_specs = (
        P("layer", "tile", None),
        P("tile", None),
        P(None, "tile", None),
        P(None, "tile", None),
        P("layer"),
        P("tile", None),
        P("tile", None, None, None),
        P("tile", None),
    )
    out_specs = (P(None, "layer", "tile", None), P("tile", None))

    return jax.shard_map(body, mesh=mesh, in_specs=in_specs, out_specs=out_specs, check_vma=False)
```

```python
import jax
import jax.numpy as jnp
from jax import lax
from jax.experimental import pallas as pl
from jax.experimental.pallas import tpu as pltpu
from jax.sharding import PartitionSpec as P


F32 = jnp.float32
BF16 = jnp.bfloat16
ROWS = 64
EXT = 68
FIELD = (EXT, 64, 128)
STRIP = (ROWS * 8, 128)
MIB = 1 << 20


def vm():
    return pl.BlockSpec(memory_space=pltpu.VMEM)


def sm():
    return pl.BlockSpec(memory_space=pltpu.SMEM)


def hbm():
    return pl.BlockSpec(memory_space=pltpu.HBM)


def far(x):
    return pltpu.with_memory_space_constraint(x, pltpu.HBM)


def kept(*shape, dtype=F32):
    return pltpu.VMEM(shape, dtype)


def near(x):
    return pltpu.with_memory_space_constraint(x, pltpu.VMEM)


def row(r):
    return pl.ds(pl.multiple_of(r * 8, 8), 8)


def at(l):
    return pl.ds(l * 8, 8)


def place(sc):
    return sc[0] & 1, sc[0] >> 1


def lanes():
    lane = lax.broadcasted_iota(jnp.int32, (8, 128), 1)
    sub = lax.broadcasted_iota(jnp.int32, (8, 128), 0)
    return lane, sub


def east(x, last):
    r = pltpu.roll(x, 127, 1)
    return jnp.where(last, pltpu.roll(r, 7, 0), r)


def west(x, first):
    r = pltpu.roll(x, 1, 1)
    return jnp.where(first, pltpu.roll(r, 1, 0), r)


def code_of(t):
    return jnp.where(t < 512, (128 + (t & 127)) << (t >> 7), 0)


def narrow_kernel(visc, narrow, vx, vy, vin, vout):
    layers = visc.shape[0]
    takes = [pltpu.make_async_copy(visc.at[i], vx.at[i], vin.at[i]) for i in range(layers)]
    gives = [pltpu.make_async_copy(vy.at[i], narrow.at[i], vout.at[i]) for i in range(layers)]
    for i in takes:
        i.start()
    for i in range(layers):
        takes[i].wait()
        vy[i] = vx[i].astype(BF16)
        gives[i].start()
    for i in gives:
        i.wait()


def narrowed(visc):
    return pl.pallas_call(
        narrow_kernel,
        in_specs=[hbm()],
        out_specs=hbm(),
        out_shape=pltpu.HBM(visc.shape, BF16),
        scratch_shapes=[
            pltpu.VMEM(visc.shape, F32),
            pltpu.VMEM(visc.shape, BF16),
            pltpu.SemaphoreType.DMA((visc.shape[0],)),
            pltpu.SemaphoreType.DMA((visc.shape[0],)),
        ],
        compiler_params=pltpu.CompilerParams(vmem_limit_bytes=8 * MIB),
    )(far(visc))


def pack_kernel(sc, slots, target, o, x, y, t, f, codes, sin, sout, st):
    own, _ = place(sc)
    n = slots.shape[0]
    step = n // CHUNKS
    tin = pltpu.make_async_copy(target, t, st)
    tin.start()
    ins = [
        pltpu.make_async_copy(slots.at[pl.ds(i * step, step)], x.at[pl.ds(i * step, step)], sin.at[i])
        for i in range(CHUNKS)
    ]
    outs = [
        pltpu.make_async_copy(y.at[pl.ds(i * step, step)], o.at[pl.ds(i * step, step)], sout.at[i])
        for i in range(CHUNKS)
    ]
    for i in ins:
        i.start()
    tin.wait()
    c = code_of(t[...]).astype(F32)
    codes[...] = jnp.concatenate([c, c], axis=1)
    for i in range(CHUNKS):
        ins[i].wait()

        def one(d, carry):
            f[d] = x[d].astype(F32)
            y[d, pl.ds(0, 64), :] = f[d, pl.ds(own, 64, stride=2), :].astype(BF16)
            y[d, pl.ds(64, 8), :] = jnp.broadcast_to(codes[pl.ds(d, 1), :], (8, 128)).astype(BF16)
            return carry

        lax.fori_loop(i * step, (i + 1) * step, one, 0, unroll=8)
        outs[i].start()
    for i in outs:
        i.wait()


CHUNKS = 8


def pack(sc, slots, target):
    n = slots.shape[0]
    return pl.pallas_call(
        pack_kernel,
        in_specs=[sm(), hbm(), hbm()],
        out_specs=hbm(),
        out_shape=pltpu.HBM((n, 72, 128), BF16),
        scratch_shapes=[
            pltpu.VMEM((n, 128, 128), BF16),
            pltpu.VMEM((n, 72, 128), BF16),
            pltpu.VMEM((n, 64), jnp.int32),
            pltpu.VMEM((n, 128, 128), F32),
            pltpu.VMEM((n, 128), F32),
            pltpu.SemaphoreType.DMA((CHUNKS,)),
            pltpu.SemaphoreType.DMA((CHUNKS,)),
            pltpu.SemaphoreType.DMA,
        ],
        compiler_params=pltpu.CompilerParams(vmem_limit_bytes=16 * MIB),
    )(sc, far(slots), far(target))


def edge_kernel(sc, visc, mask, fric, to_a, to_b, v, m, d, s, sem):
    _, odd = place(sc)
    copies = []
    for side in range(2):
        at = pl.ds(side * (ROWS - 8), 8)
        copies.append(pltpu.make_async_copy(visc.at[:, at, :], v.at[side], sem.at[side * 3]))
        copies.append(pltpu.make_async_copy(mask.at[at, :], m.at[side], sem.at[side * 3 + 1]))
        copies.append(pltpu.make_async_copy(fric.at[at, :], d.at[side], sem.at[side * 3 + 2]))
    for c in copies:
        c.start()
    for c in copies:
        c.wait()
    for side in range(2):
        for i in range(4):
            s[side, pl.ds(3 * i, 3), :] = v[side, i, pl.ds(5 * side, 3), :]
        s[side, pl.ds(12, 2), :] = m[side, pl.ds(6 * side, 2), :].astype(F32)
        s[side, pl.ds(14, 2), :] = d[side, pl.ds(6 * side, 2), :]
    to_a[...] = s[1 - odd].astype(BF16)
    to_b[...] = s[odd].astype(BF16)


def edge_rows(sc, visc, mask, fric):
    return pl.pallas_call(
        edge_kernel,
        in_specs=[sm(), hbm(), hbm(), hbm()],
        out_specs=[vm()] * 2,
        out_shape=[kept(16, 1024, dtype=BF16)] * 2,
        scratch_shapes=[
            pltpu.VMEM((2, 4, 8, 1024), F32),
            pltpu.VMEM((2, 8, 1024), jnp.int32),
            pltpu.VMEM((2, 8, 1024), F32),
            pltpu.VMEM((2, 16, 1024), F32),
            pltpu.SemaphoreType.DMA((6,)),
        ],
        compiler_params=pltpu.CompilerParams(vmem_limit_bytes=8 * MIB),
    )(sc, far(visc), far(mask), far(fric))


def spread(dst, at, x):
    n = x.shape[0]
    for k in range(8):
        dst[pl.ds(at + k, n, stride=8), :] = x[:, k * 128 : (k + 1) * 128]


def weights(c):
    return jnp.where(c == 0, 4.0, 1.0), jnp.where(c == 0, 1.0, 4.0)


def coefficient_row(view, m, drag, r, pairs, fz, fr, fc, invs):
    lane, sub = lanes()
    last, first = lane == 127, lane == 0
    end = last & (sub == 7)
    start = first & (sub == 0)
    prev = None
    for l in range(8):
        c = view(l, 0)
        fe = 0.5 * (c + jnp.where(end, 0.0, east(c, last)))
        fw = 0.5 * (c + jnp.where(start, 0.0, west(c, first)))
        south = 0.5 * (c + view(l, 1))
        north = 0.5 * (c + view(l, -1))
        below = 4.0 * c if l == 0 else prev
        above = 4.0 * (c + view(l + 1, 0)) if l < 7 else 4.0 * c
        fz[r, at(l), :] = above
        fr[r, at(l), :] = south
        fc[r, at(l), :] = jnp.where(end, 0.0, fe)
        rows_, cols_, both = north + south, fe + fw, below + above
        if l == 0:
            both = both + drag
        for (rw, cw), inv, shift in zip(pairs, *invs):
            diag = both + rw * rows_ + cw * cols_
            inv[r + shift, at(l), :] = jnp.where(m, 0.7 / diag, 0.0)
        prev = above


GROUPS = ((3, 16), (16, 32), (32, 48), (48, 60), (60, 65))
INSIDE = pl.ds(3, 62)
EARLY = pl.ds(3, 13)
LATER = ((16, 16), (32, 16), (48, 17))
RIM = (8, 32, 128)
N_FIELDS = 5


def coef_kernel(sc, visc, other, fric, mask, bvel, svel, *refs):
    outs, rest = refs[:11], refs[11:]
    fields, (wo, wx, svm, msk, rim, rimd, drg, v, bv, sem, sem2) = rest[:N_FIELDS], rest[N_FIELDS:]
    fz, fr, fc, inv_own, inv_oth = fields
    own, _ = place(sc)
    for i in range(4):
        for src, to in ((visc, own * 4 + i), (other, (1 - own) * 4 + i)):
            for h in range(0, ROWS, 16):
                spread(v.at[to], h * 8, src[i, h : h + 16, :].astype(F32))
    for h in range(0, ROWS, 16):
        spread(msk, h * 8, mask[h : h + 16, :].astype(F32))
        spread(drg, h * 8, fric[h : h + 16, :])
        spread(svm, h * 8, svel[own, h : h + 16, :])
        spread(bv.at[0], h * 8, bvel[own, h : h + 16, :])
        spread(bv.at[1], h * 8, bvel[1 - own, h : h + 16, :])
    for l in range(8):
        rim[l, pl.ds(0, 16), :] = v[l, pl.ds(0, 16), :]
        rim[l, pl.ds(16, 16), :] = v[l, pl.ds((ROWS - 2) * 8, 16), :]
    rimd[pl.ds(0, 8), :] = drg[row(0), :]
    rimd[pl.ds(8, 8), :] = drg[row(ROWS - 1), :]
    pairs = (weights(own), weights(1 - own))

    def strips(r):
        m, d = msk[row(r), :], drg[row(r), :]
        svm[row(r), :] = svm[row(r), :] * m
        for c, w in enumerate((wo, wx)):
            w[row(r), :] = (-m * d) * bv[c, row(r), :]
        return m, d

    def step(r, carry):
        m, d = strips(r)
        invs = ((inv_own, inv_oth), (0, 0))
        coefficient_row(lambda l, j: v[l, row(r + j), :], m > 0.5, d, r + 2, pairs, fz, fr, fc, invs)
        return carry

    strips(0)
    strips(ROWS - 1)
    copies = []
    for i, (src, dst) in enumerate(zip((msk, rim, rimd), outs[8:])):
        copies.append(pltpu.make_async_copy(src, dst, sem2.at[i]))
    for c in copies:
        c.start()
    for k, (a, b) in enumerate(GROUPS):
        lax.fori_loop(a - 2, b - 2, step, 0)
        part = pl.ds(a, b - a)
        for i, src in enumerate(fields):
            copies.append(pltpu.make_async_copy(src.at[part], outs[i].at[part], sem.at[k, i]))
            copies[-1].start()
    for i, (src, dst) in enumerate(zip((wo, wx, svm), outs[5:])):
        copies.append(pltpu.make_async_copy(src, dst, sem2.at[3 + i]))
        copies[-1].start()
    for c in copies:
        c.wait()


def coefficients(sc, visc, other, fric, mask, bvel, svel):
    shapes = (FIELD,) * N_FIELDS + (STRIP,) * 4 + (RIM, (16, 128))
    return pl.pallas_call(
        coef_kernel,
        in_specs=[sm()] + [vm()] * 6,
        out_specs=[hbm()] * 11,
        out_shape=[pltpu.HBM(x, F32) for x in shapes],
        scratch_shapes=[pltpu.VMEM(x, F32) for x in shapes]
        + [
            pltpu.VMEM(STRIP, F32),
            pltpu.VMEM((8, (ROWS + 1) * 8, 128), F32),
            pltpu.VMEM((2, *STRIP), F32),
            pltpu.SemaphoreType.DMA((len(GROUPS), N_FIELDS)),
            pltpu.SemaphoreType.DMA((6,)),
        ],
        compiler_params=pltpu.CompilerParams(vmem_limit_bytes=32 * MIB),
    )(sc, visc, other, fric, mask, bvel, svel)


def ghost_kernel(sc, ea, eb, relayed, msk, rim, rimd, fz0, fr0, fc0, inv0, fz, fr, fc, inv, gx, g, u):
    own, odd = place(sc)
    pairs = (weights(own), weights(1 - own))
    for kind, pair in enumerate(((ea, relayed.at[pl.ds(0, 16)]), (eb, relayed.at[pl.ds(16, 16)]))):
        side = jnp.where((odd + kind) % 2 == 1, 0, 1)
        for who, e in enumerate(pair):
            spread(g.at[side, who], 0, e[...].astype(F32))
    for side in range(2):
        to = 0 if side == 0 else 2
        for who in range(2):
            base = (own if who == 0 else 1 - own) * 4
            for i in range(4):
                u[side, base + i, pl.ds(to * 8, 24), :] = g[side, who, pl.ds(i * 24, 24), :]
        for l in range(8):
            u[side, l, pl.ds(24 * (1 - side), 16), :] = rim[l, pl.ds(16 * side, 16), :]
        for j in range(3):
            if side == 0:
                r, ghost, inside = j, j, 0
            else:
                r, ghost, inside = ROWS + 1 + j, j - 1, ROWS - 1
            if (side == 0 and j == 2) or (side == 1 and j == 0):
                m, d = msk[row(inside), :], rimd[pl.ds(8 * side, 8), :]
            else:
                m, d = g[side, 0, pl.ds((12 + ghost) * 8, 8), :], g[side, 0, pl.ds((14 + ghost) * 8, 8), :]
            invs = ((inv, gx), (0, 0 if side == 0 else 3 - (ROWS + 1)))
            coefficient_row(lambda l, s: u[side, l, row(j + 1 + s), :], m > 0.5, d, r, pairs, fz, fr, fc, invs)


def ghosts(sc, ea, eb, relayed, msk, rim, rimd, fz, fr, fc, inv):
    return pl.pallas_call(
        ghost_kernel,
        in_specs=[sm()] + [vm()] * 10,
        out_specs=[vm()] * 5,
        out_shape=[kept(*FIELD)] * 4 + [kept(6, 64, 128)],
        scratch_shapes=[pltpu.VMEM((2, 2, 128, 128), F32), pltpu.VMEM((2, 8, 40, 128), F32)],
        input_output_aliases={7: 0, 8: 1, 9: 2, 10: 3},
        compiler_params=pltpu.CompilerParams(vmem_limit_bytes=24 * MIB),
    )(sc, *(near(x) for x in (ea, eb, relayed, msk, rim, rimd, fz, fr, fc, inv)))


PARTS = 4


def misfit_kernel(sc, got_h, svm_h, *refs):
    n_kept = len(KEPT)
    here, (m_out, ea, eb), refs = refs[:n_kept], refs[n_kept : n_kept + 3], refs[n_kept + 3 :]
    kept_, (got, svm, hot, rhs, pc, sem, sem2) = refs[:n_kept], refs[n_kept:]
    _, odd = place(sc)
    n = got.shape[0] // PARTS
    parts = [
        pltpu.make_async_copy(got_h.at[pl.ds(i * n, n)], got.at[pl.ds(i * n, n)], sem.at[i]) for i in range(PARTS)
    ]
    strips = pltpu.make_async_copy(svm_h, svm, sem.at[PARTS])
    rest = []
    for i, (x, y) in enumerate(zip(here, kept_)):
        if KEPT[i] == FIELD:
            x, y = x.at[EARLY], y.at[EARLY]
        rest.append(pltpu.make_async_copy(x, y, sem2.at[i]))
    for c in (*parts, strips, *rest):
        c.start()
    msk = kept_[0]
    p = lax.broadcasted_iota(jnp.int32, (512, 128), 0)
    pc[...] = code_of(p).astype(F32)
    rhs[:, pl.ds(128, 128)] = jnp.ones((rhs.shape[0], 128), BF16)
    lane = lax.broadcasted_iota(jnp.int32, (8, 128), 1)
    for part in parts:
        part.wait()
    for part in range(PARTS):
        for b in range(n // 2):
            s = part * n + 2 * b
            for h in range(2):
                rhs[pl.ds((s + h) * 64, 64), pl.ds(0, 128)] = got[s + h, pl.ds(0, 64), :]
            c = jnp.where(lane < 64, got[s, pl.ds(64, 8), :].astype(F32), got[s + 1, pl.ds(64, 8), :].astype(F32))
            same = pc[...].reshape(64, 8, 128) == c[None]
            hot[:, pl.ds(s * 64, 128)] = jnp.where(same, 1.0, 0.0).reshape(512, 128).astype(BF16)
    sums = jnp.dot(hot[...], rhs[...], preferred_element_type=F32)
    strips.wait()
    rest[0].wait()
    m_out[...] = sums[:, 128:] * svm[...] - msk[...] * sums[:, :128]
    for kind, e in enumerate((ea, eb)):
        start = jnp.where((odd + kind) % 2 == 0, ROWS - 2, 0)
        for r in range(2):
            e[pl.ds(r * 8, 8), :] = m_out[row(start + r), :]
    for c in rest[1:]:
        c.wait()


KEPT = (STRIP, RIM, (16, 128), STRIP) + (FIELD,) * 4


def misfit(sc, got, svm, *rest):
    k = got.shape[0] * 64
    return pl.pallas_call(
        misfit_kernel,
        in_specs=[sm()] + [hbm()] * (2 + len(KEPT)),
        out_specs=[vm()] * (3 + len(KEPT)),
        out_shape=[kept(*STRIP), kept(16, 128), kept(16, 128)] + [kept(*x) for x in KEPT],
        scratch_shapes=[
            pltpu.VMEM(got.shape, BF16),
            pltpu.VMEM(STRIP, F32),
            pltpu.VMEM((512, k), BF16),
            pltpu.VMEM((k, 256), BF16),
            pltpu.VMEM((512, 128), F32),
            pltpu.SemaphoreType.DMA((PARTS + 1,)),
            pltpu.SemaphoreType.DMA((len(KEPT),)),
        ],
        compiler_params=pltpu.CompilerParams(vmem_limit_bytes=24 * MIB),
    )(sc, *(far(x) for x in (got, svm, *rest)))


class Sweeps:
    def __init__(self, sc, t1, t2, c, coefs, state, turned):
        self.own, self.odd = place(sc)
        self.fz, self.fr, self.fc, self.inv, self.wgt = coefs
        self.a1, self.a2, self.a3, self.acc = state
        self.turned = turned
        self.thick = [jnp.where(self.own == l // 4, t1[l % 4], t2[l % 4]) for l in range(8)]
        self.rw, self.cw = weights(c)
        lane, _ = lanes()
        self.last, self.first_lane = lane == 127, lane == 0

    def turn(self, k, r, slot=0):
        a = (self.a1, self.a2)[k]
        for l in range(8):
            x, f = a[r, at(l), :], self.fc[r, at(l), :]
            self.turned[k, slot, l] = self.cw * (f * east(x, self.last) + west(f * x, self.first_lane))

    def neighbours(self, k, l, r, slot):
        a = (self.a1, self.a2)[k]
        n = None
        if l < 7:
            n = self.fz[r, at(l), :] * a[r, at(l + 1), :]
        if l > 0:
            t = self.fz[r, at(l - 1), :] * a[r, at(l - 1), :]
            n = t if n is None else n + t
        rows_ = self.fr[r, at(l), :] * a[r + 1, at(l), :] + self.fr[r - 1, at(l), :] * a[r - 1, at(l), :]
        return self.inv[r, at(l), :] * (n + self.rw * rows_ + self.turned[k, slot, l])

    def first(self, r, m):
        for l in range(8):
            self.a1[r, at(l), :] = self.inv[r, at(l), :] * (self.thick[l] * m)

    def second(self, r, slot=0):
        for l in range(8):
            self.a2[r, at(l), :] = 1.3 * self.a1[r, at(l), :] + self.neighbours(0, l, r, slot)

    def third(self, r, slot=0):
        total = None
        for l in range(8):
            y = 0.3 * self.a2[r, at(l), :] + (self.a1[r, at(l), :] + self.neighbours(1, l, r, slot))
            self.a3[l, row(r - 2), :] = y
            total = self.thick[l] * y if l == 0 else total + self.thick[l] * y
        self.acc[row(r - 2), :] = self.wgt[row(r - 2), :] * total

    def interior(self, m, ready=()):
        for r in (1, EXT - 2):
            self.a1[r] = jnp.zeros((64, 128), F32)

        def stage(p, static):
            for k, back in ((1, 4), (1, 3), (0, 2), (0, 1), (None, 0)):
                q = p - back
                if static and not (2 if k == 1 else 1) <= q <= (31 if k == 1 else 32):
                    continue
                for j in range(2):
                    r = 2 * q + j
                    if back == 4:
                        self.third(r, j)
                    elif back == 2:
                        self.second(r, j)
                    elif back:
                        self.turn(k, r, j)
                    else:
                        self.first(r, m[row(r - 2), :])

        def step(p, carry):
            stage(p, False)
            return carry

        for p in range(1, 6):
            stage(p, True)
        at_ = 6
        for upto, wait in ready:
            lax.fori_loop(at_, upto, step, 0)
            wait()
            at_ = upto
        lax.fori_loop(at_, 33, step, 0)
        for p in range(33, 36):
            stage(p, True)

    def edges(self, ga, gb):
        up = jnp.where(self.odd == 1, ga[...], gb[...])
        down = jnp.where(self.odd == 1, gb[...], ga[...])
        for ghost, firsts, seconds, thirds in (
            (up, (0, 1), (1, 2), (2, 3)),
            (down, (66, 67), (65, 66), (64, 65)),
        ):
            for i, r in enumerate(firsts):
                self.first(r, ghost[i * 8 : i * 8 + 8, :])
            for r in seconds:
                self.turn(0, r)
                self.second(r)
            for r in thirds:
                self.turn(1, r)
                self.third(r)


INNER, OUTER = range(8, ROWS - 8, 8), (0, ROWS - 8)


def gather_rows(dst, src, rows=range(0, ROWS, 8)):
    for h in rows:
        for k in range(8):
            dst[pl.ds(h, 8), pl.ds(k * 128, 128)] = src[pl.ds(h * 8 + k, 8, stride=8), :]


TURNED = (2, 2, 8, 8, 128)
STATE = (FIELD, FIELD, (8, (ROWS + 1) * 8, 128), STRIP)
N_STATE = len(STATE)
STAGE = (4, ROWS, 1024)


def own_kernel(sc, t1, t2, fz_h, fr_h, fc_h, inv_h, invx_h, wgtx_h, gx, m, wgt, *refs):
    fields, state, (invx, wgtx, turned, sem, sem2) = refs[4:8], refs[8:12], refs[12:]
    own, _ = place(sc)
    groups = []
    for i, (first, rows) in enumerate(LATER):
        part = pl.ds(first, rows)
        pairs = zip((fz_h, fr_h, fc_h, inv_h), fields)
        groups.append([pltpu.make_async_copy(x.at[part], y.at[part], sem.at[i, j]) for j, (x, y) in enumerate(pairs)])
    copies = (
        pltpu.make_async_copy(invx_h.at[INSIDE], invx.at[INSIDE], sem2.at[0]),
        pltpu.make_async_copy(wgtx_h, wgtx, sem2.at[1]),
    )
    for c in (*groups[0], *groups[1], *groups[2], *copies):
        c.start()

    def waiting(group):
        def wait():
            for c in group:
                c.wait()

        return wait

    ready = [(first // 2, waiting(group)) for (first, _), group in zip(LATER, groups)]
    Sweeps(sc, t1, t2, own, (*fields, wgt), state, turned).interior(m, ready)
    for c in copies:
        c.wait()
    invx[pl.ds(0, 3)] = gx[pl.ds(0, 3)]
    invx[pl.ds(ROWS + 1, 3)] = gx[pl.ds(3, 3)]


def own_sweeps(sc, t1, t2, stored, invx, wgtx, gx, m, wgt, fields):
    return pl.pallas_call(
        own_kernel,
        in_specs=[sm()] * 3 + [hbm()] * 6 + [vm()] * 7,
        out_specs=[vm()] * 10,
        out_shape=[kept(*s) for s in (*(FIELD,) * 4, *STATE, FIELD, STRIP)],
        scratch_shapes=[
            pltpu.VMEM(TURNED, F32),
            pltpu.SemaphoreType.DMA((len(LATER), 4)),
            pltpu.SemaphoreType.DMA((2,)),
        ],
        input_output_aliases={12 + i: i for i in range(4)},
        compiler_params=pltpu.CompilerParams(vmem_limit_bytes=24 * MIB),
    )(sc, t1, t2, *(far(x) for x in (*stored, invx, wgtx)), *(near(x) for x in (gx, m, wgt, *fields)))


def both_kernel(sc, t1, t2, ga, gb, m, *refs):
    (fz, fr, fc, inv, wgt, invx, wgtx), refs = refs[:7], refs[7 + N_STATE :]
    done, todo, adj, (stage, turned, sem) = refs[:4], refs[4:8], refs[8], refs[9:]
    own, _ = place(sc)
    Sweeps(sc, t1, t2, own, (fz, fr, fc, inv, wgt), done, turned).edges(ga, gb)
    for i in range(4):
        gather_rows(stage.at[i], done[2].at[own * 4 + i])
    copy = pltpu.make_async_copy(stage, adj.at[own], sem)
    copy.start()
    Sweeps(sc, t1, t2, 1 - own, (fz, fr, fc, invx, wgtx), todo, turned).interior(m)
    copy.wait()


def both_sweeps(sc, t1, t2, ga, gb, m, coefs, others, state):
    return pl.pallas_call(
        both_kernel,
        in_specs=[sm()] * 3 + [vm()] * (3 + 7 + N_STATE),
        out_specs=[vm()] * (2 * N_STATE) + [hbm()],
        out_shape=[kept(*s) for s in STATE] * 2 + [pltpu.HBM((2, *STAGE), F32)],
        scratch_shapes=[pltpu.VMEM(STAGE, F32), pltpu.VMEM(TURNED, F32), pltpu.SemaphoreType.DMA],
        input_output_aliases={13 + i: i for i in range(N_STATE)},
        compiler_params=pltpu.CompilerParams(vmem_limit_bytes=24 * MIB),
    )(sc, t1, t2, *(near(x) for x in (ga, gb, m, *coefs, *others, *state)))


def last_kernel(sc, t1, t2, g, racc, fz, fr, fc, inv, wgt, *refs):
    state, (adj, grad), (stage, sum_, turned, sem) = refs[5:9], refs[9:11], refs[11:]
    _, _, a3, acc = state
    own, _ = place(sc)
    to = adj.at[1 - own]
    spans = (pl.ds(8, ROWS - 16), pl.ds(0, 8), pl.ds(ROWS - 8, 8))
    copies = [pltpu.make_async_copy(stage.at[:, x, :], to.at[:, x, :], sem.at[i]) for i, x in enumerate(spans)]
    copies += [pltpu.make_async_copy(sum_.at[x, :], grad.at[x, :], sem.at[3 + i]) for i, x in enumerate(spans)]
    for i in range(4):
        gather_rows(stage.at[i], a3.at[own * 4 + i], INNER)
    copies[0].start()
    for r in INNER:
        acc[pl.ds(r * 8, 64), :] = acc[pl.ds(r * 8, 64), :] + racc[pl.ds(r * 8, 64), :]
    gather_rows(sum_, acc, INNER)
    copies[3].start()
    Sweeps(sc, t1, t2, 1 - own, (fz, fr, fc, inv, wgt), state, turned).edges(
        g.at[pl.ds(0, 16), :], g.at[pl.ds(16, 16), :]
    )
    for i in range(4):
        gather_rows(stage.at[i], a3.at[own * 4 + i], OUTER)
    copies[1].start()
    copies[2].start()
    for r in OUTER:
        acc[pl.ds(r * 8, 64), :] = acc[pl.ds(r * 8, 64), :] + racc[pl.ds(r * 8, 64), :]
    gather_rows(sum_, acc, OUTER)
    copies[4].start()
    copies[5].start()
    for c in copies:
        c.wait()


def last_sweeps(sc, t1, t2, g, racc, coefs, state, adj):
    return pl.pallas_call(
        last_kernel,
        in_specs=[sm()] * 3 + [vm()] * 11 + [hbm()],
        out_specs=[vm()] * 4 + [hbm(), hbm()],
        out_shape=[kept(*s) for s in STATE]
        + [pltpu.HBM((2, *STAGE), F32), pltpu.HBM((ROWS, 1024), F32)],
        scratch_shapes=[
            pltpu.VMEM(STAGE, F32),
            pltpu.VMEM((ROWS, 1024), F32),
            pltpu.VMEM(TURNED, F32),
            pltpu.SemaphoreType.DMA((6,)),
        ],
        input_output_aliases={10: 0, 11: 1, 12: 2, 13: 3, 14: 4},
        compiler_params=pltpu.CompilerParams(vmem_limit_bytes=24 * MIB),
    )(sc, t1, t2, *(near(x) for x in (g, racc, *coefs, *state)), far(adj))[4:]


def swaps(tiles, offset):
    perm = []
    for t in range(offset, tiles - 1, 2):
        perm += [(t, t + 1), (t + 1, t)]
    return perm


def swap_layers(x):
    return lax.ppermute(x, "layer", [(0, 1), (1, 0)])


def body(viscosity, friction, base_vel, surf_vel, layer_thick, ice_mask, obs_slots, obs_target):
    tiles = lax.axis_size("tile")
    own = lax.axis_index("layer")
    odd = lax.axis_index("tile") % 2
    sc = (own + 2 * odd).astype(jnp.int32).reshape(1)

    def swap(x, kind):
        return lax.ppermute(x, "tile", swaps(tiles, kind))

    other = swap_layers(narrowed(viscosity))
    payload = pack(sc, obs_slots.reshape(tiles, 128, 128), obs_target)
    got = lax.all_to_all(payload, "tile", split_axis=0, concat_axis=0, tiled=True)
    thick_other = swap_layers(layer_thick)

    to_a, to_b = edge_rows(sc, viscosity, ice_mask, friction)
    near_rows = (swap(to_a, 0), swap(to_b, 1))
    relayed = swap_layers(jnp.concatenate(near_rows))
    fz, fr, fc, inv, invx, wgt, wgtx, svm, msk, rim, rimd = coefficients(
        sc, viscosity, other, friction, ice_mask, base_vel, surf_vel
    )
    stored = (fz, fr, fc, inv)
    got, near_rows, thick_other = lax.optimization_barrier((got, near_rows, thick_other))
    m_own, ea, eb, msk, rim, rimd, wgt, fz, fr, fc, inv = misfit(
        sc, got, svm, msk, rim, rimd, wgt, fz, fr, fc, inv
    )
    fz, fr, fc, inv, gx = ghosts(sc, *near_rows, relayed, msk, rim, rimd, fz, fr, fc, inv)
    th = (sc, layer_thick, thick_other)

    ga, gb = swap(ea, 0), swap(eb, 1)
    m_oth = swap_layers(m_own)
    fz, fr, fc, inv, *state, invx, wgtx = own_sweeps(*th, stored, invx, wgtx, gx, m_own, wgt, (fz, fr, fc, inv))
    g_oth = swap_layers(jnp.concatenate([ga, gb]))
    *both, adj = both_sweeps(*th, ga, gb, m_oth, (fz, fr, fc, inv, wgt), (invx, wgtx), state)
    adjoint, gradient = last_sweeps(*th, g_oth, both[3], (fz, fr, fc, invx, wgtx), both[4:], adj)
    return adjoint, gradient


def solution(mesh):
    in_specs = (
        P("layer", "tile", None),
        P("tile", None),
        P(None, "tile", None),
        P(None, "tile", None),
        P("layer"),
        P("tile", None),
        P("tile", None, None, None),
        P("tile", None),
    )
    out_specs = (P(None, "layer", "tile", None), P("tile", None))

    return jax.shard_map(body, mesh=mesh, in_specs=in_specs, out_specs=out_specs, check_vma=False)
```

```python
import jax
import jax.numpy as jnp
from jax import lax
from jax.experimental import pallas as pl
from jax.experimental.pallas import tpu as pltpu
from jax.sharding import PartitionSpec as P


F32 = jnp.float32
BF16 = jnp.bfloat16
ROWS = 64
EXT = 68
FIELD = (EXT, 64, 128)
STRIP = (ROWS * 8, 128)
MIB = 1 << 20


def vm():
    return pl.BlockSpec(memory_space=pltpu.VMEM)


def sm():
    return pl.BlockSpec(memory_space=pltpu.SMEM)


def hbm():
    return pl.BlockSpec(memory_space=pltpu.HBM)


def far(x):
    return pltpu.with_memory_space_constraint(x, pltpu.HBM)


def kept(*shape, dtype=F32):
    return pltpu.VMEM(shape, dtype)


def near(x):
    return pltpu.with_memory_space_constraint(x, pltpu.VMEM)


def row(r):
    return pl.ds(pl.multiple_of(r * 8, 8), 8)


def at(l):
    return pl.ds(l * 8, 8)


def place(sc):
    return sc[0] & 1, sc[0] >> 1


def lanes():
    lane = lax.broadcasted_iota(jnp.int32, (8, 128), 1)
    sub = lax.broadcasted_iota(jnp.int32, (8, 128), 0)
    return lane, sub


def east(x, last):
    r = pltpu.roll(x, 127, 1)
    return jnp.where(last, pltpu.roll(r, 7, 0), r)


def west(x, first):
    r = pltpu.roll(x, 1, 1)
    return jnp.where(first, pltpu.roll(r, 1, 0), r)


def code_of(t):
    return jnp.where(t < 512, (128 + (t & 127)) << (t >> 7), 0)


def narrow_kernel(visc, slots, target, narrow, x, t, vx, vy, vin, vout, st):
    layers = visc.shape[0]
    takes = [pltpu.make_async_copy(visc.at[i], vx.at[i], vin.at[i]) for i in range(layers)]
    gives = [pltpu.make_async_copy(vy.at[i], narrow.at[i], vout.at[i]) for i in range(layers)]
    fetch = [pltpu.make_async_copy(target, t, st.at[0]), pltpu.make_async_copy(slots, x, st.at[1])]
    for i in (*takes, *fetch):
        i.start()
    for i in range(layers):
        takes[i].wait()
        vy[i] = vx[i].astype(BF16)
        gives[i].start()
    for i in (*gives, *fetch):
        i.wait()


def narrowed(visc, slots, target):
    return pl.pallas_call(
        narrow_kernel,
        in_specs=[hbm()] * 3,
        out_specs=[hbm(), vm(), vm()],
        out_shape=[pltpu.HBM(visc.shape, BF16), kept(*slots.shape, dtype=BF16), kept(*target.shape, dtype=jnp.int32)],
        scratch_shapes=[
            pltpu.VMEM(visc.shape, F32),
            pltpu.VMEM(visc.shape, BF16),
            pltpu.SemaphoreType.DMA((visc.shape[0],)),
            pltpu.SemaphoreType.DMA((visc.shape[0],)),
            pltpu.SemaphoreType.DMA((2,)),
        ],
        compiler_params=pltpu.CompilerParams(vmem_limit_bytes=8 * MIB),
    )(far(visc), far(slots), far(target))


def pack_kernel(sc, x, t, o, y, f, codes, sout):
    own, _ = place(sc)
    n = x.shape[0]
    step = n // CHUNKS
    outs = [
        pltpu.make_async_copy(y.at[pl.ds(i * step, step)], o.at[pl.ds(i * step, step)], sout.at[i])
        for i in range(CHUNKS)
    ]
    c = code_of(t[...]).astype(F32)
    codes[...] = jnp.concatenate([c, c], axis=1)
    for i in range(CHUNKS):

        def one(d, carry):
            f[d] = x[d].astype(F32)
            y[d, pl.ds(0, 64), :] = f[d, pl.ds(own, 64, stride=2), :].astype(BF16)
            y[d, pl.ds(64, 8), :] = jnp.broadcast_to(codes[pl.ds(d, 1), :], (8, 128)).astype(BF16)
            return carry

        lax.fori_loop(i * step, (i + 1) * step, one, 0, unroll=8)
        outs[i].start()
    for i in outs:
        i.wait()


CHUNKS = 8


def pack(sc, slots, target):
    n = slots.shape[0]
    return pl.pallas_call(
        pack_kernel,
        in_specs=[sm(), vm(), vm()],
        out_specs=hbm(),
        out_shape=pltpu.HBM((n, 72, 128), BF16),
        scratch_shapes=[
            pltpu.VMEM((n, 72, 128), BF16),
            pltpu.VMEM((n, 128, 128), F32),
            pltpu.VMEM((n, 128), F32),
            pltpu.SemaphoreType.DMA((CHUNKS,)),
        ],
        compiler_params=pltpu.CompilerParams(vmem_limit_bytes=16 * MIB),
    )(sc, near(slots), near(target))


def edge_kernel(sc, visc, mask, fric, to_a, to_b, v, m, d, s, sem):
    _, odd = place(sc)
    copies = []
    for side in range(2):
        at = pl.ds(side * (ROWS - 8), 8)
        copies.append(pltpu.make_async_copy(visc.at[:, at, :], v.at[side], sem.at[side * 3]))
        copies.append(pltpu.make_async_copy(mask.at[at, :], m.at[side], sem.at[side * 3 + 1]))
        copies.append(pltpu.make_async_copy(fric.at[at, :], d.at[side], sem.at[side * 3 + 2]))
    for c in copies:
        c.start()
    for c in copies:
        c.wait()
    for side in range(2):
        for i in range(4):
            s[side, pl.ds(3 * i, 3), :] = v[side, i, pl.ds(5 * side, 3), :]
        s[side, pl.ds(12, 2), :] = m[side, pl.ds(6 * side, 2), :].astype(F32)
        s[side, pl.ds(14, 2), :] = d[side, pl.ds(6 * side, 2), :]
    to_a[...] = s[1 - odd].astype(BF16)
    to_b[...] = s[odd].astype(BF16)


def edge_rows(sc, visc, mask, fric):
    return pl.pallas_call(
        edge_kernel,
        in_specs=[sm(), hbm(), hbm(), hbm()],
        out_specs=[vm()] * 2,
        out_shape=[kept(16, 1024, dtype=BF16)] * 2,
        scratch_shapes=[
            pltpu.VMEM((2, 4, 8, 1024), F32),
            pltpu.VMEM((2, 8, 1024), jnp.int32),
            pltpu.VMEM((2, 8, 1024), F32),
            pltpu.VMEM((2, 16, 1024), F32),
            pltpu.SemaphoreType.DMA((6,)),
        ],
        compiler_params=pltpu.CompilerParams(vmem_limit_bytes=8 * MIB),
    )(sc, far(visc), far(mask), far(fric))


def spread(dst, at, x):
    n = x.shape[0]
    for k in range(8):
        dst[pl.ds(at + k, n, stride=8), :] = x[:, k * 128 : (k + 1) * 128]


def weights(c):
    return jnp.where(c == 0, 4.0, 1.0), jnp.where(c == 0, 1.0, 4.0)


def coefficient_row(view, m, drag, r, pairs, fz, fr, fc, invs):
    lane, sub = lanes()
    last, first = lane == 127, lane == 0
    end = last & (sub == 7)
    start = first & (sub == 0)
    prev = None
    for l in range(8):
        c = view(l, 0)
        fe = 0.5 * (c + jnp.where(end, 0.0, east(c, last)))
        fw = 0.5 * (c + jnp.where(start, 0.0, west(c, first)))
        south = 0.5 * (c + view(l, 1))
        north = 0.5 * (c + view(l, -1))
        below = 4.0 * c if l == 0 else prev
        above = 4.0 * (c + view(l + 1, 0)) if l < 7 else 4.0 * c
        fz[r, at(l), :] = above
        fr[r, at(l), :] = south
        fc[r, at(l), :] = jnp.where(end, 0.0, fe)
        rows_, cols_, both = north + south, fe + fw, below + above
        if l == 0:
            both = both + drag
        for (rw, cw), inv, shift in zip(pairs, *invs):
            diag = both + rw * rows_ + cw * cols_
            inv[r + shift, at(l), :] = jnp.where(m, 0.7 / diag, 0.0)
        prev = above


GROUPS = ((3, 16), (16, 32), (32, 48), (48, 60), (60, 65))
INSIDE = pl.ds(3, 62)
EARLY = pl.ds(3, 29)
LATER = ((32, 16), (48, 17))
RIM = (8, 32, 128)
N_FIELDS = 5


def coef_kernel(sc, visc, other, fric, mask, bvel, svel, *refs):
    outs, rest = refs[:11], refs[11:]
    fields, (wo, wx, svm, msk, rim, rimd, drg, v, bv, sem, sem2) = rest[:N_FIELDS], rest[N_FIELDS:]
    fz, fr, fc, inv_own, inv_oth = fields
    own, _ = place(sc)
    for i in range(4):
        for src, to in ((visc, own * 4 + i), (other, (1 - own) * 4 + i)):
            for h in range(0, ROWS, 16):
                spread(v.at[to], h * 8, src[i, h : h + 16, :].astype(F32))
    for h in range(0, ROWS, 16):
        spread(msk, h * 8, mask[h : h + 16, :].astype(F32))
        spread(drg, h * 8, fric[h : h + 16, :])
        spread(svm, h * 8, svel[own, h : h + 16, :])
        spread(bv.at[0], h * 8, bvel[own, h : h + 16, :])
        spread(bv.at[1], h * 8, bvel[1 - own, h : h + 16, :])
    for l in range(8):
        rim[l, pl.ds(0, 16), :] = v[l, pl.ds(0, 16), :]
        rim[l, pl.ds(16, 16), :] = v[l, pl.ds((ROWS - 2) * 8, 16), :]
    rimd[pl.ds(0, 8), :] = drg[row(0), :]
    rimd[pl.ds(8, 8), :] = drg[row(ROWS - 1), :]
    pairs = (weights(own), weights(1 - own))

    def strips(r):
        m, d = msk[row(r), :], drg[row(r), :]
        svm[row(r), :] = svm[row(r), :] * m
        for c, w in enumerate((wo, wx)):
            w[row(r), :] = (-m * d) * bv[c, row(r), :]
        return m, d

    def step(r, carry):
        m, d = strips(r)
        invs = ((inv_own, inv_oth), (0, 0))
        coefficient_row(lambda l, j: v[l, row(r + j), :], m > 0.5, d, r + 2, pairs, fz, fr, fc, invs)
        return carry

    strips(0)
    strips(ROWS - 1)
    copies = []
    for i, (src, dst) in enumerate(zip((msk, rim, rimd), outs[8:])):
        copies.append(pltpu.make_async_copy(src, dst, sem2.at[i]))
    for c in copies:
        c.start()
    for k, (a, b) in enumerate(GROUPS):
        lax.fori_loop(a - 2, b - 2, step, 0)
        part = pl.ds(a, b - a)
        for i, src in enumerate(fields):
            copies.append(pltpu.make_async_copy(src.at[part], outs[i].at[part], sem.at[k, i]))
            copies[-1].start()
    for i, (src, dst) in enumerate(zip((wo, wx, svm), outs[5:])):
        copies.append(pltpu.make_async_copy(src, dst, sem2.at[3 + i]))
        copies[-1].start()
    for c in copies:
        c.wait()


def coefficients(sc, visc, other, fric, mask, bvel, svel):
    shapes = (FIELD,) * N_FIELDS + (STRIP,) * 4 + (RIM, (16, 128))
    return pl.pallas_call(
        coef_kernel,
        in_specs=[sm()] + [vm()] * 6,
        out_specs=[hbm()] * 11,
        out_shape=[pltpu.HBM(x, F32) for x in shapes],
        scratch_shapes=[pltpu.VMEM(x, F32) for x in shapes]
        + [
            pltpu.VMEM(STRIP, F32),
            pltpu.VMEM((8, (ROWS + 1) * 8, 128), F32),
            pltpu.VMEM((2, *STRIP), F32),
            pltpu.SemaphoreType.DMA((len(GROUPS), N_FIELDS)),
            pltpu.SemaphoreType.DMA((6,)),
        ],
        compiler_params=pltpu.CompilerParams(vmem_limit_bytes=32 * MIB),
    )(sc, visc, other, fric, mask, bvel, svel)


def ghost_kernel(sc, ea, eb, relayed, msk, rim, rimd, fz0, fr0, fc0, inv0, fz, fr, fc, inv, gx, g, u):
    own, odd = place(sc)
    pairs = (weights(own), weights(1 - own))
    for kind, pair in enumerate(((ea, relayed.at[pl.ds(0, 16)]), (eb, relayed.at[pl.ds(16, 16)]))):
        side = jnp.where((odd + kind) % 2 == 1, 0, 1)
        for who, e in enumerate(pair):
            spread(g.at[side, who], 0, e[...].astype(F32))
    for side in range(2):
        to = 0 if side == 0 else 2
        for who in range(2):
            base = (own if who == 0 else 1 - own) * 4
            for i in range(4):
                u[side, base + i, pl.ds(to * 8, 24), :] = g[side, who, pl.ds(i * 24, 24), :]
        for l in range(8):
            u[side, l, pl.ds(24 * (1 - side), 16), :] = rim[l, pl.ds(16 * side, 16), :]
        for j in range(3):
            if side == 0:
                r, ghost, inside = j, j, 0
            else:
                r, ghost, inside = ROWS + 1 + j, j - 1, ROWS - 1
            if (side == 0 and j == 2) or (side == 1 and j == 0):
                m, d = msk[row(inside), :], rimd[pl.ds(8 * side, 8), :]
            else:
                m, d = g[side, 0, pl.ds((12 + ghost) * 8, 8), :], g[side, 0, pl.ds((14 + ghost) * 8, 8), :]
            invs = ((inv, gx), (0, 0 if side == 0 else 3 - (ROWS + 1)))
            coefficient_row(lambda l, s: u[side, l, row(j + 1 + s), :], m > 0.5, d, r, pairs, fz, fr, fc, invs)


def ghosts(sc, ea, eb, relayed, msk, rim, rimd, fz, fr, fc, inv):
    return pl.pallas_call(
        ghost_kernel,
        in_specs=[sm()] + [vm()] * 10,
        out_specs=[vm()] * 5,
        out_shape=[kept(*FIELD)] * 4 + [kept(6, 64, 128)],
        scratch_shapes=[pltpu.VMEM((2, 2, 128, 128), F32), pltpu.VMEM((2, 8, 40, 128), F32)],
        input_output_aliases={7: 0, 8: 1, 9: 2, 10: 3},
        compiler_params=pltpu.CompilerParams(vmem_limit_bytes=24 * MIB),
    )(sc, *(near(x) for x in (ea, eb, relayed, msk, rim, rimd, fz, fr, fc, inv)))


PARTS = 4


def misfit_kernel(sc, got_h, svm_h, *refs):
    n_kept = len(KEPT)
    here, (m_out, ea, eb), refs = refs[:n_kept], refs[n_kept : n_kept + 3], refs[n_kept + 3 :]
    kept_, (got, svm, hot, rhs, pc, sem, sem2) = refs[:n_kept], refs[n_kept:]
    _, odd = place(sc)
    n = got.shape[0] // PARTS
    parts = [
        pltpu.make_async_copy(got_h.at[pl.ds(i * n, n)], got.at[pl.ds(i * n, n)], sem.at[i]) for i in range(PARTS)
    ]
    strips = pltpu.make_async_copy(svm_h, svm, sem.at[PARTS])
    rest = []
    for i, (x, y) in enumerate(zip(here, kept_)):
        if KEPT[i] == FIELD:
            x, y = x.at[EARLY], y.at[EARLY]
        rest.append(pltpu.make_async_copy(x, y, sem2.at[i]))
    for c in (*parts, strips, *rest):
        c.start()
    msk = kept_[0]
    p = lax.broadcasted_iota(jnp.int32, (512, 128), 0)
    pc[...] = code_of(p).astype(F32)
    rhs[:, pl.ds(128, 128)] = jnp.ones((rhs.shape[0], 128), BF16)
    lane = lax.broadcasted_iota(jnp.int32, (8, 128), 1)
    for part in parts:
        part.wait()
    for part in range(PARTS):
        for b in range(n // 2):
            s = part * n + 2 * b
            for h in range(2):
                rhs[pl.ds((s + h) * 64, 64), pl.ds(0, 128)] = got[s + h, pl.ds(0, 64), :]
            c = jnp.where(lane < 64, got[s, pl.ds(64, 8), :].astype(F32), got[s + 1, pl.ds(64, 8), :].astype(F32))
            same = pc[...].reshape(64, 8, 128) == c[None]
            hot[:, pl.ds(s * 64, 128)] = jnp.where(same, 1.0, 0.0).reshape(512, 128).astype(BF16)
    sums = jnp.dot(hot[...], rhs[...], preferred_element_type=F32)
    strips.wait()
    rest[0].wait()
    m_out[...] = sums[:, 128:] * svm[...] - msk[...] * sums[:, :128]
    for kind, e in enumerate((ea, eb)):
        start = jnp.where((odd + kind) % 2 == 0, ROWS - 2, 0)
        for r in range(2):
            e[pl.ds(r * 8, 8), :] = m_out[row(start + r), :]
    for c in rest[1:]:
        c.wait()


KEPT = (STRIP, RIM, (16, 128), STRIP) + (FIELD,) * 4


def misfit(sc, got, svm, *rest):
    k = got.shape[0] * 64
    return pl.pallas_call(
        misfit_kernel,
        in_specs=[sm()] + [hbm()] * (2 + len(KEPT)),
        out_specs=[vm()] * (3 + len(KEPT)),
        out_shape=[kept(*STRIP), kept(16, 128), kept(16, 128)] + [kept(*x) for x in KEPT],
        scratch_shapes=[
            pltpu.VMEM(got.shape, BF16),
            pltpu.VMEM(STRIP, F32),
            pltpu.VMEM((512, k), BF16),
            pltpu.VMEM((k, 256), BF16),
            pltpu.VMEM((512, 128), F32),
            pltpu.SemaphoreType.DMA((PARTS + 1,)),
            pltpu.SemaphoreType.DMA((len(KEPT),)),
        ],
        compiler_params=pltpu.CompilerParams(vmem_limit_bytes=24 * MIB),
    )(sc, *(far(x) for x in (got, svm, *rest)))


class Sweeps:
    def __init__(self, sc, t1, t2, c, coefs, state, turned):
        self.own, self.odd = place(sc)
        self.fz, self.fr, self.fc, self.inv, self.wgt = coefs
        self.a1, self.a2, self.a3, self.acc = state
        self.turned = turned
        self.thick = [jnp.where(self.own == l // 4, t1[l % 4], t2[l % 4]) for l in range(8)]
        self.rw, self.cw = weights(c)
        lane, _ = lanes()
        self.last, self.first_lane = lane == 127, lane == 0

    def turn(self, k, r, slot=0):
        a = (self.a1, self.a2)[k]
        for l in range(8):
            x, f = a[r, at(l), :], self.fc[r, at(l), :]
            self.turned[k, slot, l] = self.cw * (f * east(x, self.last) + west(f * x, self.first_lane))

    def neighbours(self, k, l, r, slot):
        a = (self.a1, self.a2)[k]
        n = None
        if l < 7:
            n = self.fz[r, at(l), :] * a[r, at(l + 1), :]
        if l > 0:
            t = self.fz[r, at(l - 1), :] * a[r, at(l - 1), :]
            n = t if n is None else n + t
        rows_ = self.fr[r, at(l), :] * a[r + 1, at(l), :] + self.fr[r - 1, at(l), :] * a[r - 1, at(l), :]
        return self.inv[r, at(l), :] * (n + self.rw * rows_ + self.turned[k, slot, l])

    def first(self, r, m):
        for l in range(8):
            self.a1[r, at(l), :] = self.inv[r, at(l), :] * (self.thick[l] * m)

    def second(self, r, slot=0):
        for l in range(8):
            self.a2[r, at(l), :] = 1.3 * self.a1[r, at(l), :] + self.neighbours(0, l, r, slot)

    def third(self, r, slot=0):
        total = None
        for l in range(8):
            y = 0.3 * self.a2[r, at(l), :] + (self.a1[r, at(l), :] + self.neighbours(1, l, r, slot))
            self.a3[l, row(r - 2), :] = y
            total = self.thick[l] * y if l == 0 else total + self.thick[l] * y
        self.acc[row(r - 2), :] = self.wgt[row(r - 2), :] * total

    def interior(self, m, ready=()):
        for r in (1, EXT - 2):
            self.a1[r] = jnp.zeros((64, 128), F32)

        def stage(p, static):
            for k, back in ((1, 4), (1, 3), (0, 2), (0, 1), (None, 0)):
                q = p - back
                if static and not (2 if k == 1 else 1) <= q <= (31 if k == 1 else 32):
                    continue
                for j in range(2):
                    r = 2 * q + j
                    if back == 4:
                        self.third(r, j)
                    elif back == 2:
                        self.second(r, j)
                    elif back:
                        self.turn(k, r, j)
                    else:
                        self.first(r, m[row(r - 2), :])

        def step(p, carry):
            stage(p, False)
            return carry

        for p in range(1, 6):
            stage(p, True)
        at_ = 6
        for upto, wait in ready:
            lax.fori_loop(at_, upto, step, 0)
            wait()
            at_ = upto
        lax.fori_loop(at_, 33, step, 0)
        for p in range(33, 36):
            stage(p, True)

    def edges(self, ga, gb):
        up = jnp.where(self.odd == 1, ga[...], gb[...])
        down = jnp.where(self.odd == 1, gb[...], ga[...])
        for ghost, firsts, seconds, thirds in (
            (up, (0, 1), (1, 2), (2, 3)),
            (down, (66, 67), (65, 66), (64, 65)),
        ):
            for i, r in enumerate(firsts):
                self.first(r, ghost[i * 8 : i * 8 + 8, :])
            for r in seconds:
                self.turn(0, r)
                self.second(r)
            for r in thirds:
                self.turn(1, r)
                self.third(r)


INNER, OUTER = range(8, ROWS - 8, 8), (0, ROWS - 8)


def gather_rows(dst, src, rows=range(0, ROWS, 8)):
    for h in rows:
        for k in range(8):
            dst[pl.ds(h, 8), pl.ds(k * 128, 128)] = src[pl.ds(h * 8 + k, 8, stride=8), :]


TURNED = (2, 2, 8, 8, 128)
STATE = (FIELD, FIELD, (8, (ROWS + 1) * 8, 128), STRIP)
N_STATE = len(STATE)
STAGE = (4, ROWS, 1024)


def own_kernel(sc, t1, t2, fz_h, fr_h, fc_h, inv_h, invx_h, wgtx_h, gx, m, wgt, *refs):
    fields, state, (invx, wgtx, turned, sem, sem2) = refs[4:8], refs[8:12], refs[12:]
    own, _ = place(sc)
    groups = []
    for i, (first, rows) in enumerate(LATER):
        part = pl.ds(first, rows)
        pairs = zip((fz_h, fr_h, fc_h, inv_h), fields)
        groups.append([pltpu.make_async_copy(x.at[part], y.at[part], sem.at[i, j]) for j, (x, y) in enumerate(pairs)])
    copies = (
        pltpu.make_async_copy(invx_h.at[INSIDE], invx.at[INSIDE], sem2.at[0]),
        pltpu.make_async_copy(wgtx_h, wgtx, sem2.at[1]),
    )
    for c in (*groups[0], *groups[1], *copies):
        c.start()

    def waiting(group):
        def wait():
            for c in group:
                c.wait()

        return wait

    ready = [(first // 2, waiting(group)) for (first, _), group in zip(LATER, groups)]
    Sweeps(sc, t1, t2, own, (*fields, wgt), state, turned).interior(m, ready)
    for c in copies:
        c.wait()
    invx[pl.ds(0, 3)] = gx[pl.ds(0, 3)]
    invx[pl.ds(ROWS + 1, 3)] = gx[pl.ds(3, 3)]


def own_sweeps(sc, t1, t2, stored, invx, wgtx, gx, m, wgt, fields):
    return pl.pallas_call(
        own_kernel,
        in_specs=[sm()] * 3 + [hbm()] * 6 + [vm()] * 7,
        out_specs=[vm()] * 10,
        out_shape=[kept(*s) for s in (*(FIELD,) * 4, *STATE, FIELD, STRIP)],
        scratch_shapes=[
            pltpu.VMEM(TURNED, F32),
            pltpu.SemaphoreType.DMA((len(LATER), 4)),
            pltpu.SemaphoreType.DMA((2,)),
        ],
        input_output_aliases={12 + i: i for i in range(4)},
        compiler_params=pltpu.CompilerParams(vmem_limit_bytes=24 * MIB),
    )(sc, t1, t2, *(far(x) for x in (*stored, invx, wgtx)), *(near(x) for x in (gx, m, wgt, *fields)))


def both_kernel(sc, t1, t2, ga, gb, m, *refs):
    (fz, fr, fc, inv, wgt, invx, wgtx), refs = refs[:7], refs[7 + N_STATE :]
    done, todo, adj, (stage, turned, sem) = refs[:4], refs[4:8], refs[8], refs[9:]
    own, _ = place(sc)
    Sweeps(sc, t1, t2, own, (fz, fr, fc, inv, wgt), done, turned).edges(ga, gb)
    for i in range(4):
        gather_rows(stage.at[i], done[2].at[own * 4 + i])
    copy = pltpu.make_async_copy(stage, adj.at[own], sem)
    copy.start()
    Sweeps(sc, t1, t2, 1 - own, (fz, fr, fc, invx, wgtx), todo, turned).interior(m)
    copy.wait()


def both_sweeps(sc, t1, t2, ga, gb, m, coefs, others, state):
    return pl.pallas_call(
        both_kernel,
        in_specs=[sm()] * 3 + [vm()] * (3 + 7 + N_STATE),
        out_specs=[vm()] * (2 * N_STATE) + [hbm()],
        out_shape=[kept(*s) for s in STATE] * 2 + [pltpu.HBM((2, *STAGE), F32)],
        scratch_shapes=[pltpu.VMEM(STAGE, F32), pltpu.VMEM(TURNED, F32), pltpu.SemaphoreType.DMA],
        input_output_aliases={13 + i: i for i in range(N_STATE)},
        compiler_params=pltpu.CompilerParams(vmem_limit_bytes=24 * MIB),
    )(sc, t1, t2, *(near(x) for x in (ga, gb, m, *coefs, *others, *state)))


def last_kernel(sc, t1, t2, g, racc, fz, fr, fc, inv, wgt, *refs):
    state, (adj, grad), (stage, sum_, turned, sem) = refs[5:9], refs[9:11], refs[11:]
    _, _, a3, acc = state
    own, _ = place(sc)
    to = adj.at[1 - own]
    spans = (pl.ds(8, ROWS - 16), pl.ds(0, 8), pl.ds(ROWS - 8, 8))
    copies = [pltpu.make_async_copy(stage.at[:, x, :], to.at[:, x, :], sem.at[i]) for i, x in enumerate(spans)]
    copies += [pltpu.make_async_copy(sum_.at[x, :], grad.at[x, :], sem.at[3 + i]) for i, x in enumerate(spans)]
    for i in range(4):
        gather_rows(stage.at[i], a3.at[own * 4 + i], INNER)
    copies[0].start()
    for r in INNER:
        acc[pl.ds(r * 8, 64), :] = acc[pl.ds(r * 8, 64), :] + racc[pl.ds(r * 8, 64), :]
    gather_rows(sum_, acc, INNER)
    copies[3].start()
    Sweeps(sc, t1, t2, 1 - own, (fz, fr, fc, inv, wgt), state, turned).edges(
        g.at[pl.ds(0, 16), :], g.at[pl.ds(16, 16), :]
    )
    for i in range(4):
        gather_rows(stage.at[i], a3.at[own * 4 + i], OUTER)
    copies[1].start()
    copies[2].start()
    for r in OUTER:
        acc[pl.ds(r * 8, 64), :] = acc[pl.ds(r * 8, 64), :] + racc[pl.ds(r * 8, 64), :]
    gather_rows(sum_, acc, OUTER)
    copies[4].start()
    copies[5].start()
    for c in copies:
        c.wait()


def last_sweeps(sc, t1, t2, g, racc, coefs, state, adj):
    return pl.pallas_call(
        last_kernel,
        in_specs=[sm()] * 3 + [vm()] * 11 + [hbm()],
        out_specs=[vm()] * 4 + [hbm(), hbm()],
        out_shape=[kept(*s) for s in STATE]
        + [pltpu.HBM((2, *STAGE), F32), pltpu.HBM((ROWS, 1024), F32)],
        scratch_shapes=[
            pltpu.VMEM(STAGE, F32),
            pltpu.VMEM((ROWS, 1024), F32),
            pltpu.VMEM(TURNED, F32),
            pltpu.SemaphoreType.DMA((6,)),
        ],
        input_output_aliases={10: 0, 11: 1, 12: 2, 13: 3, 14: 4},
        compiler_params=pltpu.CompilerParams(vmem_limit_bytes=24 * MIB),
    )(sc, t1, t2, *(near(x) for x in (g, racc, *coefs, *state)), far(adj))[4:]


def swaps(tiles, offset):
    perm = []
    for t in range(offset, tiles - 1, 2):
        perm += [(t, t + 1), (t + 1, t)]
    return perm


def swap_layers(x):
    return lax.ppermute(x, "layer", [(0, 1), (1, 0)])


def body(viscosity, friction, base_vel, surf_vel, layer_thick, ice_mask, obs_slots, obs_target):
    tiles = lax.axis_size("tile")
    own = lax.axis_index("layer")
    odd = lax.axis_index("tile") % 2
    sc = (own + 2 * odd).astype(jnp.int32).reshape(1)

    def swap(x, kind):
        return lax.ppermute(x, "tile", swaps(tiles, kind))

    narrow, slots, target = narrowed(viscosity, obs_slots.reshape(tiles, 128, 128), obs_target)
    other = swap_layers(narrow)
    payload = pack(sc, slots, target)
    got = lax.all_to_all(payload, "tile", split_axis=0, concat_axis=0, tiled=True)
    thick_other = swap_layers(layer_thick)

    to_a, to_b = edge_rows(sc, viscosity, ice_mask, friction)
    near_rows = (swap(to_a, 0), swap(to_b, 1))
    relayed = swap_layers(jnp.concatenate(near_rows))
    fz, fr, fc, inv, invx, wgt, wgtx, svm, msk, rim, rimd = coefficients(
        sc, viscosity, other, friction, ice_mask, base_vel, surf_vel
    )
    stored = (fz, fr, fc, inv)
    got, near_rows, thick_other = lax.optimization_barrier((got, near_rows, thick_other))
    m_own, ea, eb, msk, rim, rimd, wgt, fz, fr, fc, inv = misfit(
        sc, got, svm, msk, rim, rimd, wgt, fz, fr, fc, inv
    )
    fz, fr, fc, inv, gx = ghosts(sc, *near_rows, relayed, msk, rim, rimd, fz, fr, fc, inv)
    th = (sc, layer_thick, thick_other)

    ga, gb = swap(ea, 0), swap(eb, 1)
    m_oth = swap_layers(m_own)
    fz, fr, fc, inv, *state, invx, wgtx = own_sweeps(*th, stored, invx, wgtx, gx, m_own, wgt, (fz, fr, fc, inv))
    g_oth = swap_layers(jnp.concatenate([ga, gb]))
    *both, adj = both_sweeps(*th, ga, gb, m_oth, (fz, fr, fc, inv, wgt), (invx, wgtx), state)
    adjoint, gradient = last_sweeps(*th, g_oth, both[3], (fz, fr, fc, invx, wgtx), both[4:], adj)
    return adjoint, gradient


def solution(mesh):
    in_specs = (
        P("layer", "tile", None),
        P("tile", None),
        P(None, "tile", None),
        P(None, "tile", None),
        P("layer"),
        P("tile", None),
        P("tile", None, None, None),
        P("tile", None),
    )
    out_specs = (P(None, "layer", "tile", None), P("tile", None))

    return jax.shard_map(body, mesh=mesh, in_specs=in_specs, out_specs=out_specs, check_vma=False)
```

```python
import jax
import jax.numpy as jnp
from jax import lax
from jax.experimental import pallas as pl
from jax.experimental.pallas import tpu as pltpu
from jax.sharding import PartitionSpec as P


F32 = jnp.float32
BF16 = jnp.bfloat16
ROWS = 64
EXT = 68
FIELD = (EXT, 64, 128)
STRIP = (ROWS * 8, 128)
MIB = 1 << 20


def vm():
    return pl.BlockSpec(memory_space=pltpu.VMEM)


def sm():
    return pl.BlockSpec(memory_space=pltpu.SMEM)


def hbm():
    return pl.BlockSpec(memory_space=pltpu.HBM)


def far(x):
    return pltpu.with_memory_space_constraint(x, pltpu.HBM)


def kept(*shape, dtype=F32):
    return pltpu.VMEM(shape, dtype)


def near(x):
    return pltpu.with_memory_space_constraint(x, pltpu.VMEM)


def row(r):
    return pl.ds(pl.multiple_of(r * 8, 8), 8)


def at(l):
    return pl.ds(l * 8, 8)


def place(sc):
    return sc[0] & 1, sc[0] >> 1


def lanes():
    lane = lax.broadcasted_iota(jnp.int32, (8, 128), 1)
    sub = lax.broadcasted_iota(jnp.int32, (8, 128), 0)
    return lane, sub


def east(x, last):
    r = pltpu.roll(x, 127, 1)
    return jnp.where(last, pltpu.roll(r, 7, 0), r)


def west(x, first):
    r = pltpu.roll(x, 1, 1)
    return jnp.where(first, pltpu.roll(r, 1, 0), r)


def code_of(t):
    return jnp.where(t < 512, (128 + (t & 127)) << (t >> 7), 0)


def narrow_kernel(visc, slots, target, narrow, x, t, vx, vy, vin, vout, st):
    layers = visc.shape[0]
    takes = [pltpu.make_async_copy(visc.at[i], vx.at[i], vin.at[i]) for i in range(layers)]
    gives = [pltpu.make_async_copy(vy.at[i], narrow.at[i], vout.at[i]) for i in range(layers)]
    fetch = [pltpu.make_async_copy(target, t, st.at[0]), pltpu.make_async_copy(slots, x, st.at[1])]
    for i in (*takes, *fetch):
        i.start()
    for i in range(layers):
        takes[i].wait()
        vy[i] = vx[i].astype(BF16)
        gives[i].start()
    for i in (*gives, *fetch):
        i.wait()


def narrowed(visc, slots, target):
    return pl.pallas_call(
        narrow_kernel,
        in_specs=[hbm()] * 3,
        out_specs=[hbm(), vm(), vm()],
        out_shape=[pltpu.HBM(visc.shape, BF16), kept(*slots.shape, dtype=BF16), kept(*target.shape, dtype=jnp.int32)],
        scratch_shapes=[
            pltpu.VMEM(visc.shape, F32),
            pltpu.VMEM(visc.shape, BF16),
            pltpu.SemaphoreType.DMA((visc.shape[0],)),
            pltpu.SemaphoreType.DMA((visc.shape[0],)),
            pltpu.SemaphoreType.DMA((2,)),
        ],
        compiler_params=pltpu.CompilerParams(vmem_limit_bytes=8 * MIB),
    )(far(visc), far(slots), far(target))


def pack_kernel(sc, x, t, o, y, f, codes, sout):
    own, _ = place(sc)
    n = x.shape[0]
    step = n // CHUNKS
    outs = [
        pltpu.make_async_copy(y.at[pl.ds(i * step, step)], o.at[pl.ds(i * step, step)], sout.at[i])
        for i in range(CHUNKS)
    ]
    c = code_of(t[...]).astype(F32)
    codes[...] = jnp.concatenate([c, c], axis=1)
    for i in range(CHUNKS):

        def one(d, carry):
            f[d] = x[d].astype(F32)
            y[d, pl.ds(0, 64), :] = f[d, pl.ds(own, 64, stride=2), :].astype(BF16)
            y[d, pl.ds(64, 8), :] = jnp.broadcast_to(codes[pl.ds(d, 1), :], (8, 128)).astype(BF16)
            return carry

        lax.fori_loop(i * step, (i + 1) * step, one, 0, unroll=8)
        outs[i].start()
    for i in outs:
        i.wait()


CHUNKS = 8


def pack(sc, slots, target):
    n = slots.shape[0]
    return pl.pallas_call(
        pack_kernel,
        in_specs=[sm(), vm(), vm()],
        out_specs=hbm(),
        out_shape=pltpu.HBM((n, 72, 128), BF16),
        scratch_shapes=[
            pltpu.VMEM((n, 72, 128), BF16),
            pltpu.VMEM((n, 128, 128), F32),
            pltpu.VMEM((n, 128), F32),
            pltpu.SemaphoreType.DMA((CHUNKS,)),
        ],
        compiler_params=pltpu.CompilerParams(vmem_limit_bytes=16 * MIB),
    )(sc, near(slots), near(target))


def edge_kernel(sc, visc, mask, fric, to_a, to_b, v, m, d, s, sem):
    _, odd = place(sc)
    copies = []
    for side in range(2):
        at = pl.ds(side * (ROWS - 8), 8)
        copies.append(pltpu.make_async_copy(visc.at[:, at, :], v.at[side], sem.at[side * 3]))
        copies.append(pltpu.make_async_copy(mask.at[at, :], m.at[side], sem.at[side * 3 + 1]))
        copies.append(pltpu.make_async_copy(fric.at[at, :], d.at[side], sem.at[side * 3 + 2]))
    for c in copies:
        c.start()
    for c in copies:
        c.wait()
    for side in range(2):
        for i in range(4):
            s[side, pl.ds(3 * i, 3), :] = v[side, i, pl.ds(5 * side, 3), :]
        s[side, pl.ds(12, 2), :] = m[side, pl.ds(6 * side, 2), :].astype(F32)
        s[side, pl.ds(14, 2), :] = d[side, pl.ds(6 * side, 2), :]
    to_a[...] = s[1 - odd].astype(BF16)
    to_b[...] = s[odd].astype(BF16)


def edge_rows(sc, visc, mask, fric):
    return pl.pallas_call(
        edge_kernel,
        in_specs=[sm(), hbm(), hbm(), hbm()],
        out_specs=[vm()] * 2,
        out_shape=[kept(16, 1024, dtype=BF16)] * 2,
        scratch_shapes=[
            pltpu.VMEM((2, 4, 8, 1024), F32),
            pltpu.VMEM((2, 8, 1024), jnp.int32),
            pltpu.VMEM((2, 8, 1024), F32),
            pltpu.VMEM((2, 16, 1024), F32),
            pltpu.SemaphoreType.DMA((6,)),
        ],
        compiler_params=pltpu.CompilerParams(vmem_limit_bytes=8 * MIB),
    )(sc, far(visc), far(mask), far(fric))


def spread(dst, at, x):
    n = x.shape[0]
    for k in range(8):
        dst[pl.ds(at + k, n, stride=8), :] = x[:, k * 128 : (k + 1) * 128]


def weights(c):
    return jnp.where(c == 0, 4.0, 1.0), jnp.where(c == 0, 1.0, 4.0)


def coefficient_row(view, m, drag, r, pairs, fz, fr, fc, invs):
    lane, sub = lanes()
    last, first = lane == 127, lane == 0
    end = last & (sub == 7)
    start = first & (sub == 0)
    prev = None
    for l in range(8):
        c = view(l, 0)
        fe = 0.5 * (c + jnp.where(end, 0.0, east(c, last)))
        fw = 0.5 * (c + jnp.where(start, 0.0, west(c, first)))
        south = 0.5 * (c + view(l, 1))
        north = 0.5 * (c + view(l, -1))
        below = 4.0 * c if l == 0 else prev
        above = 4.0 * (c + view(l + 1, 0)) if l < 7 else 4.0 * c
        fz[r, at(l), :] = above
        fr[r, at(l), :] = south
        fc[r, at(l), :] = jnp.where(end, 0.0, fe)
        rows_, cols_, both = north + south, fe + fw, below + above
        if l == 0:
            both = both + drag
        for (rw, cw), inv, shift in zip(pairs, *invs):
            diag = both + rw * rows_ + cw * cols_
            inv[r + shift, at(l), :] = jnp.where(m, 0.7 / diag, 0.0)
        prev = above


GROUPS = ((3, 16), (16, 32), (32, 48), (48, 60), (60, 65))
INSIDE = pl.ds(3, 62)
EARLY = pl.ds(3, 45)
LATER = ((48, 17),)
RIM = (8, 32, 128)
N_FIELDS = 5


def coef_kernel(sc, visc, other, fric, mask, bvel, svel, *refs):
    outs, rest = refs[:11], refs[11:]
    fields, (wo, wx, svm, msk, rim, rimd, drg, v, bv, sem, sem2) = rest[:N_FIELDS], rest[N_FIELDS:]
    fz, fr, fc, inv_own, inv_oth = fields
    own, _ = place(sc)
    for i in range(4):
        for src, to in ((visc, own * 4 + i), (other, (1 - own) * 4 + i)):
            for h in range(0, ROWS, 16):
                spread(v.at[to], h * 8, src[i, h : h + 16, :].astype(F32))
    for h in range(0, ROWS, 16):
        spread(msk, h * 8, mask[h : h + 16, :].astype(F32))
        spread(drg, h * 8, fric[h : h + 16, :])
        spread(svm, h * 8, svel[own, h : h + 16, :])
        spread(bv.at[0], h * 8, bvel[own, h : h + 16, :])
        spread(bv.at[1], h * 8, bvel[1 - own, h : h + 16, :])
    for l in range(8):
        rim[l, pl.ds(0, 16), :] = v[l, pl.ds(0, 16), :]
        rim[l, pl.ds(16, 16), :] = v[l, pl.ds((ROWS - 2) * 8, 16), :]
    rimd[pl.ds(0, 8), :] = drg[row(0), :]
    rimd[pl.ds(8, 8), :] = drg[row(ROWS - 1), :]
    pairs = (weights(own), weights(1 - own))

    def strips(r):
        m, d = msk[row(r), :], drg[row(r), :]
        svm[row(r), :] = svm[row(r), :] * m
        for c, w in enumerate((wo, wx)):
            w[row(r), :] = (-m * d) * bv[c, row(r), :]
        return m, d

    def step(r, carry):
        m, d = strips(r)
        invs = ((inv_own, inv_oth), (0, 0))
        coefficient_row(lambda l, j: v[l, row(r + j), :], m > 0.5, d, r + 2, pairs, fz, fr, fc, invs)
        return carry

    strips(0)
    strips(ROWS - 1)
    copies = []
    for i, (src, dst) in enumerate(zip((msk, rim, rimd), outs[8:])):
        copies.append(pltpu.make_async_copy(src, dst, sem2.at[i]))
    for c in copies:
        c.start()
    for k, (a, b) in enumerate(GROUPS):
        lax.fori_loop(a - 2, b - 2, step, 0)
        part = pl.ds(a, b - a)
        for i, src in enumerate(fields):
            copies.append(pltpu.make_async_copy(src.at[part], outs[i].at[part], sem.at[k, i]))
            copies[-1].start()
    for i, (src, dst) in enumerate(zip((wo, wx, svm), outs[5:])):
        copies.append(pltpu.make_async_copy(src, dst, sem2.at[3 + i]))
        copies[-1].start()
    for c in copies:
        c.wait()


def coefficients(sc, visc, other, fric, mask, bvel, svel):
    shapes = (FIELD,) * N_FIELDS + (STRIP,) * 4 + (RIM, (16, 128))
    return pl.pallas_call(
        coef_kernel,
        in_specs=[sm()] + [vm()] * 6,
        out_specs=[hbm()] * 11,
        out_shape=[pltpu.HBM(x, F32) for x in shapes],
        scratch_shapes=[pltpu.VMEM(x, F32) for x in shapes]
        + [
            pltpu.VMEM(STRIP, F32),
            pltpu.VMEM((8, (ROWS + 1) * 8, 128), F32),
            pltpu.VMEM((2, *STRIP), F32),
            pltpu.SemaphoreType.DMA((len(GROUPS), N_FIELDS)),
            pltpu.SemaphoreType.DMA((6,)),
        ],
        compiler_params=pltpu.CompilerParams(vmem_limit_bytes=32 * MIB),
    )(sc, visc, other, fric, mask, bvel, svel)


def ghost_kernel(sc, ea, eb, relayed, msk, rim, rimd, fz0, fr0, fc0, inv0, fz, fr, fc, inv, gx, g, u):
    own, odd = place(sc)
    pairs = (weights(own), weights(1 - own))
    for kind, pair in enumerate(((ea, relayed.at[pl.ds(0, 16)]), (eb, relayed.at[pl.ds(16, 16)]))):
        side = jnp.where((odd + kind) % 2 == 1, 0, 1)
        for who, e in enumerate(pair):
            spread(g.at[side, who], 0, e[...].astype(F32))
    for side in range(2):
        to = 0 if side == 0 else 2
        for who in range(2):
            base = (own if who == 0 else 1 - own) * 4
            for i in range(4):
                u[side, base + i, pl.ds(to * 8, 24), :] = g[side, who, pl.ds(i * 24, 24), :]
        for l in range(8):
            u[side, l, pl.ds(24 * (1 - side), 16), :] = rim[l, pl.ds(16 * side, 16), :]
        for j in range(3):
            if side == 0:
                r, ghost, inside = j, j, 0
            else:
                r, ghost, inside = ROWS + 1 + j, j - 1, ROWS - 1
            if (side == 0 and j == 2) or (side == 1 and j == 0):
                m, d = msk[row(inside), :], rimd[pl.ds(8 * side, 8), :]
            else:
                m, d = g[side, 0, pl.ds((12 + ghost) * 8, 8), :], g[side, 0, pl.ds((14 + ghost) * 8, 8), :]
            invs = ((inv, gx), (0, 0 if side == 0 else 3 - (ROWS + 1)))
            coefficient_row(lambda l, s: u[side, l, row(j + 1 + s), :], m > 0.5, d, r, pairs, fz, fr, fc, invs)


def ghosts(sc, ea, eb, relayed, msk, rim, rimd, fz, fr, fc, inv):
    return pl.pallas_call(
        ghost_kernel,
        in_specs=[sm()] + [vm()] * 10,
        out_specs=[vm()] * 5,
        out_shape=[kept(*FIELD)] * 4 + [kept(6, 64, 128)],
        scratch_shapes=[pltpu.VMEM((2, 2, 128, 128), F32), pltpu.VMEM((2, 8, 40, 128), F32)],
        input_output_aliases={7: 0, 8: 1, 9: 2, 10: 3},
        compiler_params=pltpu.CompilerParams(vmem_limit_bytes=24 * MIB),
    )(sc, *(near(x) for x in (ea, eb, relayed, msk, rim, rimd, fz, fr, fc, inv)))


PARTS = 4


def misfit_kernel(sc, got_h, svm_h, *refs):
    n_kept = len(KEPT)
    here, (m_out, ea, eb), refs = refs[:n_kept], refs[n_kept : n_kept + 3], refs[n_kept + 3 :]
    kept_, (got, svm, hot, rhs, pc, sem, sem2) = refs[:n_kept], refs[n_kept:]
    _, odd = place(sc)
    n = got.shape[0] // PARTS
    parts = [
        pltpu.make_async_copy(got_h.at[pl.ds(i * n, n)], got.at[pl.ds(i * n, n)], sem.at[i]) for i in range(PARTS)
    ]
    strips = pltpu.make_async_copy(svm_h, svm, sem.at[PARTS])
    rest = []
    for i, (x, y) in enumerate(zip(here, kept_)):
        if KEPT[i] == FIELD:
            x, y = x.at[EARLY], y.at[EARLY]
        rest.append(pltpu.make_async_copy(x, y, sem2.at[i]))
    for c in (*parts, strips, *rest):
        c.start()
    msk = kept_[0]
    p = lax.broadcasted_iota(jnp.int32, (512, 128), 0)
    pc[...] = code_of(p).astype(F32)
    rhs[:, pl.ds(128, 128)] = jnp.ones((rhs.shape[0], 128), BF16)
    lane = lax.broadcasted_iota(jnp.int32, (8, 128), 1)
    for part in parts:
        part.wait()
    for part in range(PARTS):
        for b in range(n // 2):
            s = part * n + 2 * b
            for h in range(2):
                rhs[pl.ds((s + h) * 64, 64), pl.ds(0, 128)] = got[s + h, pl.ds(0, 64), :]
            c = jnp.where(lane < 64, got[s, pl.ds(64, 8), :].astype(F32), got[s + 1, pl.ds(64, 8), :].astype(F32))
            same = pc[...].reshape(64, 8, 128) == c[None]
            hot[:, pl.ds(s * 64, 128)] = jnp.where(same, 1.0, 0.0).reshape(512, 128).astype(BF16)
    sums = jnp.dot(hot[...], rhs[...], preferred_element_type=F32)
    strips.wait()
    rest[0].wait()
    m_out[...] = sums[:, 128:] * svm[...] - msk[...] * sums[:, :128]
    for kind, e in enumerate((ea, eb)):
        start = jnp.where((odd + kind) % 2 == 0, ROWS - 2, 0)
        for r in range(2):
            e[pl.ds(r * 8, 8), :] = m_out[row(start + r), :]
    for c in rest[1:]:
        c.wait()


KEPT = (STRIP, RIM, (16, 128), STRIP) + (FIELD,) * 4


def misfit(sc, got, svm, *rest):
    k = got.shape[0] * 64
    return pl.pallas_call(
        misfit_kernel,
        in_specs=[sm()] + [hbm()] * (2 + len(KEPT)),
        out_specs=[vm()] * (3 + len(KEPT)),
        out_shape=[kept(*STRIP), kept(16, 128), kept(16, 128)] + [kept(*x) for x in KEPT],
        scratch_shapes=[
            pltpu.VMEM(got.shape, BF16),
            pltpu.VMEM(STRIP, F32),
            pltpu.VMEM((512, k), BF16),
            pltpu.VMEM((k, 256), BF16),
            pltpu.VMEM((512, 128), F32),
            pltpu.SemaphoreType.DMA((PARTS + 1,)),
            pltpu.SemaphoreType.DMA((len(KEPT),)),
        ],
        compiler_params=pltpu.CompilerParams(vmem_limit_bytes=24 * MIB),
    )(sc, *(far(x) for x in (got, svm, *rest)))


class Sweeps:
    def __init__(self, sc, t1, t2, c, coefs, state, turned):
        self.own, self.odd = place(sc)
        self.fz, self.fr, self.fc, self.inv, self.wgt = coefs
        self.a1, self.a2, self.a3, self.acc = state
        self.turned = turned
        self.thick = [jnp.where(self.own == l // 4, t1[l % 4], t2[l % 4]) for l in range(8)]
        self.rw, self.cw = weights(c)
        lane, _ = lanes()
        self.last, self.first_lane = lane == 127, lane == 0

    def turn(self, k, r, slot=0):
        a = (self.a1, self.a2)[k]
        for l in range(8):
            x, f = a[r, at(l), :], self.fc[r, at(l), :]
            self.turned[k, slot, l] = self.cw * (f * east(x, self.last) + west(f * x, self.first_lane))

    def neighbours(self, k, l, r, slot):
        a = (self.a1, self.a2)[k]
        n = None
        if l < 7:
            n = self.fz[r, at(l), :] * a[r, at(l + 1), :]
        if l > 0:
            t = self.fz[r, at(l - 1), :] * a[r, at(l - 1), :]
            n = t if n is None else n + t
        rows_ = self.fr[r, at(l), :] * a[r + 1, at(l), :] + self.fr[r - 1, at(l), :] * a[r - 1, at(l), :]
        return self.inv[r, at(l), :] * (n + self.rw * rows_ + self.turned[k, slot, l])

    def first(self, r, m):
        for l in range(8):
            self.a1[r, at(l), :] = self.inv[r, at(l), :] * (self.thick[l] * m)

    def second(self, r, slot=0):
        for l in range(8):
            self.a2[r, at(l), :] = 1.3 * self.a1[r, at(l), :] + self.neighbours(0, l, r, slot)

    def third(self, r, slot=0):
        total = None
        for l in range(8):
            y = 0.3 * self.a2[r, at(l), :] + (self.a1[r, at(l), :] + self.neighbours(1, l, r, slot))
            self.a3[l, row(r - 2), :] = y
            total = self.thick[l] * y if l == 0 else total + self.thick[l] * y
        self.acc[row(r - 2), :] = self.wgt[row(r - 2), :] * total

    def interior(self, m, ready=()):
        for r in (1, EXT - 2):
            self.a1[r] = jnp.zeros((64, 128), F32)

        def stage(p, static):
            for k, back in ((1, 4), (1, 3), (0, 2), (0, 1), (None, 0)):
                q = p - back
                if static and not (2 if k == 1 else 1) <= q <= (31 if k == 1 else 32):
                    continue
                for j in range(2):
                    r = 2 * q + j
                    if back == 4:
                        self.third(r, j)
                    elif back == 2:
                        self.second(r, j)
                    elif back:
                        self.turn(k, r, j)
                    else:
                        self.first(r, m[row(r - 2), :])

        def step(p, carry):
            stage(p, False)
            return carry

        for p in range(1, 6):
            stage(p, True)
        at_ = 6
        for upto, wait in ready:
            lax.fori_loop(at_, upto, step, 0)
            wait()
            at_ = upto
        lax.fori_loop(at_, 33, step, 0)
        for p in range(33, 36):
            stage(p, True)

    def edges(self, ga, gb):
        up = jnp.where(self.odd == 1, ga[...], gb[...])
        down = jnp.where(self.odd == 1, gb[...], ga[...])
        for ghost, firsts, seconds, thirds in (
            (up, (0, 1), (1, 2), (2, 3)),
            (down, (66, 67), (65, 66), (64, 65)),
        ):
            for i, r in enumerate(firsts):
                self.first(r, ghost[i * 8 : i * 8 + 8, :])
            for r in seconds:
                self.turn(0, r)
                self.second(r)
            for r in thirds:
                self.turn(1, r)
                self.third(r)


INNER, OUTER = range(8, ROWS - 8, 8), (0, ROWS - 8)


def gather_rows(dst, src, rows=range(0, ROWS, 8)):
    for h in rows:
        for k in range(8):
            dst[pl.ds(h, 8), pl.ds(k * 128, 128)] = src[pl.ds(h * 8 + k, 8, stride=8), :]


TURNED = (2, 2, 8, 8, 128)
STATE = (FIELD, FIELD, (8, (ROWS + 1) * 8, 128), STRIP)
N_STATE = len(STATE)
STAGE = (4, ROWS, 1024)


def own_kernel(sc, t1, t2, fz_h, fr_h, fc_h, inv_h, invx_h, wgtx_h, gx, m, wgt, *refs):
    fields, state, (invx, wgtx, turned, sem, sem2) = refs[4:8], refs[8:12], refs[12:]
    own, _ = place(sc)
    groups = []
    for i, (first, rows) in enumerate(LATER):
        part = pl.ds(first, rows)
        pairs = zip((fz_h, fr_h, fc_h, inv_h), fields)
        groups.append([pltpu.make_async_copy(x.at[part], y.at[part], sem.at[i, j]) for j, (x, y) in enumerate(pairs)])
    copies = (
        pltpu.make_async_copy(invx_h.at[INSIDE], invx.at[INSIDE], sem2.at[0]),
        pltpu.make_async_copy(wgtx_h, wgtx, sem2.at[1]),
    )
    for c in (*(c for group in groups for c in group), *copies):
        c.start()

    def waiting(group):
        def wait():
            for c in group:
                c.wait()

        return wait

    ready = [(first // 2, waiting(group)) for (first, _), group in zip(LATER, groups)]
    Sweeps(sc, t1, t2, own, (*fields, wgt), state, turned).interior(m, ready)
    for c in copies:
        c.wait()
    invx[pl.ds(0, 3)] = gx[pl.ds(0, 3)]
    invx[pl.ds(ROWS + 1, 3)] = gx[pl.ds(3, 3)]


def own_sweeps(sc, t1, t2, stored, invx, wgtx, gx, m, wgt, fields):
    return pl.pallas_call(
        own_kernel,
        in_specs=[sm()] * 3 + [hbm()] * 6 + [vm()] * 7,
        out_specs=[vm()] * 10,
        out_shape=[kept(*s) for s in (*(FIELD,) * 4, *STATE, FIELD, STRIP)],
        scratch_shapes=[
            pltpu.VMEM(TURNED, F32),
            pltpu.SemaphoreType.DMA((len(LATER), 4)),
            pltpu.SemaphoreType.DMA((2,)),
        ],
        input_output_aliases={12 + i: i for i in range(4)},
        compiler_params=pltpu.CompilerParams(vmem_limit_bytes=24 * MIB),
    )(sc, t1, t2, *(far(x) for x in (*stored, invx, wgtx)), *(near(x) for x in (gx, m, wgt, *fields)))


def both_kernel(sc, t1, t2, ga, gb, m, *refs):
    (fz, fr, fc, inv, wgt, invx, wgtx), refs = refs[:7], refs[7 + N_STATE :]
    done, todo, adj, (stage, turned, sem) = refs[:4], refs[4:8], refs[8], refs[9:]
    own, _ = place(sc)
    Sweeps(sc, t1, t2, own, (fz, fr, fc, inv, wgt), done, turned).edges(ga, gb)
    for i in range(4):
        gather_rows(stage.at[i], done[2].at[own * 4 + i])
    copy = pltpu.make_async_copy(stage, adj.at[own], sem)
    copy.start()
    Sweeps(sc, t1, t2, 1 - own, (fz, fr, fc, invx, wgtx), todo, turned).interior(m)
    copy.wait()


def both_sweeps(sc, t1, t2, ga, gb, m, coefs, others, state):
    return pl.pallas_call(
        both_kernel,
        in_specs=[sm()] * 3 + [vm()] * (3 + 7 + N_STATE),
        out_specs=[vm()] * (2 * N_STATE) + [hbm()],
        out_shape=[kept(*s) for s in STATE] * 2 + [pltpu.HBM((2, *STAGE), F32)],
        scratch_shapes=[pltpu.VMEM(STAGE, F32), pltpu.VMEM(TURNED, F32), pltpu.SemaphoreType.DMA],
        input_output_aliases={13 + i: i for i in range(N_STATE)},
        compiler_params=pltpu.CompilerParams(vmem_limit_bytes=24 * MIB),
    )(sc, t1, t2, *(near(x) for x in (ga, gb, m, *coefs, *others, *state)))


def last_kernel(sc, t1, t2, g, racc, fz, fr, fc, inv, wgt, *refs):
    state, (adj, grad), (stage, sum_, turned, sem) = refs[5:9], refs[9:11], refs[11:]
    _, _, a3, acc = state
    own, _ = place(sc)
    to = adj.at[1 - own]
    spans = (pl.ds(8, ROWS - 16), pl.ds(0, 8), pl.ds(ROWS - 8, 8))
    copies = [pltpu.make_async_copy(stage.at[:, x, :], to.at[:, x, :], sem.at[i]) for i, x in enumerate(spans)]
    copies += [pltpu.make_async_copy(sum_.at[x, :], grad.at[x, :], sem.at[3 + i]) for i, x in enumerate(spans)]
    for i in range(4):
        gather_rows(stage.at[i], a3.at[own * 4 + i], INNER)
    copies[0].start()
    for r in INNER:
        acc[pl.ds(r * 8, 64), :] = acc[pl.ds(r * 8, 64), :] + racc[pl.ds(r * 8, 64), :]
    gather_rows(sum_, acc, INNER)
    copies[3].start()
    Sweeps(sc, t1, t2, 1 - own, (fz, fr, fc, inv, wgt), state, turned).edges(
        g.at[pl.ds(0, 16), :], g.at[pl.ds(16, 16), :]
    )
    for i in range(4):
        gather_rows(stage.at[i], a3.at[own * 4 + i], OUTER)
    copies[1].start()
    copies[2].start()
    for r in OUTER:
        acc[pl.ds(r * 8, 64), :] = acc[pl.ds(r * 8, 64), :] + racc[pl.ds(r * 8, 64), :]
    gather_rows(sum_, acc, OUTER)
    copies[4].start()
    copies[5].start()
    for c in copies:
        c.wait()


def last_sweeps(sc, t1, t2, g, racc, coefs, state, adj):
    return pl.pallas_call(
        last_kernel,
        in_specs=[sm()] * 3 + [vm()] * 11 + [hbm()],
        out_specs=[vm()] * 4 + [hbm(), hbm()],
        out_shape=[kept(*s) for s in STATE]
        + [pltpu.HBM((2, *STAGE), F32), pltpu.HBM((ROWS, 1024), F32)],
        scratch_shapes=[
            pltpu.VMEM(STAGE, F32),
            pltpu.VMEM((ROWS, 1024), F32),
            pltpu.VMEM(TURNED, F32),
            pltpu.SemaphoreType.DMA((6,)),
        ],
        input_output_aliases={10: 0, 11: 1, 12: 2, 13: 3, 14: 4},
        compiler_params=pltpu.CompilerParams(vmem_limit_bytes=24 * MIB),
    )(sc, t1, t2, *(near(x) for x in (g, racc, *coefs, *state)), far(adj))[4:]


def swaps(tiles, offset):
    perm = []
    for t in range(offset, tiles - 1, 2):
        perm += [(t, t + 1), (t + 1, t)]
    return perm


def swap_layers(x):
    return lax.ppermute(x, "layer", [(0, 1), (1, 0)])


def body(viscosity, friction, base_vel, surf_vel, layer_thick, ice_mask, obs_slots, obs_target):
    tiles = lax.axis_size("tile")
    own = lax.axis_index("layer")
    odd = lax.axis_index("tile") % 2
    sc = (own + 2 * odd).astype(jnp.int32).reshape(1)

    def swap(x, kind):
        return lax.ppermute(x, "tile", swaps(tiles, kind))

    narrow, slots, target = narrowed(viscosity, obs_slots.reshape(tiles, 128, 128), obs_target)
    other = swap_layers(narrow)
    payload = pack(sc, slots, target)
    got = lax.all_to_all(payload, "tile", split_axis=0, concat_axis=0, tiled=True)
    thick_other = swap_layers(layer_thick)

    to_a, to_b = edge_rows(sc, viscosity, ice_mask, friction)
    near_rows = (swap(to_a, 0), swap(to_b, 1))
    relayed = swap_layers(jnp.concatenate(near_rows))
    fz, fr, fc, inv, invx, wgt, wgtx, svm, msk, rim, rimd = coefficients(
        sc, viscosity, other, friction, ice_mask, base_vel, surf_vel
    )
    stored = (fz, fr, fc, inv)
    got, near_rows, thick_other = lax.optimization_barrier((got, near_rows, thick_other))
    m_own, ea, eb, msk, rim, rimd, wgt, fz, fr, fc, inv = misfit(
        sc, got, svm, msk, rim, rimd, wgt, fz, fr, fc, inv
    )
    fz, fr, fc, inv, gx = ghosts(sc, *near_rows, relayed, msk, rim, rimd, fz, fr, fc, inv)
    th = (sc, layer_thick, thick_other)

    ga, gb = swap(ea, 0), swap(eb, 1)
    m_oth = swap_layers(m_own)
    fz, fr, fc, inv, *state, invx, wgtx = own_sweeps(*th, stored, invx, wgtx, gx, m_own, wgt, (fz, fr, fc, inv))
    g_oth = swap_layers(jnp.concatenate([ga, gb]))
    *both, adj = both_sweeps(*th, ga, gb, m_oth, (fz, fr, fc, inv, wgt), (invx, wgtx), state)
    adjoint, gradient = last_sweeps(*th, g_oth, both[3], (fz, fr, fc, invx, wgtx), both[4:], adj)
    return adjoint, gradient


def solution(mesh):
    in_specs = (
        P("layer", "tile", None),
        P("tile", None),
        P(None, "tile", None),
        P(None, "tile", None),
        P("layer"),
        P("tile", None),
        P("tile", None, None, None),
        P("tile", None),
    )
    out_specs = (P(None, "layer", "tile", None), P("tile", None))

    return jax.shard_map(body, mesh=mesh, in_specs=in_specs, out_specs=out_specs, check_vma=False)
```

```python
import jax
import jax.numpy as jnp
from jax import lax
from jax.experimental import pallas as pl
from jax.experimental.pallas import tpu as pltpu
from jax.sharding import PartitionSpec as P


F32 = jnp.float32
BF16 = jnp.bfloat16
ROWS = 64
EXT = 68
FIELD = (EXT, 72, 128)
STRIP = (ROWS * 8, 128)
MIB = 1 << 20


def vm():
    return pl.BlockSpec(memory_space=pltpu.VMEM)


def sm():
    return pl.BlockSpec(memory_space=pltpu.SMEM)


def hbm():
    return pl.BlockSpec(memory_space=pltpu.HBM)


def far(x):
    return pltpu.with_memory_space_constraint(x, pltpu.HBM)


def kept(*shape, dtype=F32):
    return pltpu.VMEM(shape, dtype)


def near(x):
    return pltpu.with_memory_space_constraint(x, pltpu.VMEM)


def row(r):
    return pl.ds(pl.multiple_of(r * 8, 8), 8)


def at(l):
    return pl.ds(l * 8, 8)


def place(sc):
    return sc[0] & 1, sc[0] >> 1


def lanes():
    lane = lax.broadcasted_iota(jnp.int32, (8, 128), 1)
    sub = lax.broadcasted_iota(jnp.int32, (8, 128), 0)
    return lane, sub


def east(x, last):
    r = pltpu.roll(x, 127, 1)
    return jnp.where(last, pltpu.roll(r, 7, 0), r)


def west(x, first):
    r = pltpu.roll(x, 1, 1)
    return jnp.where(first, pltpu.roll(r, 1, 0), r)


def code_of(t):
    return jnp.where(t < 512, (128 + (t & 127)) << (t >> 7), 0)


def narrow_kernel(visc, slots, target, narrow, x, t, vx, vy, vin, vout, st):
    layers = visc.shape[0]
    takes = [pltpu.make_async_copy(visc.at[i], vx.at[i], vin.at[i]) for i in range(layers)]
    gives = [pltpu.make_async_copy(vy.at[i], narrow.at[i], vout.at[i]) for i in range(layers)]
    fetch = [pltpu.make_async_copy(target, t, st.at[0]), pltpu.make_async_copy(slots, x, st.at[1])]
    for i in (*takes, *fetch):
        i.start()
    for i in range(layers):
        takes[i].wait()
        vy[i] = vx[i].astype(BF16)
        gives[i].start()
    for i in (*gives, *fetch):
        i.wait()


def narrowed(visc, slots, target):
    return pl.pallas_call(
        narrow_kernel,
        in_specs=[hbm()] * 3,
        out_specs=[hbm(), vm(), vm()],
        out_shape=[pltpu.HBM(visc.shape, BF16), kept(*slots.shape, dtype=BF16), kept(*target.shape, dtype=jnp.int32)],
        scratch_shapes=[
            pltpu.VMEM(visc.shape, F32),
            pltpu.VMEM(visc.shape, BF16),
            pltpu.SemaphoreType.DMA((visc.shape[0],)),
            pltpu.SemaphoreType.DMA((visc.shape[0],)),
            pltpu.SemaphoreType.DMA((2,)),
        ],
        compiler_params=pltpu.CompilerParams(vmem_limit_bytes=8 * MIB),
    )(far(visc), far(slots), far(target))


def pack_kernel(sc, x, t, o, y, f, codes, sout):
    own, _ = place(sc)
    n = x.shape[0]
    step = n // CHUNKS
    outs = [
        pltpu.make_async_copy(y.at[pl.ds(i * step, step)], o.at[pl.ds(i * step, step)], sout.at[i])
        for i in range(CHUNKS)
    ]
    c = code_of(t[...]).astype(F32)
    codes[...] = jnp.concatenate([c, c], axis=1)
    for i in range(CHUNKS):

        def one(d, carry):
            f[d] = x[d].astype(F32)
            y[d, pl.ds(0, 64), :] = f[d, pl.ds(own, 64, stride=2), :].astype(BF16)
            y[d, pl.ds(64, 8), :] = jnp.broadcast_to(codes[pl.ds(d, 1), :], (8, 128)).astype(BF16)
            return carry

        lax.fori_loop(i * step, (i + 1) * step, one, 0, unroll=8)
        outs[i].start()
    for i in outs:
        i.wait()


CHUNKS = 8


def pack(sc, slots, target):
    n = slots.shape[0]
    return pl.pallas_call(
        pack_kernel,
        in_specs=[sm(), vm(), vm()],
        out_specs=hbm(),
        out_shape=pltpu.HBM((n, 72, 128), BF16),
        scratch_shapes=[
            pltpu.VMEM((n, 72, 128), BF16),
            pltpu.VMEM((n, 128, 128), F32),
            pltpu.VMEM((n, 128), F32),
            pltpu.SemaphoreType.DMA((CHUNKS,)),
        ],
        compiler_params=pltpu.CompilerParams(vmem_limit_bytes=16 * MIB),
    )(sc, near(slots), near(target))


def edge_kernel(sc, visc, mask, fric, to_a, to_b, v, m, d, s, sem):
    _, odd = place(sc)
    copies = []
    for side in range(2):
        at = pl.ds(side * (ROWS - 8), 8)
        copies.append(pltpu.make_async_copy(visc.at[:, at, :], v.at[side], sem.at[side * 3]))
        copies.append(pltpu.make_async_copy(mask.at[at, :], m.at[side], sem.at[side * 3 + 1]))
        copies.append(pltpu.make_async_copy(fric.at[at, :], d.at[side], sem.at[side * 3 + 2]))
    for c in copies:
        c.start()
    for c in copies:
        c.wait()
    for side in range(2):
        for i in range(4):
            s[side, pl.ds(3 * i, 3), :] = v[side, i, pl.ds(5 * side, 3), :]
        s[side, pl.ds(12, 2), :] = m[side, pl.ds(6 * side, 2), :].astype(F32)
        s[side, pl.ds(14, 2), :] = d[side, pl.ds(6 * side, 2), :]
    to_a[...] = s[1 - odd].astype(BF16)
    to_b[...] = s[odd].astype(BF16)


def edge_rows(sc, visc, mask, fric):
    return pl.pallas_call(
        edge_kernel,
        in_specs=[sm(), hbm(), hbm(), hbm()],
        out_specs=[vm()] * 2,
        out_shape=[kept(16, 1024, dtype=BF16)] * 2,
        scratch_shapes=[
            pltpu.VMEM((2, 4, 8, 1024), F32),
            pltpu.VMEM((2, 8, 1024), jnp.int32),
            pltpu.VMEM((2, 8, 1024), F32),
            pltpu.VMEM((2, 16, 1024), F32),
            pltpu.SemaphoreType.DMA((6,)),
        ],
        compiler_params=pltpu.CompilerParams(vmem_limit_bytes=8 * MIB),
    )(sc, far(visc), far(mask), far(fric))


def spread(dst, at, x):
    n = x.shape[0]
    for k in range(8):
        dst[pl.ds(at + k, n, stride=8), :] = x[:, k * 128 : (k + 1) * 128]


def weights(c):
    return jnp.where(c == 0, 4.0, 1.0), jnp.where(c == 0, 1.0, 4.0)


def coefficient_row(view, m, drag, r, pairs, fz, fr, fc, invs):
    lane, sub = lanes()
    last, first = lane == 127, lane == 0
    end = last & (sub == 7)
    start = first & (sub == 0)
    prev = None
    for l in range(8):
        c = view(l, 0)
        fe = 0.5 * (c + jnp.where(end, 0.0, east(c, last)))
        fw = 0.5 * (c + jnp.where(start, 0.0, west(c, first)))
        south = 0.5 * (c + view(l, 1))
        north = 0.5 * (c + view(l, -1))
        below = 4.0 * c if l == 0 else prev
        above = 4.0 * (c + view(l + 1, 0)) if l < 7 else 4.0 * c
        fz[r, at(l), :] = above
        fr[r, at(l), :] = south
        fc[r, at(l), :] = jnp.where(end, 0.0, fe)
        rows_, cols_, both = north + south, fe + fw, below + above
        if l == 0:
            both = both + drag
        for (rw, cw), inv, shift in zip(pairs, *invs):
            diag = both + rw * rows_ + cw * cols_
            inv[r + shift, at(l), :] = jnp.where(m, 0.7 / diag, 0.0)
        prev = above


GROUPS = ((3, 16), (16, 32), (32, 48), (48, 60), (60, 65))
INSIDE = pl.ds(3, 62)
EARLY = pl.ds(3, 29)
LATER = ((32, 16), (48, 17))
RIM = (8, 32, 128)
N_FIELDS = 5


def coef_kernel(sc, visc, other, fric, mask, bvel, svel, *refs):
    outs, rest = refs[:11], refs[11:]
    fields, (wo, wx, svm, msk, rim, rimd, drg, v, bv, sem, sem2) = rest[:N_FIELDS], rest[N_FIELDS:]
    fz, fr, fc, inv_own, inv_oth = fields
    own, _ = place(sc)
    for i in range(4):
        for src, to in ((visc, own * 4 + i), (other, (1 - own) * 4 + i)):
            for h in range(0, ROWS, 16):
                spread(v.at[to], h * 8, src[i, h : h + 16, :].astype(F32))
    for h in range(0, ROWS, 16):
        spread(msk, h * 8, mask[h : h + 16, :].astype(F32))
        spread(drg, h * 8, fric[h : h + 16, :])
        spread(svm, h * 8, svel[own, h : h + 16, :])
        spread(bv.at[0], h * 8, bvel[own, h : h + 16, :])
        spread(bv.at[1], h * 8, bvel[1 - own, h : h + 16, :])
    for l in range(8):
        rim[l, pl.ds(0, 16), :] = v[l, pl.ds(0, 16), :]
        rim[l, pl.ds(16, 16), :] = v[l, pl.ds((ROWS - 2) * 8, 16), :]
    rimd[pl.ds(0, 8), :] = drg[row(0), :]
    rimd[pl.ds(8, 8), :] = drg[row(ROWS - 1), :]
    pairs = (weights(own), weights(1 - own))

    def strips(r):
        m, d = msk[row(r), :], drg[row(r), :]
        svm[row(r), :] = svm[row(r), :] * m
        for c, w in enumerate((wo, wx)):
            w[row(r), :] = (-m * d) * bv[c, row(r), :]
        return m, d

    def step(r, carry):
        m, d = strips(r)
        invs = ((inv_own, inv_oth), (0, 0))
        coefficient_row(lambda l, j: v[l, row(r + j), :], m > 0.5, d, r + 2, pairs, fz, fr, fc, invs)
        return carry

    strips(0)
    strips(ROWS - 1)
    copies = []
    for i, (src, dst) in enumerate(zip((msk, rim, rimd), outs[8:])):
        copies.append(pltpu.make_async_copy(src, dst, sem2.at[i]))
    for c in copies:
        c.start()
    for k, (a, b) in enumerate(GROUPS):
        lax.fori_loop(a - 2, b - 2, step, 0)
        part = pl.ds(a, b - a)
        for i, src in enumerate(fields):
            copies.append(pltpu.make_async_copy(src.at[part], outs[i].at[part], sem.at[k, i]))
            copies[-1].start()
    for i, (src, dst) in enumerate(zip((wo, wx, svm), outs[5:])):
        copies.append(pltpu.make_async_copy(src, dst, sem2.at[3 + i]))
        copies[-1].start()
    for c in copies:
        c.wait()


def coefficients(sc, visc, other, fric, mask, bvel, svel):
    shapes = (FIELD,) * N_FIELDS + (STRIP,) * 4 + (RIM, (16, 128))
    return pl.pallas_call(
        coef_kernel,
        in_specs=[sm()] + [vm()] * 6,
        out_specs=[hbm()] * 11,
        out_shape=[pltpu.HBM(x, F32) for x in shapes],
        scratch_shapes=[pltpu.VMEM(x, F32) for x in shapes]
        + [
            pltpu.VMEM(STRIP, F32),
            pltpu.VMEM((8, (ROWS + 1) * 8, 128), F32),
            pltpu.VMEM((2, *STRIP), F32),
            pltpu.SemaphoreType.DMA((len(GROUPS), N_FIELDS)),
            pltpu.SemaphoreType.DMA((6,)),
        ],
        compiler_params=pltpu.CompilerParams(vmem_limit_bytes=32 * MIB),
    )(sc, visc, other, fric, mask, bvel, svel)


def ghost_kernel(sc, ea, eb, relayed, msk, rim, rimd, fz0, fr0, fc0, inv0, fz, fr, fc, inv, gx, g, u):
    own, odd = place(sc)
    pairs = (weights(own), weights(1 - own))
    for kind, pair in enumerate(((ea, relayed.at[pl.ds(0, 16)]), (eb, relayed.at[pl.ds(16, 16)]))):
        side = jnp.where((odd + kind) % 2 == 1, 0, 1)
        for who, e in enumerate(pair):
            spread(g.at[side, who], 0, e[...].astype(F32))
    for side in range(2):
        to = 0 if side == 0 else 2
        for who in range(2):
            base = (own if who == 0 else 1 - own) * 4
            for i in range(4):
                u[side, base + i, pl.ds(to * 8, 24), :] = g[side, who, pl.ds(i * 24, 24), :]
        for l in range(8):
            u[side, l, pl.ds(24 * (1 - side), 16), :] = rim[l, pl.ds(16 * side, 16), :]
        for j in range(3):
            if side == 0:
                r, ghost, inside = j, j, 0
            else:
                r, ghost, inside = ROWS + 1 + j, j - 1, ROWS - 1
            if (side == 0 and j == 2) or (side == 1 and j == 0):
                m, d = msk[row(inside), :], rimd[pl.ds(8 * side, 8), :]
            else:
                m, d = g[side, 0, pl.ds((12 + ghost) * 8, 8), :], g[side, 0, pl.ds((14 + ghost) * 8, 8), :]
            invs = ((inv, gx), (0, 0 if side == 0 else 3 - (ROWS + 1)))
            coefficient_row(lambda l, s: u[side, l, row(j + 1 + s), :], m > 0.5, d, r, pairs, fz, fr, fc, invs)


def ghosts(sc, ea, eb, relayed, msk, rim, rimd, fz, fr, fc, inv):
    return pl.pallas_call(
        ghost_kernel,
        in_specs=[sm()] + [vm()] * 10,
        out_specs=[vm()] * 5,
        out_shape=[kept(*FIELD)] * 4 + [kept(6, 72, 128)],
        scratch_shapes=[pltpu.VMEM((2, 2, 128, 128), F32), pltpu.VMEM((2, 8, 40, 128), F32)],
        input_output_aliases={7: 0, 8: 1, 9: 2, 10: 3},
        compiler_params=pltpu.CompilerParams(vmem_limit_bytes=24 * MIB),
    )(sc, *(near(x) for x in (ea, eb, relayed, msk, rim, rimd, fz, fr, fc, inv)))


PARTS = 4


def misfit_kernel(sc, got_h, svm_h, *refs):
    n_kept = len(KEPT)
    here, (m_out, ea, eb), refs = refs[:n_kept], refs[n_kept : n_kept + 3], refs[n_kept + 3 :]
    kept_, (got, svm, hot, rhs, pc, sem, sem2) = refs[:n_kept], refs[n_kept:]
    _, odd = place(sc)
    n = got.shape[0] // PARTS
    parts = [
        pltpu.make_async_copy(got_h.at[pl.ds(i * n, n)], got.at[pl.ds(i * n, n)], sem.at[i]) for i in range(PARTS)
    ]
    strips = pltpu.make_async_copy(svm_h, svm, sem.at[PARTS])
    rest = []
    for i, (x, y) in enumerate(zip(here, kept_)):
        if KEPT[i] == FIELD:
            x, y = x.at[EARLY], y.at[EARLY]
        rest.append(pltpu.make_async_copy(x, y, sem2.at[i]))
    for c in (*parts, strips, *rest):
        c.start()
    msk = kept_[0]
    p = lax.broadcasted_iota(jnp.int32, (512, 128), 0)
    pc[...] = code_of(p).astype(F32)
    rhs[:, pl.ds(128, 128)] = jnp.ones((rhs.shape[0], 128), BF16)
    lane = lax.broadcasted_iota(jnp.int32, (8, 128), 1)
    for part in parts:
        part.wait()
    for part in range(PARTS):
        for b in range(n // 2):
            s = part * n + 2 * b
            for h in range(2):
                rhs[pl.ds((s + h) * 64, 64), pl.ds(0, 128)] = got[s + h, pl.ds(0, 64), :]
            c = jnp.where(lane < 64, got[s, pl.ds(64, 8), :].astype(F32), got[s + 1, pl.ds(64, 8), :].astype(F32))
            same = pc[...].reshape(64, 8, 128) == c[None]
            hot[:, pl.ds(s * 64, 128)] = jnp.where(same, 1.0, 0.0).reshape(512, 128).astype(BF16)
    sums = jnp.dot(hot[...], rhs[...], preferred_element_type=F32)
    strips.wait()
    rest[0].wait()
    m_out[...] = sums[:, 128:] * svm[...] - msk[...] * sums[:, :128]
    for kind, e in enumerate((ea, eb)):
        start = jnp.where((odd + kind) % 2 == 0, ROWS - 2, 0)
        for r in range(2):
            e[pl.ds(r * 8, 8), :] = m_out[row(start + r), :]
    for c in rest[1:]:
        c.wait()


KEPT = (STRIP, RIM, (16, 128), STRIP) + (FIELD,) * 4


def misfit(sc, got, svm, *rest):
    k = got.shape[0] * 64
    return pl.pallas_call(
        misfit_kernel,
        in_specs=[sm()] + [hbm()] * (2 + len(KEPT)),
        out_specs=[vm()] * (3 + len(KEPT)),
        out_shape=[kept(*STRIP), kept(16, 128), kept(16, 128)] + [kept(*x) for x in KEPT],
        scratch_shapes=[
            pltpu.VMEM(got.shape, BF16),
            pltpu.VMEM(STRIP, F32),
            pltpu.VMEM((512, k), BF16),
            pltpu.VMEM((k, 256), BF16),
            pltpu.VMEM((512, 128), F32),
            pltpu.SemaphoreType.DMA((PARTS + 1,)),
            pltpu.SemaphoreType.DMA((len(KEPT),)),
        ],
        compiler_params=pltpu.CompilerParams(vmem_limit_bytes=24 * MIB),
    )(sc, *(far(x) for x in (got, svm, *rest)))


class Sweeps:
    def __init__(self, sc, t1, t2, c, coefs, state, turned):
        self.own, self.odd = place(sc)
        self.fz, self.fr, self.fc, self.inv, self.wgt = coefs
        self.a1, self.a2, self.a3, self.acc = state
        self.turned = turned
        self.thick = [jnp.where(self.own == l // 4, t1[l % 4], t2[l % 4]) for l in range(8)]
        self.rw, self.cw = weights(c)
        lane, _ = lanes()
        self.last, self.first_lane = lane == 127, lane == 0

    def turn(self, k, r, slot=0):
        a = (self.a1, self.a2)[k]
        for l in range(8):
            x, f = a[r, at(l), :], self.fc[r, at(l), :]
            self.turned[k, slot, l] = self.cw * (f * east(x, self.last) + west(f * x, self.first_lane))

    def neighbours(self, k, l, r, slot):
        a = (self.a1, self.a2)[k]
        n = None
        if l < 7:
            n = self.fz[r, at(l), :] * a[r, at(l + 1), :]
        if l > 0:
            t = self.fz[r, at(l - 1), :] * a[r, at(l - 1), :]
            n = t if n is None else n + t
        rows_ = self.fr[r, at(l), :] * a[r + 1, at(l), :] + self.fr[r - 1, at(l), :] * a[r - 1, at(l), :]
        return self.inv[r, at(l), :] * (n + self.rw * rows_ + self.turned[k, slot, l])

    def first(self, r, m):
        for l in range(8):
            self.a1[r, at(l), :] = self.inv[r, at(l), :] * (self.thick[l] * m)

    def second(self, r, slot=0):
        for l in range(8):
            self.a2[r, at(l), :] = 1.3 * self.a1[r, at(l), :] + self.neighbours(0, l, r, slot)

    def third(self, r, slot=0):
        total = None
        for l in range(8):
            y = 0.3 * self.a2[r, at(l), :] + (self.a1[r, at(l), :] + self.neighbours(1, l, r, slot))
            self.a3[l, row(r - 2), :] = y
            total = self.thick[l] * y if l == 0 else total + self.thick[l] * y
        self.acc[row(r - 2), :] = self.wgt[row(r - 2), :] * total

    def interior(self, m, ready=()):
        for r in (1, EXT - 2):
            self.a1[r] = jnp.zeros(FIELD[1:], F32)

        def stage(p, static):
            for k, back in ((1, 4), (1, 3), (0, 2), (0, 1), (None, 0)):
                q = p - back
                if static and not (2 if k == 1 else 1) <= q <= (31 if k == 1 else 32):
                    continue
                for j in range(2):
                    r = 2 * q + j
                    if back == 4:
                        self.third(r, j)
                    elif back == 2:
                        self.second(r, j)
                    elif back:
                        self.turn(k, r, j)
                    else:
                        self.first(r, m[row(r - 2), :])

        def step(p, carry):
            stage(p, False)
            return carry

        for p in range(1, 6):
            stage(p, True)
        at_ = 6
        for upto, wait in ready:
            lax.fori_loop(at_, upto, step, 0)
            wait()
            at_ = upto
        lax.fori_loop(at_, 33, step, 0)
        for p in range(33, 36):
            stage(p, True)

    def edges(self, ga, gb):
        up = jnp.where(self.odd == 1, ga[...], gb[...])
        down = jnp.where(self.odd == 1, gb[...], ga[...])
        for ghost, firsts, seconds, thirds in (
            (up, (0, 1), (1, 2), (2, 3)),
            (down, (66, 67), (65, 66), (64, 65)),
        ):
            for i, r in enumerate(firsts):
                self.first(r, ghost[i * 8 : i * 8 + 8, :])
            for r in seconds:
                self.turn(0, r)
                self.second(r)
            for r in thirds:
                self.turn(1, r)
                self.third(r)


INNER, OUTER = range(8, ROWS - 8, 8), (0, ROWS - 8)


def gather_rows(dst, src, rows=range(0, ROWS, 8)):
    for h in rows:
        for k in range(8):
            dst[pl.ds(h, 8), pl.ds(k * 128, 128)] = src[pl.ds(h * 8 + k, 8, stride=8), :]


TURNED = (2, 2, 8, 8, 128)
STATE = (FIELD, FIELD, (8, (ROWS + 1) * 8, 128), STRIP)
N_STATE = len(STATE)
STAGE = (4, ROWS, 1024)


def own_kernel(sc, t1, t2, fz_h, fr_h, fc_h, inv_h, invx_h, wgtx_h, gx, m, wgt, *refs):
    fields, state, (invx, wgtx, turned, sem, sem2) = refs[4:8], refs[8:12], refs[12:]
    own, _ = place(sc)
    groups = []
    for i, (first, rows) in enumerate(LATER):
        part = pl.ds(first, rows)
        pairs = zip((fz_h, fr_h, fc_h, inv_h), fields)
        groups.append([pltpu.make_async_copy(x.at[part], y.at[part], sem.at[i, j]) for j, (x, y) in enumerate(pairs)])
    copies = (
        pltpu.make_async_copy(invx_h.at[INSIDE], invx.at[INSIDE], sem2.at[0]),
        pltpu.make_async_copy(wgtx_h, wgtx, sem2.at[1]),
    )
    for c in (*groups[0], *groups[1], *copies):
        c.start()

    def waiting(group):
        def wait():
            for c in group:
                c.wait()

        return wait

    ready = [(first // 2, waiting(group)) for (first, _), group in zip(LATER, groups)]
    Sweeps(sc, t1, t2, own, (*fields, wgt), state, turned).interior(m, ready)
    for c in copies:
        c.wait()
    invx[pl.ds(0, 3)] = gx[pl.ds(0, 3)]
    invx[pl.ds(ROWS + 1, 3)] = gx[pl.ds(3, 3)]


def own_sweeps(sc, t1, t2, stored, invx, wgtx, gx, m, wgt, fields):
    return pl.pallas_call(
        own_kernel,
        in_specs=[sm()] * 3 + [hbm()] * 6 + [vm()] * 7,
        out_specs=[vm()] * 10,
        out_shape=[kept(*s) for s in (*(FIELD,) * 4, *STATE, FIELD, STRIP)],
        scratch_shapes=[
            pltpu.VMEM(TURNED, F32),
            pltpu.SemaphoreType.DMA((len(LATER), 4)),
            pltpu.SemaphoreType.DMA((2,)),
        ],
        input_output_aliases={12 + i: i for i in range(4)},
        compiler_params=pltpu.CompilerParams(vmem_limit_bytes=24 * MIB),
    )(sc, t1, t2, *(far(x) for x in (*stored, invx, wgtx)), *(near(x) for x in (gx, m, wgt, *fields)))


def both_kernel(sc, t1, t2, ga, gb, m, *refs):
    (fz, fr, fc, inv, wgt, invx, wgtx), refs = refs[:7], refs[7 + N_STATE :]
    done, todo, adj, (stage, turned, sem) = refs[:4], refs[4:8], refs[8], refs[9:]
    own, _ = place(sc)
    Sweeps(sc, t1, t2, own, (fz, fr, fc, inv, wgt), done, turned).edges(ga, gb)
    for i in range(4):
        gather_rows(stage.at[i], done[2].at[own * 4 + i])
    copy = pltpu.make_async_copy(stage, adj.at[own], sem)
    copy.start()
    Sweeps(sc, t1, t2, 1 - own, (fz, fr, fc, invx, wgtx), todo, turned).interior(m)
    copy.wait()


def both_sweeps(sc, t1, t2, ga, gb, m, coefs, others, state):
    return pl.pallas_call(
        both_kernel,
        in_specs=[sm()] * 3 + [vm()] * (3 + 7 + N_STATE),
        out_specs=[vm()] * (2 * N_STATE) + [hbm()],
        out_shape=[kept(*s) for s in STATE] * 2 + [pltpu.HBM((2, *STAGE), F32)],
        scratch_shapes=[pltpu.VMEM(STAGE, F32), pltpu.VMEM(TURNED, F32), pltpu.SemaphoreType.DMA],
        input_output_aliases={13 + i: i for i in range(N_STATE)},
        compiler_params=pltpu.CompilerParams(vmem_limit_bytes=24 * MIB),
    )(sc, t1, t2, *(near(x) for x in (ga, gb, m, *coefs, *others, *state)))


def last_kernel(sc, t1, t2, g, racc, fz, fr, fc, inv, wgt, *refs):
    state, (adj, grad), (stage, sum_, turned, sem) = refs[5:9], refs[9:11], refs[11:]
    _, _, a3, acc = state
    own, _ = place(sc)
    to = adj.at[1 - own]
    spans = (pl.ds(8, ROWS - 16), pl.ds(0, 8), pl.ds(ROWS - 8, 8))
    copies = [pltpu.make_async_copy(stage.at[:, x, :], to.at[:, x, :], sem.at[i]) for i, x in enumerate(spans)]
    copies += [pltpu.make_async_copy(sum_.at[x, :], grad.at[x, :], sem.at[3 + i]) for i, x in enumerate(spans)]
    for i in range(4):
        gather_rows(stage.at[i], a3.at[own * 4 + i], INNER)
    copies[0].start()
    for r in INNER:
        acc[pl.ds(r * 8, 64), :] = acc[pl.ds(r * 8, 64), :] + racc[pl.ds(r * 8, 64), :]
    gather_rows(sum_, acc, INNER)
    copies[3].start()
    Sweeps(sc, t1, t2, 1 - own, (fz, fr, fc, inv, wgt), state, turned).edges(
        g.at[pl.ds(0, 16), :], g.at[pl.ds(16, 16), :]
    )
    for i in range(4):
        gather_rows(stage.at[i], a3.at[own * 4 + i], OUTER)
    copies[1].start()
    copies[2].start()
    for r in OUTER:
        acc[pl.ds(r * 8, 64), :] = acc[pl.ds(r * 8, 64), :] + racc[pl.ds(r * 8, 64), :]
    gather_rows(sum_, acc, OUTER)
    copies[4].start()
    copies[5].start()
    for c in copies:
        c.wait()


def last_sweeps(sc, t1, t2, g, racc, coefs, state, adj):
    return pl.pallas_call(
        last_kernel,
        in_specs=[sm()] * 3 + [vm()] * 11 + [hbm()],
        out_specs=[vm()] * 4 + [hbm(), hbm()],
        out_shape=[kept(*s) for s in STATE]
        + [pltpu.HBM((2, *STAGE), F32), pltpu.HBM((ROWS, 1024), F32)],
        scratch_shapes=[
            pltpu.VMEM(STAGE, F32),
            pltpu.VMEM((ROWS, 1024), F32),
            pltpu.VMEM(TURNED, F32),
            pltpu.SemaphoreType.DMA((6,)),
        ],
        input_output_aliases={10: 0, 11: 1, 12: 2, 13: 3, 14: 4},
        compiler_params=pltpu.CompilerParams(vmem_limit_bytes=24 * MIB),
    )(sc, t1, t2, *(near(x) for x in (g, racc, *coefs, *state)), far(adj))[4:]


def swaps(tiles, offset):
    perm = []
    for t in range(offset, tiles - 1, 2):
        perm += [(t, t + 1), (t + 1, t)]
    return perm


def swap_layers(x):
    return lax.ppermute(x, "layer", [(0, 1), (1, 0)])


def body(viscosity, friction, base_vel, surf_vel, layer_thick, ice_mask, obs_slots, obs_target):
    tiles = lax.axis_size("tile")
    own = lax.axis_index("layer")
    odd = lax.axis_index("tile") % 2
    sc = (own + 2 * odd).astype(jnp.int32).reshape(1)

    def swap(x, kind):
        return lax.ppermute(x, "tile", swaps(tiles, kind))

    narrow, slots, target = narrowed(viscosity, obs_slots.reshape(tiles, 128, 128), obs_target)
    other = swap_layers(narrow)
    payload = pack(sc, slots, target)
    got = lax.all_to_all(payload, "tile", split_axis=0, concat_axis=0, tiled=True)
    thick_other = swap_layers(layer_thick)

    to_a, to_b = edge_rows(sc, viscosity, ice_mask, friction)
    near_rows = (swap(to_a, 0), swap(to_b, 1))
    relayed = swap_layers(jnp.concatenate(near_rows))
    fz, fr, fc, inv, invx, wgt, wgtx, svm, msk, rim, rimd = coefficients(
        sc, viscosity, other, friction, ice_mask, base_vel, surf_vel
    )
    stored = (fz, fr, fc, inv)
    got, near_rows, thick_other = lax.optimization_barrier((got, near_rows, thick_other))
    m_own, ea, eb, msk, rim, rimd, wgt, fz, fr, fc, inv = misfit(
        sc, got, svm, msk, rim, rimd, wgt, fz, fr, fc, inv
    )
    fz, fr, fc, inv, gx = ghosts(sc, *near_rows, relayed, msk, rim, rimd, fz, fr, fc, inv)
    th = (sc, layer_thick, thick_other)

    ga, gb = swap(ea, 0), swap(eb, 1)
    m_oth = swap_layers(m_own)
    fz, fr, fc, inv, *state, invx, wgtx = own_sweeps(*th, stored, invx, wgtx, gx, m_own, wgt, (fz, fr, fc, inv))
    g_oth = swap_layers(jnp.concatenate([ga, gb]))
    *both, adj = both_sweeps(*th, ga, gb, m_oth, (fz, fr, fc, inv, wgt), (invx, wgtx), state)
    adjoint, gradient = last_sweeps(*th, g_oth, both[3], (fz, fr, fc, invx, wgtx), both[4:], adj)
    return adjoint, gradient


def solution(mesh):
    in_specs = (
        P("layer", "tile", None),
        P("tile", None),
        P(None, "tile", None),
        P(None, "tile", None),
        P("layer"),
        P("tile", None),
        P("tile", None, None, None),
        P("tile", None),
    )
    out_specs = (P(None, "layer", "tile", None), P("tile", None))

    return jax.shard_map(body, mesh=mesh, in_specs=in_specs, out_specs=out_specs, check_vma=False)
```
